128 devices in a mesh: slab: 16 (over x, y), grp: 8 (over z, core).
Axes of the slice: x: 4, y: 4, z: 4, core: 2. Of those that a mesh axis runs over, the one named last changes fastest.
Arguments:
- reference_bricks: bfloat16 [8, 8192, 512], P('grp', 'slab'), may hold values from -6 to 6
- deformed: bfloat16 [32, 16, 128, 512], P('slab', 'grp'), may hold values from -6 to 6
- tap_weights: bfloat16 [8, 32, 16, 128, 512], P(None, 'slab', 'grp')
- valid_voxels: int32 [32, 16, 128, 512], P('slab', 'grp'), may hold values from 0 to 1
- sources: int32 [32, 16, 128], P('slab', 'grp'), may hold values from 0 to 8191, as said below
Outputs:
- coefficients: float32 [3, 32, 16, 128], P(None, 'slab', 'grp')
- residual: float32 [32, 16, 128, 512], P('slab', 'grp')
The draws below stay inside these ranges and needn't reach their ends.
Inputs may be any that keep to these rules, and one draw needn't show every extreme that they name: The cells of one band (equal y // 2) name each of the band's 8192 reference bricks exactly once; the 512 cells of one block of 2 z-cells of a band take exactly 32 sources from each run of 512 consecutive reference bricks of the band.
All inputs are finite; a program needn't handle non-finite values.
Results may differ from the reference program's by a relative error of at most 0.00035.
Values may be sent and summed in bfloat16 or wider, within the bound.
No kernel may reach another device: no remote copies, remote signals or barrier semaphores. Data moves between devices by JAX's collectives and lax.ppermute only.
A program may use at most 128 MiB of HBM per device.

```python
import jax
import jax.numpy as jnp
from jax import lax

BZD = 2
BYD = 2
BX = 128
ITERS = 2
BR_DEV = 512
SLABS = 16
BANDS = 8
BZ = 32
BY = 16
NCOL = 8192


def draw_tap_weights(key, part):
    fraction = jax.random.uniform(key, (3, BZ, BY, BX, 512), jnp.float32)
    taps = []
    for corner in range(8):
        corner_bits = (corner // 4, corner // 2 % 2, corner % 2)
        product = jnp.ones((BZ, BY, BX, 512), jnp.float32)
        for bit_value, share in zip(corner_bits, (fraction[0], fraction[1], fraction[2])):
            product = product * (share if bit_value else 1.0 - share)
        taps.append(product)
    return jnp.stack(taps).astype(jnp.bfloat16)


def draw_valid_voxels(key, part):
    layers = jnp.arange(BZ, dtype=jnp.int32)[:, None, None, None]
    ceiling = 250 + 600 * layers // max(BZ - 1, 1)
    sample_ints = jax.random.randint(key, (BZ, BY, BX, 512), 0, 1000, dtype=jnp.int32)
    return (sample_ints < ceiling).astype(jnp.int32)


def permute_one(sub_key):
    return jax.random.permutation(sub_key, BR_DEV).astype(jnp.int32)


def draw_sources(key, part):
    per_owner = BR_DEV // SLABS
    key_list = jax.random.split(jax.random.fold_in(key, 7), BANDS * SLABS)
    orders = jax.vmap(permute_one)(key_list).reshape(BANDS, SLABS, SLABS, per_owner)
    orders = orders + (jnp.arange(SLABS, dtype=jnp.int32) * BR_DEV)[None, :, None, None]
    grouped = jnp.transpose(orders, (0, 2, 1, 3)).reshape(BANDS, SLABS, BR_DEV)
    mix_keys = jax.random.split(jax.random.fold_in(key, 13), BANDS * SLABS)
    mixes = jax.vmap(permute_one)(mix_keys).reshape(BANDS, SLABS, BR_DEV)
    placed = jnp.take_along_axis(grouped, mixes, axis=2)
    blocks = placed.reshape(BANDS, SLABS, BZD, BYD, BX)
    return jnp.transpose(blocks, (1, 2, 0, 3, 4)).reshape(BZ, BY, BX).astype(jnp.int32)


def block_scale(rng, dims, cuts, low, largest):
    def one(position, parts):
        draws = jax.random.uniform(jax.random.fold_in(jax.random.fold_in(rng, 6), position), (parts,), jnp.float32, low / len(cuts), largest / len(cuts))
        return jnp.repeat(jnp.exp(draws), dims[position] // parts).reshape((-1,) + (1,) * (len(dims) - position - 1))

    level = one(*cuts[0])
    for cut in cuts[1:]:
        level = level * one(*cut)
    return level


def scatter_about(key, shape, deviation, reach, pieces=(), kind=jnp.bfloat16):
    loudness = block_scale(key, shape, pieces, -0.22, 0.18) if pieces else 1.0
    array = jax.random.normal(key, shape, jnp.float32) * deviation * loudness
    return jnp.minimum(jnp.maximum(array, -reach), reach).astype(kind)


def setup_inputs(seed: int = 0) -> dict:
    keys = jax.random.split(jax.random.key(seed), 6)
    return {
        "reference_bricks": scatter_about(keys[0], (BANDS, NCOL, 512), 1.0, 6.0, ((0, 8), (1, 16))),
        "deformed": scatter_about(keys[1], (BZ, BY, BX, 512), 1.0, 6.0, ((0, 16), (1, 8))),
        "tap_weights": draw_tap_weights(jax.random.fold_in(keys[5], 71), 0),
        "valid_voxels": draw_valid_voxels(jax.random.fold_in(keys[5], 71), 0),
        "sources": draw_sources(jax.random.fold_in(keys[5], 71), 0),
    }


def voxel_place():
    place = jnp.arange(512, dtype=jnp.int32)
    return place // 64, (place // 8) % 8, place % 8


def spline_rows():
    fractions = [(coord.astype(jnp.float32) + 0.5) / 8.0 for coord in voxel_place()]
    basis = []
    for corner in range(8):
        corner_bits = (corner // 4, (corner // 2) % 2, corner % 2)
        product = jnp.ones((512,), jnp.float32)
        for bit_value, fraction in zip(corner_bits, fractions):
            product = product * (fraction if bit_value else 1.0 - fraction)
        basis.append(product)
    return jnp.stack(basis)


def shift_ahead(field, stride, at_edge):
    return jnp.where(at_edge, field, jnp.roll(field, -stride, axis=-1))


def shift_behind(field, stride, at_edge):
    return jnp.where(at_edge, field, jnp.roll(field, stride, axis=-1))


def warp_fields(source, weights, image, valid_voxels):
    coords = voxel_place()
    strides = (64, 8, 1)
    warped = jnp.zeros(source.shape, jnp.float32)
    for corner in range(8):
        corner_bits = (corner // 4, (corner // 2) % 2, corner % 2)
        tapped = source
        for bit_value, stride, coord in zip(corner_bits, strides, coords):
            if bit_value:
                tapped = shift_ahead(tapped, stride, coord == 7)
        warped = warped + weights[corner].astype(jnp.float32) * tapped
    gradients = jnp.stack([0.5 * (shift_ahead(warped, stride, coord == 7) - shift_behind(warped, stride, coord == 0)) for stride, coord in zip(strides, coords)])
    valid_mask = valid_voxels.astype(jnp.float32)
    misfit = valid_mask * (warped - image.astype(jnp.float32))
    return gradients, valid_mask, misfit


def interpolate(extended, basis):
    z_cells = extended.shape[1] - 1
    y_cells = extended.shape[2] - 1
    terms = []
    for corner in range(8):
        along_z, along_y, along_x = corner // 4, (corner // 2) % 2, corner % 2
        portion = extended[:, along_z:along_z + z_cells, along_y:along_y + y_cells]
        if along_x:
            portion = jnp.pad(portion[..., 1:], ((0, 0), (0, 0), (0, 0), (0, 1)))
        terms.append(portion)
    return jnp.einsum("tczyx,tv->czyxv", jnp.stack(terms), basis, precision=lax.Precision.HIGHEST)


def corner_terms(force, basis):
    portions = jnp.einsum("czyxv,tv->tczyx", force, basis, precision=lax.Precision.HIGHEST)
    comps, z_cells, y_cells, x_cells = portions.shape[1:]
    summed = jnp.zeros((comps, z_cells + 1, y_cells + 1, x_cells), jnp.float32)
    for corner in range(8):
        along_z, along_y, along_x = corner // 4, (corner // 2) % 2, corner % 2
        portion = portions[corner]
        if along_x:
            portion = jnp.pad(portion[..., :-1], ((0, 0), (0, 0), (0, 0), (1, 0)))
        summed = summed + jnp.pad(portion, ((0, 0), (along_z, 1 - along_z), (along_y, 1 - along_y), (0, 0)))
    return summed


def reference(reference_bricks, deformed, tap_weights, valid_voxels, sources):
    band_index = (jnp.arange(BY, dtype=jnp.int32) // BYD).astype(jnp.int32)
    source = reference_bricks[band_index[None, :, None], sources]
    gradients, valid_mask, misfit = warp_fields(source.astype(jnp.float32), tap_weights, deformed, valid_voxels)
    basis = spline_rows()
    counted = jnp.sum(valid_mask)
    square_sum = jnp.sum(misfit * misfit)
    coefficients = jnp.zeros((3, BZ, BY, BX), jnp.float32)
    for sweep in range(ITERS):
        if sweep > 0:
            square_sum = jnp.sum(misfit * misfit)
        spread = square_sum / counted + 1e-6
        robust = 1.0 / (1.0 + misfit * misfit / spread)
        force = (robust * misfit)[None] * gradients
        gradient_nodes = corner_terms(force, basis)[:, :BZ, :BY]
        step_dir = -gradient_nodes
        extended = jnp.pad(step_dir, ((0, 0), (0, 1), (0, 1), (0, 0)))
        moved = valid_mask * jnp.sum(gradients * interpolate(extended, basis), axis=0)
        steep_sum = jnp.sum(gradient_nodes * gradient_nodes)
        curve_sum = jnp.sum(robust * moved * moved)
        step_size = steep_sum / curve_sum
        coefficients = coefficients + step_size * step_dir
        misfit = misfit + step_size * moved
    return coefficients, misfit
```

```python
import jax
import jax.numpy as jnp
from jax import lax
from jax.experimental import pallas as pl
from jax.experimental.pallas import tpu as pltpu
from jax.sharding import PartitionSpec as P

F32 = jnp.float32
BF16 = jnp.bfloat16
I32 = jnp.int32
EVERY = ("slab", "grp")
CELLS = 512
ROWS = 16
BLOCKS = CELLS // ROWS
CHUNKS = 4
NT = (((1,), (1,)), ((), ()))
TN = (((0,), (0,)), ((), ()))
VMEM = pl.BlockSpec(memory_space=pltpu.VMEM)


def iota(shape, axis):
    return lax.broadcasted_iota(I32, shape, axis)


def dot(a, b, dims):
    return lax.dot_general(a, b, dims, preferred_element_type=F32)


def call(body, outs, ins, name, scratch=(), limit=16):
    return pl.pallas_call(
        body,
        out_shape=[jax.ShapeDtypeStruct(s, d) for s, d in outs],
        in_specs=[VMEM] * len(ins),
        out_specs=[VMEM] * len(outs),
        scratch_shapes=list(scratch),
        compiler_params=pltpu.CompilerParams(vmem_limit_bytes=limit << 20),
        name=name,
    )(*ins)


def wanted_body(src_ref, pos_ref, want_ref):
    place = 32 * (lax.axis_index("slab") % 4)
    earlier = (iota((128, 128), 0) < iota((128, 128), 1)).astype(F32).astype(BF16)
    owners = iota((16, 128), 0)
    lanes = iota((128, 128), 0)
    before = jnp.zeros((16, 1), F32)
    want = jnp.zeros((32, 128), F32)
    for r in range(4):
        src = src_ref[r // 2, pl.ds(r % 2, 1), :]
        owner = src >> 9
        row = src & 511
        mine = jnp.where(owners == owner, 1.0, 0.0)
        count = dot(mine.astype(BF16), earlier, (((1,), (0,)), ((), ()))) + before
        before = before + jnp.sum(mine, axis=1, keepdims=True)
        rank = jnp.sum(mine * count, axis=0, keepdims=True).astype(I32)
        pos_ref[pl.ds(r, 1), :] = owner * 32 + rank
        slot = jnp.where(lanes == rank + place, 1.0, 0.0).astype(BF16)
        low = (row & 255).astype(F32)
        high = (row >> 8).astype(F32)
        parts = jnp.concatenate([mine * low, mine * high], axis=0).astype(BF16)
        want = want + dot(parts, slot, NT)
    want_ref[...] = (want[:16] + 256.0 * want[16:]).astype(I32)


def pick_body(want_ref, bricks_ref, out_ref):
    bricks = bricks_ref[0]
    rows = iota((CELLS, 128), 0)
    for r in range(4):
        index = jnp.sum(want_ref[pl.ds(4 * r, 4), :], axis=0, keepdims=True)
        chosen = jnp.where(rows == index, 1.0, 0.0).astype(BF16)
        out_ref[pl.ds(128 * r, 128), :] = dot(chosen, bricks, TN).astype(BF16)


def ahead(field, amount, at_edge):
    return jnp.where(at_edge, field, pltpu.roll(field, 128 - amount, 1))


def behind(field, amount, at_edge):
    return jnp.where(at_edge, field, pltpu.roll(field, amount, 1))


def ahead_z(chunks, swapped, low):
    return [
        jnp.where(low, swapped[j], swapped[j + 1] if j + 1 < CHUNKS else chunks[j])
        for j in range(CHUNKS)
    ]


def behind_z(chunks, swapped, low):
    return [
        jnp.where(low, swapped[j - 1] if j else chunks[j], swapped[j]) for j in range(CHUNKS)
    ]


def swap_halves(chunks):
    return [pltpu.roll(c, 64, 1) for c in chunks]


def columns(j):
    return pl.ds(128 * j, 128)


def spread_sums(values):
    lane = iota((128, 128), 1)
    out = jnp.zeros((128, 128), F32)
    for n, value in enumerate(values):
        total = jnp.sum(jnp.sum(value, axis=0, keepdims=True), axis=1, keepdims=True)
        out = jnp.where(lane == n, total, out)
    return out


def gathered_sums(ref, count):
    sums = jnp.sum(ref[...], axis=0, keepdims=True)
    lane = iota((1, 128), 1)
    return [
        jnp.sum(jnp.where(lane == n, sums, 0.0), axis=1, keepdims=True) for n in range(count)
    ]


def warp_body(pos_ref, recv_ref, image_ref, taps_ref, valid_ref, grad_ref, misfit_ref, sums_ref, source_ref):
    recv = recv_ref[...]
    rows = iota((CELLS, 128), 0)
    for r in range(4):
        chosen = jnp.where(rows == pos_ref[pl.ds(r, 1), :], 1.0, 0.0).astype(BF16)
        source_ref[pl.ds(128 * r, 128), :] = dot(chosen, recv, TN)
    lane = iota((ROWS, 128), 1)
    low = lane < 64
    x_last = (lane & 7) == 7
    x_first = (lane & 7) == 0
    y_last = (lane & 56) == 56
    y_first = (lane & 56) == 0

    def block(i, carry):
        squares, counted = carry
        at = pl.ds(pl.multiple_of(i * ROWS, ROWS), ROWS)
        base = [source_ref[at, columns(j)] for j in range(CHUNKS)]
        along_x = [ahead(c, 1, x_last) for c in base]
        plane = [
            base,
            along_x,
            [ahead(c, 8, y_last) for c in base],
            [ahead(c, 8, y_last) for c in along_x],
        ]
        warped = None
        for tap in range(8):
            chunks = plane[tap % 4]
            if tap >= 4:
                chunks = ahead_z(chunks, swap_halves(chunks), low)
            terms = [
                taps_ref[tap, at, columns(j)].astype(F32) * chunks[j] for j in range(CHUNKS)
            ]
            warped = terms if warped is None else [w + t for w, t in zip(warped, terms)]
        swapped = swap_halves(warped)
        front = ahead_z(warped, swapped, low)
        back = behind_z(warped, swapped, low)
        for j in range(CHUNKS):
            field = warped[j]
            mask = valid_ref[at, columns(j)].astype(F32)
            half = 0.5 * mask
            grad_ref[0, at, columns(j)] = half * (front[j] - back[j])
            grad_ref[1, at, columns(j)] = half * (
                ahead(field, 8, y_last) - behind(field, 8, y_first)
            )
            grad_ref[2, at, columns(j)] = half * (
                ahead(field, 1, x_last) - behind(field, 1, x_first)
            )
            misfit = mask * (field - image_ref[at, columns(j)].astype(F32))
            misfit_ref[at, columns(j)] = misfit
            squares = squares + misfit * misfit
            counted = counted + mask
        return squares, counted

    zero = jnp.zeros((ROWS, 128), F32)
    squares, counted = lax.fori_loop(0, BLOCKS, block, (zero, zero))
    sums_ref[...] = spread_sums([squares, counted])


def high_z(j, shape):
    vz = 2 * j + (iota(shape, 1) >> 6)
    return (vz.astype(F32) + 0.5) * 0.125


def plane_basis(corner, lane):
    vy = (((lane >> 3) & 7).astype(F32) + 0.5) * 0.125
    vx = ((lane & 7).astype(F32) + 0.5) * 0.125
    along_y = (corner & 2) == 2
    along_x = (corner & 1) == 1
    return jnp.where(along_y, vy, 1.0 - vy) * jnp.where(along_x, vx, 1.0 - vx)


def force_nodes(misfit_at, inverse, grad_ref, near_ref, mid_ref, far_ref, parts_ref):
    high = [high_z(j, (1, 128)) for j in range(CHUNKS)]

    def block(i, carry):
        at = pl.ds(pl.multiple_of(i * ROWS, ROWS), ROWS)
        pull = []
        for j in range(CHUNKS):
            misfit = misfit_at(at, j)
            pull.append(misfit / (1.0 + misfit * misfit * inverse))
        for k in range(3):
            force = [pull[j] * grad_ref[k, at, columns(j)] for j in range(CHUNKS)]
            total = (force[0] + force[1]) + (force[2] + force[3])
            upper = (force[0] * high[0] + force[1] * high[1]) + (
                force[2] * high[2] + force[3] * high[3]
            )
            for a, value in enumerate((total - upper, upper)):
                coarse = value.astype(BF16)
                parts_ref[2 * k + a, at, pl.ds(0, 128)] = coarse
                parts_ref[2 * k + a, at, pl.ds(128, 128)] = (value - coarse.astype(F32)).astype(BF16)
        return carry

    lax.fori_loop(0, BLOCKS, block, 0)
    corner = iota((16, 256), 0)
    basis = jnp.where(corner < 4, plane_basis(corner, iota((16, 256), 1)), 0.0).astype(BF16)
    first = iota((16, 128), 1) == 0
    nodes = {}
    for k in range(3):
        for a in range(2):
            parts = dot(basis, parts_ref[2 * k + a], NT)
            for r in range(4):
                own = parts[:, 128 * r : 128 * r + 128]
                moved = jnp.where(first, 0.0, pltpu.roll(own, 1, 1))
                for b in range(2):
                    value = own[2 * b : 2 * b + 1] + moved[2 * b + 1 : 2 * b + 2]
                    key = (r % 2 + b, (r // 2 + a) * 3 + k)
                    nodes[key] = nodes[key] + value if key in nodes else value
    for y, ref in enumerate((near_ref, mid_ref, far_ref)):
        for row in range(9):
            ref[pl.ds(row, 1), :] = nodes[(y, row)]


def first_force_body(sums_ref, misfit_ref, grad_ref, near_ref, mid_ref, far_ref, parts_ref):
    square_sum, counted = gathered_sums(sums_ref, 2)
    inverse = 1.0 / (square_sum / counted + 1e-06)
    force_nodes(
        lambda at, j: misfit_ref[at, columns(j)],
        inverse,
        grad_ref,
        near_ref,
        mid_ref,
        far_ref,
        parts_ref,
    )


def second_spread(sums_ref, steps_ref):
    square_sum, counted = gathered_sums(sums_ref, 2)
    steep, curve, cross, moved_sum = gathered_sums(steps_ref, 4)
    step = steep / curve
    updated = jnp.maximum(square_sum + step * (2.0 * cross + step * moved_sum), 0.0)
    return step, 1.0 / (updated / counted + 1e-06)


def second_force_body(
    sums_ref, steps_ref, misfit_ref, change_ref, grad_ref, near_ref, mid_ref, far_ref, out_ref, parts_ref
):
    step, inverse = second_spread(sums_ref, steps_ref)

    def misfit_at(at, j):
        misfit = misfit_ref[at, columns(j)] + step * change_ref[at, columns(j)]
        out_ref[at, columns(j)] = misfit
        return misfit

    force_nodes(misfit_at, inverse, grad_ref, near_ref, mid_ref, far_ref, parts_ref)


def band_sums(near_ref, mid_ref, far_ref, below_ref, above_ref):
    band = lax.axis_index("grp")
    last = lax.axis_size("grp") - 1
    near = near_ref[...] + jnp.where(band > 0, below_ref[...], 0.0)
    far = jnp.where(band < last, far_ref[...] + above_ref[...], 0.0)
    return near, mid_ref[...], far


def edge_body(near_ref, mid_ref, far_ref, below_ref, above_ref, down_ref, up_ref):
    for y, part in enumerate(band_sums(near_ref, mid_ref, far_ref, below_ref, above_ref)):
        down_ref[pl.ds(3 * y, 3), :] = part[0:3]
        up_ref[pl.ds(3 * y, 3), :] = part[6:9]


def move_body(
    near_ref, mid_ref, far_ref, below_ref, above_ref, under_ref, over_ref,
    sums_ref, steps_ref, misfit_ref, grad_ref, change_ref, out_ref, dir_ref, fields_ref, second,
):
    slab = lax.axis_index("slab")
    last = lax.axis_size("slab") - 1
    bands = band_sums(near_ref, mid_ref, far_ref, below_ref, above_ref)
    steep = jnp.zeros((1, 128), F32)
    nodes = {}
    for y in range(3):
        under = jnp.where(slab > 0, under_ref[pl.ds(3 * y, 3), :], 0.0)
        over = over_ref[pl.ds(3 * y, 3), :]
        layers = (
            bands[y][0:3] + under,
            bands[y][3:6],
            jnp.where(slab < last, bands[y][6:9] + over, 0.0),
        )
        for z, layer in enumerate(layers):
            direction = -layer
            if z < 2 and y < 2:
                for k in range(3):
                    dir_ref[k, z, pl.ds(y, 1), :] = direction[k : k + 1]
                steep = steep + jnp.sum(direction * direction, axis=0, keepdims=True)
            nodes[(z, y)] = jnp.concatenate([direction[k : k + 1] for k in range(3)], axis=1)
    end = (iota((1, 384), 1) & 127) == 127
    shifted = {key: jnp.where(end, 0.0, pltpu.roll(value, 383, 1)) for key, value in nodes.items()}
    rank = iota((24, 256), 0)
    lane = iota((24, 256), 1)
    basis = jnp.where(((rank >> 2) & 1) == (lane >> 7), plane_basis(rank & 3, lane), 0.0).astype(BF16)
    for r in range(4):
        rows = []
        for corner in range(8):
            key = (r // 2 + corner // 4, r % 2 + corner // 2 % 2)
            rows.append(shifted[key] if corner % 2 else nodes[key])
        full = jnp.concatenate(rows, axis=0)
        coarse = full.astype(BF16).astype(F32)
        rest = full - coarse
        middle = rest.astype(BF16).astype(F32)
        split = jnp.concatenate([coarse, middle, rest - middle], axis=0)
        fields_ref[r] = dot(split.astype(BF16), basis, TN)
    if second:
        _, inverse = second_spread(sums_ref, steps_ref)
    else:
        square_sum, counted = gathered_sums(sums_ref, 2)
        inverse = 1.0 / (square_sum / counted + 1e-06)
    high = [high_z(j, (1, 128)) for j in range(CHUNKS)]

    def block(i, carry):
        curve, cross, moved_sum = carry
        at = pl.ds(pl.multiple_of(i * ROWS, ROWS), ROWS)
        r = i // (128 // ROWS)
        x = (i % (128 // ROWS)) * ROWS
        change = [None] * CHUNKS
        for k in range(3):
            cells = pl.ds(pl.multiple_of(128 * k + x, ROWS), ROWS)
            lower = fields_ref[r, cells, pl.ds(0, 128)]
            slope = fields_ref[r, cells, pl.ds(128, 128)] - lower
            for j in range(CHUNKS):
                term = grad_ref[k, at, columns(j)] * (lower + high[j] * slope)
                change[j] = term if k == 0 else change[j] + term
        for j in range(CHUNKS):
            misfit = misfit_ref[at, columns(j)]
            change_ref[at, columns(j)] = change[j]
            square = change[j] * change[j]
            curve = curve + square / (1.0 + misfit * misfit * inverse)
            if not second:
                cross = cross + misfit * change[j]
                moved_sum = moved_sum + square
        return curve, cross, moved_sum

    zero = jnp.zeros((ROWS, 128), F32)
    curve, cross, moved_sum = lax.fori_loop(0, BLOCKS, block, (zero, zero, zero))
    out_ref[...] = spread_sums([steep, curve] + ([] if second else [cross, moved_sum]))


def first_move_body(
    near_ref, mid_ref, far_ref, below_ref, above_ref, under_ref, over_ref,
    sums_ref, misfit_ref, grad_ref, change_ref, out_ref, dir_ref, fields_ref,
):
    move_body(
        near_ref, mid_ref, far_ref, below_ref, above_ref, under_ref, over_ref,
        sums_ref, None, misfit_ref, grad_ref, change_ref, out_ref, dir_ref, fields_ref, False,
    )


def second_move_body(
    near_ref, mid_ref, far_ref, below_ref, above_ref, under_ref, over_ref,
    sums_ref, steps_ref, misfit_ref, grad_ref, change_ref, out_ref, dir_ref, fields_ref,
):
    move_body(
        near_ref, mid_ref, far_ref, below_ref, above_ref, under_ref, over_ref,
        sums_ref, steps_ref, misfit_ref, grad_ref, change_ref, out_ref, dir_ref, fields_ref, True,
    )


def finish_body(first_ref, second_ref, dir0_ref, dir1_ref, misfit_ref, change_ref, coef_ref, out_ref):
    steep, curve = gathered_sums(first_ref, 2)
    step0 = steep / curve
    steep, curve = gathered_sums(second_ref, 2)
    step1 = steep / curve
    coef_ref[...] = step0.reshape(1, 1, 1, 1) * dir0_ref[...] + step1.reshape(1, 1, 1, 1) * dir1_ref[...]
    out_ref[...] = misfit_ref[...] + step1 * change_ref[...]


def around(block, axis, distance):
    size = lax.axis_size(axis)
    return lax.ppermute(block, axis, [(i, (i + distance) % size) for i in range(size)])


def to_all(sums):
    return lax.all_to_all(sums, EVERY, 0, 0, tiled=True)


def halo(near, mid, far):
    below = around(far, "grp", 1)
    above = around(near, "grp", -1)
    down, up = call(edge_body, [((9, 128), F32)] * 2, (near, mid, far, below, above), "edges")
    under = around(up, "slab", 1)
    over = around(down, "slab", -1)
    return below, above, under, over


def shards(reference_bricks, deformed, tap_weights, valid_voxels, sources):
    big = ((CELLS, 512), F32)
    sums_shape = ((128, 128), F32)
    nodes_shape = [((9, 128), F32)] * 3
    dir_shape = ((3, 2, 2, 128), F32)
    grad_shape = ((3, CELLS, 512), F32)
    parts = [pltpu.VMEM((6, CELLS, 256), BF16)]
    fields = [pltpu.VMEM((4, 384, 256), F32)]
    taps = tap_weights.reshape(8, CELLS, 512)
    image = deformed.reshape(CELLS, 512)
    valid = valid_voxels.reshape(CELLS, 512)

    pos, want = call(wanted_body, [((4, 128), I32), ((16, 128), I32)], (sources,), "wanted")
    asked = lax.all_to_all(want, "slab", 0, 0, tiled=True)
    (sent,) = call(pick_body, [((CELLS, 512), BF16)], (asked, reference_bricks), "pick")
    recv = lax.all_to_all(sent, "slab", 0, 0, tiled=True)
    grads, misfit, sums = call(
        warp_body,
        [grad_shape, big, sums_shape],
        (pos, recv, image, taps, valid),
        "warp",
        [pltpu.VMEM((CELLS, 512), F32)],
    )
    sums = to_all(sums)
    near, mid, far = call(first_force_body, nodes_shape, (sums, misfit, grads), "force_first", parts)
    below, above, under, over = halo(near, mid, far)
    change, steps, dir0 = call(
        first_move_body,
        [big, sums_shape, dir_shape],
        (near, mid, far, below, above, under, over, sums, misfit, grads),
        "move_first",
        fields,
    )
    first = to_all(steps)
    near, mid, far, misfit = call(
        second_force_body,
        nodes_shape + [big],
        (sums, first, misfit, change, grads),
        "force_second",
        parts,
    )
    below, above, under, over = halo(near, mid, far)
    change, steps, dir1 = call(
        second_move_body,
        [big, sums_shape, dir_shape],
        (near, mid, far, below, above, under, over, sums, first, misfit, grads),
        "move_second",
        fields,
    )
    second = to_all(steps)
    coefficients, residual = call(
        finish_body, [dir_shape, big], (first, second, dir0, dir1, misfit, change), "finish"
    )
    return (coefficients, residual.reshape(2, 2, 128, 512))


def solution(mesh):
    in_specs = (
        P("grp", "slab", None),
        P("slab", "grp", None, None),
        P(None, "slab", "grp", None, None),
        P("slab", "grp", None, None),
        P("slab", "grp", None),
    )
    out_specs = (P(None, "slab", "grp", None), P("slab", "grp", None, None))
    return jax.shard_map(shards, mesh=mesh, in_specs=in_specs, out_specs=out_specs, check_vma=False)
```

```python
import jax
import jax.numpy as jnp
from jax import lax
from jax.experimental import pallas as pl
from jax.experimental.pallas import tpu as pltpu
from jax.sharding import PartitionSpec as P

F32 = jnp.float32
BF16 = jnp.bfloat16
I32 = jnp.int32
EVERY = ("slab", "grp")
CELLS = 512
ROWS = 16
BLOCKS = CELLS // ROWS
CHUNKS = 4
NT = (((1,), (1,)), ((), ()))
TN = (((0,), (0,)), ((), ()))
VMEM = pl.BlockSpec(memory_space=pltpu.VMEM)
HBM = pl.BlockSpec(memory_space=pltpu.HBM)


def iota(shape, axis):
    return lax.broadcasted_iota(I32, shape, axis)


def dot(a, b, dims):
    return lax.dot_general(a, b, dims, preferred_element_type=F32)


def call(body, outs, ins, name, scratch=(), limit=16, far=()):
    return pl.pallas_call(
        body,
        out_shape=[jax.ShapeDtypeStruct(s, d) for s, d in outs],
        in_specs=[HBM if n in far else VMEM for n in range(len(ins))],
        out_specs=[VMEM] * len(outs),
        scratch_shapes=list(scratch),
        compiler_params=pltpu.CompilerParams(vmem_limit_bytes=limit << 20),
        name=name,
    )(*[pltpu.with_memory_space_constraint(x, pltpu.HBM) if n in far else x for n, x in enumerate(ins)])


def wanted_body(src_hbm, bricks_hbm, pos_ref, want_ref, bricks_ref, src_ref, sems):
    first = pltpu.make_async_copy(src_hbm, src_ref, sems.at[0])
    fetch = pltpu.make_async_copy(bricks_hbm, bricks_ref, sems.at[1])
    first.start()
    fetch.start()
    place = 32 * (lax.axis_index("slab") % 4)
    earlier = (iota((128, 128), 0) < iota((128, 128), 1)).astype(F32).astype(BF16)
    owners = iota((16, 128), 0)
    lanes = iota((128, 128), 0)
    before = jnp.zeros((16, 1), F32)
    want = jnp.zeros((32, 128), F32)
    first.wait()
    for r in range(4):
        src = src_ref[r // 2, pl.ds(r % 2, 1), :]
        owner = src >> 9
        row = src & 511
        mine = jnp.where(owners == owner, 1.0, 0.0)
        count = dot(mine.astype(BF16), earlier, (((1,), (0,)), ((), ()))) + before
        before = before + jnp.sum(mine, axis=1, keepdims=True)
        rank = jnp.sum(mine * count, axis=0, keepdims=True).astype(I32)
        pos_ref[pl.ds(r, 1), :] = owner * 32 + rank
        slot = jnp.where(lanes == rank + place, 1.0, 0.0).astype(BF16)
        low = (row & 255).astype(F32)
        high = (row >> 8).astype(F32)
        parts = jnp.concatenate([mine * low, mine * high], axis=0).astype(BF16)
        want = want + dot(parts, slot, NT)
    want_ref[...] = (want[:16] + 256.0 * want[16:]).astype(I32)
    fetch.wait()


def pick_body(want_ref, bricks_ref, out_ref):
    bricks = bricks_ref[...]
    rows = iota((CELLS, 128), 0)
    for r in range(4):
        index = jnp.sum(want_ref[pl.ds(4 * r, 4), :], axis=0, keepdims=True)
        chosen = jnp.where(rows == index, 1.0, 0.0).astype(BF16)
        out_ref[pl.ds(128 * r, 128), :] = dot(chosen, bricks, TN).astype(BF16)


def columns(j):
    return pl.ds(128 * j, 128)


def spread_sums(values):
    lane = iota((128, 128), 1)
    out = jnp.zeros((128, 128), F32)
    for n, value in enumerate(values):
        total = jnp.sum(jnp.sum(value, axis=0, keepdims=True), axis=1, keepdims=True)
        out = jnp.where(lane == n, total, out)
    return out


def gathered_sums(ref, count):
    sums = jnp.sum(ref[...], axis=0, keepdims=True)
    lane = iota((1, 128), 1)
    return [
        jnp.sum(jnp.where(lane == n, sums, 0.0), axis=1, keepdims=True) for n in range(count)
    ]


def shift_table(width, last):
    at = iota((1, 896), 1)
    tap = (at >> 7) + 1
    lane = at & 127
    step_x = jnp.where(((tap & 1) == 1) & ((lane & 7) < 7), 1, 0)
    step_y = jnp.where(((tap & 2) == 2) & ((lane & 56) < 56), 8, 0)
    rise = (tap & 4) == 4
    if last:
        rise = rise & (lane < 64)
    target = lane + step_x + step_y + jnp.where(rise, 64, 0)
    return jnp.where(iota((width, 896), 0) == target, 1.0, 0.0).astype(BF16)


def slope_table():
    at = iota((1, 256), 1)
    lane = at & 127
    along_x = at >= 128
    place = jnp.where(along_x, lane & 7, (lane >> 3) & 7)
    stride = jnp.where(along_x, 1, 8)
    front = lane + jnp.where(place < 7, stride, 0)
    back = lane - jnp.where(place > 0, stride, 0)
    row = iota((256, 256), 0) & 127
    return (jnp.where(row == front, 0.5, 0.0) - jnp.where(row == back, 0.5, 0.0)).astype(BF16)


def warp_body(
    pos_ref, recv_ref, image_hbm, taps_hbm, valid_hbm, grad_ref, misfit_ref, sums_ref,
    source_ref, planes_ref, split_ref, mask_ref, image_ref, taps_ref, valid_ref, sems,
):
    copies = []
    for r in range(4):
        at = pl.ds(128 * r, 128)
        copies.append(
            [
                pltpu.make_async_copy(taps_hbm.at[:, at], taps_ref.at[:, at], sems.at[0, r]),
                pltpu.make_async_copy(valid_hbm.at[at], valid_ref.at[at], sems.at[1, r]),
                pltpu.make_async_copy(image_hbm.at[at], image_ref.at[at], sems.at[2, r]),
            ]
        )
    for group in copies:
        for copy in group:
            copy.start()
    recv = recv_ref[...]
    rows = iota((CELLS, 128), 0)
    for r in range(4):
        at = pl.ds(128 * r, 128)
        chosen = jnp.where(rows == pos_ref[pl.ds(r, 1), :], 1.0, 0.0).astype(BF16)
        picked = dot(chosen, recv, TN)
        planes_ref[0, at, :] = picked
        source_ref[at, :] = picked.astype(BF16)
    inner = shift_table(256, False)
    outer = shift_table(128, True)
    for j in range(CHUNKS):
        if j + 1 < CHUNKS:
            shifted = dot(source_ref[:, pl.ds(128 * j, 256)], inner, (((1,), (0,)), ((), ())))
        else:
            shifted = dot(source_ref[:, columns(j)], outer, (((1,), (0,)), ((), ())))
        for tap in range(7):
            planes_ref[tap + 1, :, columns(j)] = shifted[:, 128 * tap : 128 * tap + 128]
    low = iota((ROWS, 128), 1) < 64

    def block(i, carry):
        squares, counted = carry
        at = pl.ds(pl.multiple_of(i * ROWS, ROWS), ROWS)
        warped = []
        for j in range(CHUNKS):
            terms = [
                taps_ref[tap, at, columns(j)].astype(F32) * planes_ref[tap, at, columns(j)]
                for tap in range(8)
            ]
            warped.append(
                ((terms[0] + terms[1]) + (terms[2] + terms[3]))
                + ((terms[4] + terms[5]) + (terms[6] + terms[7]))
            )
        swapped = [pltpu.roll(c, 64, 1) for c in warped]
        for j in range(CHUNKS):
            field = warped[j]
            mask = valid_ref[at, columns(j)].astype(F32)
            mask_ref[at, columns(j)] = mask
            front = jnp.where(low, swapped[j], swapped[j + 1] if j + 1 < CHUNKS else field)
            back = jnp.where(low, swapped[j - 1] if j else field, swapped[j])
            grad_ref[0, at, columns(j)] = (0.5 * mask) * (front - back)
            coarse = field.astype(BF16)
            split_ref[at, pl.ds(256 * j, 128)] = coarse
            split_ref[at, pl.ds(256 * j + 128, 128)] = (field - coarse.astype(F32)).astype(BF16)
            misfit = mask * (field - image_ref[at, columns(j)].astype(F32))
            misfit_ref[at, columns(j)] = misfit
            squares = squares + misfit * misfit
            counted = counted + mask
        return squares, counted

    zero = jnp.zeros((ROWS, 128), F32)
    carry = (zero, zero)
    for r in range(4):
        for copy in copies[r]:
            copy.wait()
        carry = lax.fori_loop(128 * r // ROWS, 128 * (r + 1) // ROWS, block, carry)
    sums_ref[...] = spread_sums(list(carry))
    table = slope_table()
    for j in range(CHUNKS):
        slopes = dot(split_ref[:, pl.ds(256 * j, 256)], table, (((1,), (0,)), ((), ())))
        mask = mask_ref[:, columns(j)]
        grad_ref[1, :, columns(j)] = mask * slopes[:, :128]
        grad_ref[2, :, columns(j)] = mask * slopes[:, 128:]


def high_z(j, shape):
    vz = 2 * j + (iota(shape, 1) >> 6)
    return (vz.astype(F32) + 0.5) * 0.125


def plane_basis(corner, lane):
    vy = (((lane >> 3) & 7).astype(F32) + 0.5) * 0.125
    vx = ((lane & 7).astype(F32) + 0.5) * 0.125
    along_y = (corner & 2) == 2
    along_x = (corner & 1) == 1
    return jnp.where(along_y, vy, 1.0 - vy) * jnp.where(along_x, vx, 1.0 - vx)


def force_nodes(misfit_at, inverse, grad_ref, near_ref, mid_ref, far_ref, parts_ref):
    high = [high_z(j, (1, 128)) for j in range(CHUNKS)]

    def block(i, carry):
        at = pl.ds(pl.multiple_of(i * ROWS, ROWS), ROWS)
        pull = []
        for j in range(CHUNKS):
            misfit = misfit_at(at, j)
            pull.append(misfit / (1.0 + misfit * misfit * inverse))
        for k in range(3):
            force = [pull[j] * grad_ref[k, at, columns(j)] for j in range(CHUNKS)]
            total = (force[0] + force[1]) + (force[2] + force[3])
            upper = (force[0] * high[0] + force[1] * high[1]) + (
                force[2] * high[2] + force[3] * high[3]
            )
            for a, value in enumerate((total - upper, upper)):
                coarse = value.astype(BF16)
                parts_ref[2 * k + a, at, pl.ds(0, 128)] = coarse
                parts_ref[2 * k + a, at, pl.ds(128, 128)] = (value - coarse.astype(F32)).astype(BF16)
        return carry

    lax.fori_loop(0, BLOCKS, block, 0)
    corner = iota((16, 256), 0)
    basis = jnp.where(corner < 4, plane_basis(corner, iota((16, 256), 1)), 0.0).astype(BF16)
    first = iota((16, 128), 1) == 0
    nodes = {}
    for k in range(3):
        for a in range(2):
            parts = dot(basis, parts_ref[2 * k + a], NT)
            for r in range(4):
                own = parts[:, 128 * r : 128 * r + 128]
                moved = jnp.where(first, 0.0, pltpu.roll(own, 1, 1))
                for b in range(2):
                    value = own[2 * b : 2 * b + 1] + moved[2 * b + 1 : 2 * b + 2]
                    key = (r % 2 + b, (r // 2 + a) * 3 + k)
                    nodes[key] = nodes[key] + value if key in nodes else value
    for y, ref in enumerate((near_ref, mid_ref, far_ref)):
        for row in range(9):
            ref[pl.ds(row, 1), :] = nodes[(y, row)]


def first_force_body(sums_ref, misfit_ref, grad_ref, near_ref, mid_ref, far_ref, parts_ref):
    square_sum, counted = gathered_sums(sums_ref, 2)
    inverse = 1.0 / (square_sum / counted + 1e-06)
    force_nodes(
        lambda at, j: misfit_ref[at, columns(j)],
        inverse,
        grad_ref,
        near_ref,
        mid_ref,
        far_ref,
        parts_ref,
    )


def second_spread(sums_ref, steps_ref):
    square_sum, counted = gathered_sums(sums_ref, 2)
    steep, curve, cross, moved_sum = gathered_sums(steps_ref, 4)
    step = steep / curve
    updated = jnp.maximum(square_sum + step * (2.0 * cross + step * moved_sum), 0.0)
    return step, 1.0 / (updated / counted + 1e-06)


def second_force_body(
    sums_ref, steps_ref, misfit_ref, change_ref, grad_ref, near_ref, mid_ref, far_ref, out_ref, parts_ref
):
    step, inverse = second_spread(sums_ref, steps_ref)

    def misfit_at(at, j):
        misfit = misfit_ref[at, columns(j)] + step * change_ref[at, columns(j)]
        out_ref[at, columns(j)] = misfit
        return misfit

    force_nodes(misfit_at, inverse, grad_ref, near_ref, mid_ref, far_ref, parts_ref)


def band_sums(near_ref, mid_ref, far_ref, below_ref, above_ref):
    band = lax.axis_index("grp")
    last = lax.axis_size("grp") - 1
    near = near_ref[...] + jnp.where(band > 0, below_ref[...], 0.0)
    far = jnp.where(band < last, far_ref[...] + above_ref[...], 0.0)
    return near, mid_ref[...], far


def edge_body(near_ref, mid_ref, far_ref, below_ref, above_ref, down_ref, up_ref):
    for y, part in enumerate(band_sums(near_ref, mid_ref, far_ref, below_ref, above_ref)):
        down_ref[pl.ds(3 * y, 3), :] = part[0:3]
        up_ref[pl.ds(3 * y, 3), :] = part[6:9]


def move_body(
    near_ref, mid_ref, far_ref, below_ref, above_ref, under_ref, over_ref,
    sums_ref, steps_ref, misfit_ref, grad_ref, change_ref, out_ref, dir_ref, fields_ref, second,
):
    slab = lax.axis_index("slab")
    last = lax.axis_size("slab") - 1
    bands = band_sums(near_ref, mid_ref, far_ref, below_ref, above_ref)
    steep = jnp.zeros((1, 128), F32)
    nodes = {}
    for y in range(3):
        under = jnp.where(slab > 0, under_ref[pl.ds(3 * y, 3), :], 0.0)
        over = over_ref[pl.ds(3 * y, 3), :]
        layers = (
            bands[y][0:3] + under,
            bands[y][3:6],
            jnp.where(slab < last, bands[y][6:9] + over, 0.0),
        )
        for z, layer in enumerate(layers):
            direction = -layer
            if z < 2 and y < 2:
                for k in range(3):
                    dir_ref[k, z, pl.ds(y, 1), :] = direction[k : k + 1]
                steep = steep + jnp.sum(direction * direction, axis=0, keepdims=True)
            nodes[(z, y)] = jnp.concatenate([direction[k : k + 1] for k in range(3)], axis=1)
    end = (iota((1, 384), 1) & 127) == 127
    shifted = {key: jnp.where(end, 0.0, pltpu.roll(value, 383, 1)) for key, value in nodes.items()}
    rank = iota((24, 256), 0)
    lane = iota((24, 256), 1)
    basis = jnp.where(((rank >> 2) & 1) == (lane >> 7), plane_basis(rank & 3, lane), 0.0).astype(BF16)
    for r in range(4):
        rows = []
        for corner in range(8):
            key = (r // 2 + corner // 4, r % 2 + corner // 2 % 2)
            rows.append(shifted[key] if corner % 2 else nodes[key])
        full = jnp.concatenate(rows, axis=0)
        coarse = full.astype(BF16).astype(F32)
        rest = full - coarse
        middle = rest.astype(BF16).astype(F32)
        split = jnp.concatenate([coarse, middle, rest - middle], axis=0)
        fields_ref[r] = dot(split.astype(BF16), basis, TN)
    if second:
        _, inverse = second_spread(sums_ref, steps_ref)
    else:
        square_sum, counted = gathered_sums(sums_ref, 2)
        inverse = 1.0 / (square_sum / counted + 1e-06)
    high = [high_z(j, (1, 128)) for j in range(CHUNKS)]

    def block(i, carry):
        curve, cross, moved_sum = carry
        at = pl.ds(pl.multiple_of(i * ROWS, ROWS), ROWS)
        r = i // (128 // ROWS)
        x = (i % (128 // ROWS)) * ROWS
        change = [None] * CHUNKS
        for k in range(3):
            cells = pl.ds(pl.multiple_of(128 * k + x, ROWS), ROWS)
            lower = fields_ref[r, cells, pl.ds(0, 128)]
            slope = fields_ref[r, cells, pl.ds(128, 128)] - lower
            for j in range(CHUNKS):
                term = grad_ref[k, at, columns(j)] * (lower + high[j] * slope)
                change[j] = term if k == 0 else change[j] + term
        for j in range(CHUNKS):
            misfit = misfit_ref[at, columns(j)]
            change_ref[at, columns(j)] = change[j]
            square = change[j] * change[j]
            curve = curve + square / (1.0 + misfit * misfit * inverse)
            if not second:
                cross = cross + misfit * change[j]
                moved_sum = moved_sum + square
        return curve, cross, moved_sum

    zero = jnp.zeros((ROWS, 128), F32)
    curve, cross, moved_sum = lax.fori_loop(0, BLOCKS, block, (zero, zero, zero))
    out_ref[...] = spread_sums([steep, curve] + ([] if second else [cross, moved_sum]))


def first_move_body(
    near_ref, mid_ref, far_ref, below_ref, above_ref, under_ref, over_ref,
    sums_ref, misfit_ref, grad_ref, change_ref, out_ref, dir_ref, fields_ref,
):
    move_body(
        near_ref, mid_ref, far_ref, below_ref, above_ref, under_ref, over_ref,
        sums_ref, None, misfit_ref, grad_ref, change_ref, out_ref, dir_ref, fields_ref, False,
    )


def second_move_body(
    near_ref, mid_ref, far_ref, below_ref, above_ref, under_ref, over_ref,
    sums_ref, steps_ref, misfit_ref, grad_ref, change_ref, out_ref, dir_ref, fields_ref,
):
    move_body(
        near_ref, mid_ref, far_ref, below_ref, above_ref, under_ref, over_ref,
        sums_ref, steps_ref, misfit_ref, grad_ref, change_ref, out_ref, dir_ref, fields_ref, True,
    )


def finish_body(first_ref, second_ref, dir0_ref, dir1_ref, misfit_ref, change_ref, coef_ref, out_ref):
    steep, curve = gathered_sums(first_ref, 2)
    step0 = steep / curve
    steep, curve = gathered_sums(second_ref, 2)
    step1 = steep / curve
    coef_ref[...] = step0.reshape(1, 1, 1, 1) * dir0_ref[...] + step1.reshape(1, 1, 1, 1) * dir1_ref[...]
    out_ref[...] = misfit_ref[...] + step1 * change_ref[...]


def around(block, axis, distance):
    size = lax.axis_size(axis)
    return lax.ppermute(block, axis, [(i, (i + distance) % size) for i in range(size)])


def to_all(sums):
    return lax.all_to_all(sums, EVERY, 0, 0, tiled=True)


def halo(near, mid, far):
    below = around(far, "grp", 1)
    above = around(near, "grp", -1)
    down, up = call(edge_body, [((9, 128), F32)] * 2, (near, mid, far, below, above), "edges")
    under = around(up, "slab", 1)
    over = around(down, "slab", -1)
    return below, above, under, over


def shards(reference_bricks, deformed, tap_weights, valid_voxels, sources):
    big = ((CELLS, 512), F32)
    sums_shape = ((128, 128), F32)
    nodes_shape = [((9, 128), F32)] * 3
    dir_shape = ((3, 2, 2, 128), F32)
    grad_shape = ((3, CELLS, 512), F32)
    parts = [pltpu.VMEM((6, CELLS, 256), BF16)]
    fields = [pltpu.VMEM((4, 384, 256), F32)]
    taps = tap_weights.reshape(8, CELLS, 512)
    image = deformed.reshape(CELLS, 512)
    valid = valid_voxels.reshape(CELLS, 512)

    pos, want, bricks = call(
        wanted_body,
        [((4, 128), I32), ((16, 128), I32), ((CELLS, 512), BF16)],
        (sources, reference_bricks.reshape(CELLS, 512)),
        "wanted",
        [pltpu.VMEM((2, 2, 128), I32), pltpu.SemaphoreType.DMA((2,))],
        far=(0, 1),
    )
    asked = lax.all_to_all(want, "slab", 0, 0, tiled=True)
    (sent,) = call(pick_body, [((CELLS, 512), BF16)], (asked, bricks), "pick")
    recv = lax.all_to_all(sent, "slab", 0, 0, tiled=True)
    grads, misfit, sums = call(
        warp_body,
        [grad_shape, big, sums_shape],
        (pos, recv, image, taps, valid),
        "warp",
        [
            pltpu.VMEM((CELLS, 512), BF16),
            pltpu.VMEM((8, CELLS, 512), F32),
            pltpu.VMEM((CELLS, 1024), BF16),
            pltpu.VMEM((CELLS, 512), F32),
            pltpu.VMEM((CELLS, 512), BF16),
            pltpu.VMEM((8, CELLS, 512), BF16),
            pltpu.VMEM((CELLS, 512), I32),
            pltpu.SemaphoreType.DMA((3, 4)),
        ],
        40,
        (2, 3, 4),
    )
    sums = to_all(sums)
    near, mid, far = call(first_force_body, nodes_shape, (sums, misfit, grads), "force_first", parts)
    below, above, under, over = halo(near, mid, far)
    change, steps, dir0 = call(
        first_move_body,
        [big, sums_shape, dir_shape],
        (near, mid, far, below, above, under, over, sums, misfit, grads),
        "move_first",
        fields,
    )
    first = to_all(steps)
    near, mid, far, misfit = call(
        second_force_body,
        nodes_shape + [big],
        (sums, first, misfit, change, grads),
        "force_second",
        parts,
    )
    below, above, under, over = halo(near, mid, far)
    change, steps, dir1 = call(
        second_move_body,
        [big, sums_shape, dir_shape],
        (near, mid, far, below, above, under, over, sums, first, misfit, grads),
        "move_second",
        fields,
    )
    second = to_all(steps)
    coefficients, residual = call(
        finish_body, [dir_shape, big], (first, second, dir0, dir1, misfit, change), "finish"
    )
    return (coefficients, residual.reshape(2, 2, 128, 512))


def solution(mesh):
    in_specs = (
        P("grp", "slab", None),
        P("slab", "grp", None, None),
        P(None, "slab", "grp", None, None),
        P("slab", "grp", None, None),
        P("slab", "grp", None),
    )
    out_specs = (P(None, "slab", "grp", None), P("slab", "grp", None, None))
    return jax.shard_map(shards, mesh=mesh, in_specs=in_specs, out_specs=out_specs, check_vma=False)
```

```python
import jax
import jax.numpy as jnp
from jax import lax
from jax.experimental import pallas as pl
from jax.experimental.pallas import tpu as pltpu
from jax.sharding import PartitionSpec as P

F32 = jnp.float32
BF16 = jnp.bfloat16
I32 = jnp.int32
EVERY = ("slab", "grp")
CELLS = 512
ROWS = 16
BLOCKS = CELLS // ROWS
CHUNKS = 4
NT = (((1,), (1,)), ((), ()))
TN = (((0,), (0,)), ((), ()))
VMEM = pl.BlockSpec(memory_space=pltpu.VMEM)
HBM = pl.BlockSpec(memory_space=pltpu.HBM)


def iota(shape, axis):
    return lax.broadcasted_iota(I32, shape, axis)


def dot(a, b, dims):
    return lax.dot_general(a, b, dims, preferred_element_type=F32)


def call(body, outs, ins, name, scratch=(), limit=16, far=()):
    return pl.pallas_call(
        body,
        out_shape=[jax.ShapeDtypeStruct(s, d) for s, d in outs],
        in_specs=[HBM if n in far else VMEM for n in range(len(ins))],
        out_specs=[VMEM] * len(outs),
        scratch_shapes=list(scratch),
        compiler_params=pltpu.CompilerParams(vmem_limit_bytes=limit << 20),
        name=name,
    )(*[pltpu.with_memory_space_constraint(x, pltpu.HBM) if n in far else x for n, x in enumerate(ins)])


def wanted_body(src_hbm, bricks_hbm, pos_ref, want_ref, bricks_ref, src_ref, sems):
    first = pltpu.make_async_copy(src_hbm, src_ref, sems.at[0])
    fetch = pltpu.make_async_copy(bricks_hbm, bricks_ref, sems.at[1])
    first.start()
    fetch.start()
    place = 32 * (lax.axis_index("slab") % 4)
    earlier = (iota((128, 128), 0) < iota((128, 128), 1)).astype(F32).astype(BF16)
    owners = iota((16, 128), 0)
    lanes = iota((128, 128), 0)
    before = jnp.zeros((16, 1), F32)
    want = jnp.zeros((32, 128), F32)
    first.wait()
    for r in range(4):
        src = src_ref[r // 2, pl.ds(r % 2, 1), :]
        owner = src >> 9
        row = src & 511
        mine = jnp.where(owners == owner, 1.0, 0.0)
        count = dot(mine.astype(BF16), earlier, (((1,), (0,)), ((), ()))) + before
        before = before + jnp.sum(mine, axis=1, keepdims=True)
        rank = jnp.sum(mine * count, axis=0, keepdims=True).astype(I32)
        pos_ref[pl.ds(r, 1), :] = owner * 32 + rank
        slot = jnp.where(lanes == rank + place, 1.0, 0.0).astype(BF16)
        low = (row & 255).astype(F32)
        high = (row >> 8).astype(F32)
        parts = jnp.concatenate([mine * low, mine * high], axis=0).astype(BF16)
        want = want + dot(parts, slot, NT)
    want_ref[...] = (want[:16] + 256.0 * want[16:]).astype(I32)
    fetch.wait()


def pick_body(want_ref, bricks_ref, out_ref):
    bricks = bricks_ref[...]
    rows = iota((CELLS, 128), 0)
    for r in range(4):
        index = jnp.sum(want_ref[pl.ds(4 * r, 4), :], axis=0, keepdims=True)
        chosen = jnp.where(rows == index, 1.0, 0.0).astype(BF16)
        out_ref[pl.ds(128 * r, 128), :] = dot(chosen, bricks, TN).astype(BF16)


def columns(j):
    return pl.ds(128 * j, 128)


def spread_sums(values):
    lane = iota((128, 128), 1)
    out = jnp.zeros((128, 128), F32)
    for n, value in enumerate(values):
        total = jnp.sum(jnp.sum(value, axis=0, keepdims=True), axis=1, keepdims=True)
        out = jnp.where(lane == n, total, out)
    return out


def gathered_sums(ref, count):
    sums = jnp.sum(ref[...], axis=0, keepdims=True)
    lane = iota((1, 128), 1)
    return [
        jnp.sum(jnp.where(lane == n, sums, 0.0), axis=1, keepdims=True) for n in range(count)
    ]


def shift_table(width, last):
    at = iota((1, 896), 1)
    tap = (at >> 7) + 1
    lane = at & 127
    step_x = jnp.where(((tap & 1) == 1) & ((lane & 7) < 7), 1, 0)
    step_y = jnp.where(((tap & 2) == 2) & ((lane & 56) < 56), 8, 0)
    rise = (tap & 4) == 4
    if last:
        rise = rise & (lane < 64)
    target = lane + step_x + step_y + jnp.where(rise, 64, 0)
    return jnp.where(iota((width, 896), 0) == target, 1.0, 0.0).astype(BF16)


def slope_table():
    at = iota((1, 256), 1)
    lane = at & 127
    along_x = at >= 128
    place = jnp.where(along_x, lane & 7, (lane >> 3) & 7)
    stride = jnp.where(along_x, 1, 8)
    front = lane + jnp.where(place < 7, stride, 0)
    back = lane - jnp.where(place > 0, stride, 0)
    row = iota((256, 256), 0) & 127
    return (jnp.where(row == front, 0.5, 0.0) - jnp.where(row == back, 0.5, 0.0)).astype(BF16)


def warp_body(
    pos_ref, recv_ref, image_hbm, taps_hbm, valid_hbm, grad_ref, misfit_ref, sums_ref,
    source_ref, planes_ref, split_ref, mask_ref, image_ref, taps_ref, valid_ref, sems,
):
    copies = []
    for r in range(4):
        at = pl.ds(128 * r, 128)
        copies.append(
            [
                pltpu.make_async_copy(taps_hbm.at[:, at], taps_ref.at[:, at], sems.at[0, r]),
                pltpu.make_async_copy(valid_hbm.at[at], valid_ref.at[at], sems.at[1, r]),
                pltpu.make_async_copy(image_hbm.at[at], image_ref.at[at], sems.at[2, r]),
            ]
        )
    for group in copies:
        for copy in group:
            copy.start()
    recv = recv_ref[...]
    rows = iota((CELLS, 128), 0)
    for r in range(4):
        at = pl.ds(128 * r, 128)
        chosen = jnp.where(rows == pos_ref[pl.ds(r, 1), :], 1.0, 0.0).astype(BF16)
        picked = dot(chosen, recv, TN)
        planes_ref[0, at, :] = picked
        source_ref[at, :] = picked.astype(BF16)
    inner = shift_table(256, False)
    outer = shift_table(128, True)
    for j in range(CHUNKS):
        if j + 1 < CHUNKS:
            shifted = dot(source_ref[:, pl.ds(128 * j, 256)], inner, (((1,), (0,)), ((), ())))
        else:
            shifted = dot(source_ref[:, columns(j)], outer, (((1,), (0,)), ((), ())))
        for tap in range(7):
            planes_ref[tap + 1, :, columns(j)] = shifted[:, 128 * tap : 128 * tap + 128]
    low = iota((ROWS, 128), 1) < 64

    def block(i, carry):
        squares, counted = carry
        at = pl.ds(pl.multiple_of(i * ROWS, ROWS), ROWS)
        warped = []
        for j in range(CHUNKS):
            terms = [
                taps_ref[tap, at, columns(j)].astype(F32) * planes_ref[tap, at, columns(j)]
                for tap in range(8)
            ]
            warped.append(
                ((terms[0] + terms[1]) + (terms[2] + terms[3]))
                + ((terms[4] + terms[5]) + (terms[6] + terms[7]))
            )
        swapped = [pltpu.roll(c, 64, 1) for c in warped]
        for j in range(CHUNKS):
            field = warped[j]
            mask = valid_ref[at, columns(j)].astype(F32)
            mask_ref[at, columns(j)] = mask
            front = jnp.where(low, swapped[j], swapped[j + 1] if j + 1 < CHUNKS else field)
            back = jnp.where(low, swapped[j - 1] if j else field, swapped[j])
            grad_ref[0, at, columns(j)] = (0.5 * mask) * (front - back)
            coarse = field.astype(BF16)
            split_ref[at, pl.ds(256 * j, 128)] = coarse
            split_ref[at, pl.ds(256 * j + 128, 128)] = (field - coarse.astype(F32)).astype(BF16)
            misfit = mask * (field - image_ref[at, columns(j)].astype(F32))
            misfit_ref[at, columns(j)] = misfit
            squares = squares + misfit * misfit
            counted = counted + mask
        return squares, counted

    zero = jnp.zeros((ROWS, 128), F32)
    carry = (zero, zero)
    for r in range(4):
        for copy in copies[r]:
            copy.wait()
        carry = lax.fori_loop(128 * r // ROWS, 128 * (r + 1) // ROWS, block, carry)
    sums_ref[...] = spread_sums(list(carry))
    table = slope_table()
    for j in range(CHUNKS):
        slopes = dot(split_ref[:, pl.ds(256 * j, 256)], table, (((1,), (0,)), ((), ())))
        mask = mask_ref[:, columns(j)]
        grad_ref[1, :, columns(j)] = mask * slopes[:, :128]
        grad_ref[2, :, columns(j)] = mask * slopes[:, 128:]


def high_z(j, shape):
    vz = 2 * j + (iota(shape, 1) >> 6)
    return (vz.astype(F32) + 0.5) * 0.125


def plane_basis(corner, lane):
    vy = (((lane >> 3) & 7).astype(F32) + 0.5) * 0.125
    vx = ((lane & 7).astype(F32) + 0.5) * 0.125
    along_y = (corner & 2) == 2
    along_x = (corner & 1) == 1
    return jnp.where(along_y, vy, 1.0 - vy) * jnp.where(along_x, vx, 1.0 - vx)


def force_nodes(misfit_at, inverse, grad_ref, near_ref, mid_ref, far_ref, parts_ref):
    high = [high_z(j, (1, 128)) for j in range(CHUNKS)]

    def block(i, carry):
        at = pl.ds(pl.multiple_of(i * ROWS, ROWS), ROWS)
        pull = []
        for j in range(CHUNKS):
            misfit = misfit_at(at, j)
            pull.append(misfit / (1.0 + misfit * misfit * inverse))
        for k in range(3):
            force = [pull[j] * grad_ref[k, at, columns(j)] for j in range(CHUNKS)]
            total = (force[0] + force[1]) + (force[2] + force[3])
            upper = (force[0] * high[0] + force[1] * high[1]) + (
                force[2] * high[2] + force[3] * high[3]
            )
            for a, value in enumerate((total - upper, upper)):
                coarse = value.astype(BF16)
                parts_ref[2 * k + a, at, pl.ds(0, 128)] = coarse
                parts_ref[2 * k + a, at, pl.ds(128, 128)] = (value - coarse.astype(F32)).astype(BF16)
        return carry

    lax.fori_loop(0, BLOCKS, block, 0)
    corner = iota((16, 256), 0)
    basis = jnp.where(corner < 4, plane_basis(corner, iota((16, 256), 1)), 0.0).astype(BF16)
    first = iota((16, 128), 1) == 0
    nodes = {}
    for k in range(3):
        for a in range(2):
            parts = dot(basis, parts_ref[2 * k + a], NT)
            for r in range(4):
                own = parts[:, 128 * r : 128 * r + 128]
                moved = jnp.where(first, 0.0, pltpu.roll(own, 1, 1))
                for b in range(2):
                    value = own[2 * b : 2 * b + 1] + moved[2 * b + 1 : 2 * b + 2]
                    key = (r % 2 + b, (r // 2 + a) * 3 + k)
                    nodes[key] = nodes[key] + value if key in nodes else value
    upward = is_even("grp")
    for row in range(9):
        near, far = nodes[(0, row)], nodes[(2, row)]
        near_ref[pl.ds(row, 1), :] = jnp.where(upward, far, near)
        mid_ref[pl.ds(row, 1), :] = nodes[(1, row)]
        far_ref[pl.ds(row, 1), :] = jnp.where(upward, near, far)


def first_force_body(sums_ref, misfit_ref, grad_ref, near_ref, mid_ref, far_ref, parts_ref):
    square_sum, counted = gathered_sums(sums_ref, 2)
    inverse = 1.0 / (square_sum / counted + 1e-06)
    force_nodes(
        lambda at, j: misfit_ref[at, columns(j)],
        inverse,
        grad_ref,
        near_ref,
        mid_ref,
        far_ref,
        parts_ref,
    )


def second_spread(sums_ref, steps_ref):
    square_sum, counted = gathered_sums(sums_ref, 2)
    steep, curve, cross, moved_sum = gathered_sums(steps_ref, 4)
    step = steep / curve
    updated = jnp.maximum(square_sum + step * (2.0 * cross + step * moved_sum), 0.0)
    return step, 1.0 / (updated / counted + 1e-06)


def second_force_body(
    sums_ref, steps_ref, misfit_ref, change_ref, grad_ref, near_ref, mid_ref, far_ref, out_ref, parts_ref
):
    step, inverse = second_spread(sums_ref, steps_ref)

    def misfit_at(at, j):
        misfit = misfit_ref[at, columns(j)] + step * change_ref[at, columns(j)]
        out_ref[at, columns(j)] = misfit
        return misfit

    force_nodes(misfit_at, inverse, grad_ref, near_ref, mid_ref, far_ref, parts_ref)


def is_even(axis):
    return lax.axis_index(axis) % 2 == 0


def band_sums(pair_ref, mid_ref, cross_ref, from_pair_ref, from_cross_ref):
    band = lax.axis_index("grp")
    last = lax.axis_size("grp") - 1
    upward = is_even("grp")
    pair, cross = pair_ref[...], cross_ref[...]
    from_pair, from_cross = from_pair_ref[...], from_cross_ref[...]
    below = jnp.where(upward, from_cross, from_pair)
    above = jnp.where(upward, from_pair, from_cross)
    near = jnp.where(upward, cross, pair) + jnp.where(band > 0, below, 0.0)
    far = jnp.where(band < last, jnp.where(upward, pair, cross) + above, 0.0)
    return near, mid_ref[...], far


def edge_body(near_ref, mid_ref, far_ref, below_ref, above_ref, pair_ref, cross_ref):
    upward = is_even("slab")
    for y, part in enumerate(band_sums(near_ref, mid_ref, far_ref, below_ref, above_ref)):
        pair_ref[pl.ds(3 * y, 3), :] = jnp.where(upward, part[6:9], part[0:3])
        cross_ref[pl.ds(3 * y, 3), :] = jnp.where(upward, part[0:3], part[6:9])


def move_body(
    near_ref, mid_ref, far_ref, below_ref, above_ref, under_ref, over_ref,
    sums_ref, steps_ref, misfit_ref, grad_ref, change_ref, out_ref, dir_ref, fields_ref, second,
):
    slab = lax.axis_index("slab")
    last = lax.axis_size("slab") - 1
    bands = band_sums(near_ref, mid_ref, far_ref, below_ref, above_ref)
    upward = is_even("slab")
    steep = jnp.zeros((1, 128), F32)
    nodes = {}
    for y in range(3):
        from_pair, from_cross = under_ref[pl.ds(3 * y, 3), :], over_ref[pl.ds(3 * y, 3), :]
        under = jnp.where(slab > 0, jnp.where(upward, from_cross, from_pair), 0.0)
        over = jnp.where(upward, from_pair, from_cross)
        layers = (
            bands[y][0:3] + under,
            bands[y][3:6],
            jnp.where(slab < last, bands[y][6:9] + over, 0.0),
        )
        for z, layer in enumerate(layers):
            direction = -layer
            if z < 2 and y < 2:
                for k in range(3):
                    dir_ref[k, z, pl.ds(y, 1), :] = direction[k : k + 1]
                steep = steep + jnp.sum(direction * direction, axis=0, keepdims=True)
            nodes[(z, y)] = jnp.concatenate([direction[k : k + 1] for k in range(3)], axis=1)
    end = (iota((1, 384), 1) & 127) == 127
    shifted = {key: jnp.where(end, 0.0, pltpu.roll(value, 383, 1)) for key, value in nodes.items()}
    rank = iota((24, 256), 0)
    lane = iota((24, 256), 1)
    basis = jnp.where(((rank >> 2) & 1) == (lane >> 7), plane_basis(rank & 3, lane), 0.0).astype(BF16)
    for r in range(4):
        rows = []
        for corner in range(8):
            key = (r // 2 + corner // 4, r % 2 + corner // 2 % 2)
            rows.append(shifted[key] if corner % 2 else nodes[key])
        full = jnp.concatenate(rows, axis=0)
        coarse = full.astype(BF16).astype(F32)
        rest = full - coarse
        middle = rest.astype(BF16).astype(F32)
        split = jnp.concatenate([coarse, middle, rest - middle], axis=0)
        fields_ref[r] = dot(split.astype(BF16), basis, TN)
    if second:
        _, inverse = second_spread(sums_ref, steps_ref)
    else:
        square_sum, counted = gathered_sums(sums_ref, 2)
        inverse = 1.0 / (square_sum / counted + 1e-06)
    high = [high_z(j, (1, 128)) for j in range(CHUNKS)]

    def block(i, carry):
        curve, cross, moved_sum = carry
        at = pl.ds(pl.multiple_of(i * ROWS, ROWS), ROWS)
        r = i // (128 // ROWS)
        x = (i % (128 // ROWS)) * ROWS
        change = [None] * CHUNKS
        for k in range(3):
            cells = pl.ds(pl.multiple_of(128 * k + x, ROWS), ROWS)
            lower = fields_ref[r, cells, pl.ds(0, 128)]
            slope = fields_ref[r, cells, pl.ds(128, 128)] - lower
            for j in range(CHUNKS):
                term = grad_ref[k, at, columns(j)] * (lower + high[j] * slope)
                change[j] = term if k == 0 else change[j] + term
        for j in range(CHUNKS):
            misfit = misfit_ref[at, columns(j)]
            change_ref[at, columns(j)] = change[j]
            square = change[j] * change[j]
            curve = curve + square / (1.0 + misfit * misfit * inverse)
            if not second:
                cross = cross + misfit * change[j]
                moved_sum = moved_sum + square
        return curve, cross, moved_sum

    zero = jnp.zeros((ROWS, 128), F32)
    curve, cross, moved_sum = lax.fori_loop(0, BLOCKS, block, (zero, zero, zero))
    out_ref[...] = spread_sums([steep, curve] + ([] if second else [cross, moved_sum]))


def first_move_body(
    near_ref, mid_ref, far_ref, below_ref, above_ref, under_ref, over_ref,
    sums_ref, misfit_ref, grad_ref, change_ref, out_ref, dir_ref, fields_ref,
):
    move_body(
        near_ref, mid_ref, far_ref, below_ref, above_ref, under_ref, over_ref,
        sums_ref, None, misfit_ref, grad_ref, change_ref, out_ref, dir_ref, fields_ref, False,
    )


def second_move_body(
    near_ref, mid_ref, far_ref, below_ref, above_ref, under_ref, over_ref,
    sums_ref, steps_ref, misfit_ref, grad_ref, change_ref, out_ref, dir_ref, fields_ref,
):
    move_body(
        near_ref, mid_ref, far_ref, below_ref, above_ref, under_ref, over_ref,
        sums_ref, steps_ref, misfit_ref, grad_ref, change_ref, out_ref, dir_ref, fields_ref, True,
    )


def finish_body(first_ref, second_ref, dir0_ref, dir1_ref, misfit_ref, change_ref, coef_ref, out_ref):
    steep, curve = gathered_sums(first_ref, 2)
    step0 = steep / curve
    steep, curve = gathered_sums(second_ref, 2)
    step1 = steep / curve
    coef_ref[...] = step0.reshape(1, 1, 1, 1) * dir0_ref[...] + step1.reshape(1, 1, 1, 1) * dir1_ref[...]
    out_ref[...] = misfit_ref[...] + step1 * change_ref[...]


def swap(block, axis, offset):
    size = lax.axis_size(axis)
    route = []
    for i in range(offset, size + offset, 2):
        route += [(i % size, (i + 1) % size), ((i + 1) % size, i % size)]
    return lax.ppermute(block, axis, route)


def to_all(sums):
    return lax.all_to_all(sums, EVERY, 0, 0, tiled=True)


def halo(near, mid, far):
    below = swap(near, "grp", 0)
    above = swap(far, "grp", 1)
    pair, cross = call(edge_body, [((9, 128), F32)] * 2, (near, mid, far, below, above), "edges")
    under = swap(pair, "slab", 0)
    over = swap(cross, "slab", 1)
    return below, above, under, over


def shards(reference_bricks, deformed, tap_weights, valid_voxels, sources):
    big = ((CELLS, 512), F32)
    sums_shape = ((128, 128), F32)
    nodes_shape = [((9, 128), F32)] * 3
    dir_shape = ((3, 2, 2, 128), F32)
    grad_shape = ((3, CELLS, 512), F32)
    parts = [pltpu.VMEM((6, CELLS, 256), BF16)]
    fields = [pltpu.VMEM((4, 384, 256), F32)]
    taps = tap_weights.reshape(8, CELLS, 512)
    image = deformed.reshape(CELLS, 512)
    valid = valid_voxels.reshape(CELLS, 512)

    pos, want, bricks = call(
        wanted_body,
        [((4, 128), I32), ((16, 128), I32), ((CELLS, 512), BF16)],
        (sources, reference_bricks.reshape(CELLS, 512)),
        "wanted",
        [pltpu.VMEM((2, 2, 128), I32), pltpu.SemaphoreType.DMA((2,))],
        far=(0, 1),
    )
    asked = lax.all_to_all(want, "slab", 0, 0, tiled=True)
    (sent,) = call(pick_body, [((CELLS, 512), BF16)], (asked, bricks), "pick")
    recv = lax.all_to_all(sent, "slab", 0, 0, tiled=True)
    grads, misfit, sums = call(
        warp_body,
        [grad_shape, big, sums_shape],
        (pos, recv, image, taps, valid),
        "warp",
        [
            pltpu.VMEM((CELLS, 512), BF16),
            pltpu.VMEM((8, CELLS, 512), F32),
            pltpu.VMEM((CELLS, 1024), BF16),
            pltpu.VMEM((CELLS, 512), F32),
            pltpu.VMEM((CELLS, 512), BF16),
            pltpu.VMEM((8, CELLS, 512), BF16),
            pltpu.VMEM((CELLS, 512), I32),
            pltpu.SemaphoreType.DMA((3, 4)),
        ],
        40,
        (2, 3, 4),
    )
    sums = to_all(sums)
    near, mid, far = call(first_force_body, nodes_shape, (sums, misfit, grads), "force_first", parts)
    below, above, under, over = halo(near, mid, far)
    change, steps, dir0 = call(
        first_move_body,
        [big, sums_shape, dir_shape],
        (near, mid, far, below, above, under, over, sums, misfit, grads),
        "move_first",
        fields,
    )
    first = to_all(steps)
    near, mid, far, misfit = call(
        second_force_body,
        nodes_shape + [big],
        (sums, first, misfit, change, grads),
        "force_second",
        parts,
    )
    below, above, under, over = halo(near, mid, far)
    change, steps, dir1 = call(
        second_move_body,
        [big, sums_shape, dir_shape],
        (near, mid, far, below, above, under, over, sums, first, misfit, grads),
        "move_second",
        fields,
    )
    second = to_all(steps)
    coefficients, residual = call(
        finish_body, [dir_shape, big], (first, second, dir0, dir1, misfit, change), "finish"
    )
    return (coefficients, residual.reshape(2, 2, 128, 512))


def solution(mesh):
    in_specs = (
        P("grp", "slab", None),
        P("slab", "grp", None, None),
        P(None, "slab", "grp", None, None),
        P("slab", "grp", None, None),
        P("slab", "grp", None),
    )
    out_specs = (P(None, "slab", "grp", None), P("slab", "grp", None, None))
    return jax.shard_map(shards, mesh=mesh, in_specs=in_specs, out_specs=out_specs, check_vma=False)
```

```python
import jax
import jax.numpy as jnp
from jax import lax
from jax.experimental import pallas as pl
from jax.experimental.pallas import tpu as pltpu
from jax.sharding import PartitionSpec as P

F32 = jnp.float32
BF16 = jnp.bfloat16
I32 = jnp.int32
EVERY = ("slab", "grp")
CELLS = 512
ROWS = 16
BLOCKS = CELLS // ROWS
CHUNKS = 4
NN = (((1,), (0,)), ((), ()))
NT = (((1,), (1,)), ((), ()))
TN = (((0,), (0,)), ((), ()))
VMEM = pl.BlockSpec(memory_space=pltpu.VMEM)
HBM = pl.BlockSpec(memory_space=pltpu.HBM)


def iota(shape, axis):
    return lax.broadcasted_iota(I32, shape, axis)


def dot(a, b, dims):
    return lax.dot_general(a, b, dims, preferred_element_type=F32)


def call(body, outs, ins, name, scratch=(), limit=16, far=(), stored=False):
    return pl.pallas_call(
        body,
        out_shape=[jax.ShapeDtypeStruct(s, d) for s, d in outs],
        in_specs=[HBM if n in far else VMEM for n in range(len(ins))],
        out_specs=[HBM if stored else VMEM] * len(outs),
        scratch_shapes=list(scratch),
        compiler_params=pltpu.CompilerParams(vmem_limit_bytes=limit << 20),
        name=name,
    )(*[pltpu.with_memory_space_constraint(x, pltpu.HBM) if n in far else x for n, x in enumerate(ins)])


def wanted_body(
    src_hbm, bricks_hbm, pos_ref, want_ref, bricks_ref, level_ref, inner_ref, outer_ref, slope_ref,
    src_ref, sems,
):
    first = pltpu.make_async_copy(src_hbm, src_ref, sems.at[0])
    fetches = []
    for r in range(4):
        at = pl.ds(128 * r, 128)
        fetches.append(pltpu.make_async_copy(bricks_hbm.at[at], bricks_ref.at[at], sems.at[r + 1]))
    first.start()
    for fetch in fetches:
        fetch.start()
    place = 32 * (lax.axis_index("slab") % 4)
    earlier = (iota((128, 128), 0) < iota((128, 128), 1)).astype(F32).astype(BF16)
    owners = iota((16, 128), 0)
    lanes = iota((128, 128), 0)
    before = jnp.zeros((16, 1), F32)
    want = jnp.zeros((32, 128), F32)
    level_ref[...] = level_table()
    inner_ref[...] = rise_table(256)
    outer_ref[...] = rise_table(128)
    slope_ref[...] = slope_table()
    first.wait()
    for r in range(4):
        src = src_ref[r // 2, pl.ds(r % 2, 1), :]
        owner = src >> 9
        row = src & 511
        mine = jnp.where(owners == owner, 1.0, 0.0)
        count = dot(mine.astype(BF16), earlier, NN) + before
        before = before + jnp.sum(mine, axis=1, keepdims=True)
        rank = jnp.sum(mine * count, axis=0, keepdims=True).astype(I32)
        pos = (owner * 32 + rank).astype(F32)
        pos_ref[pl.ds(128 * r, 128), :] = jnp.transpose(jnp.broadcast_to(pos, (128, 128)))
        slot = jnp.where(lanes == rank + place, 1.0, 0.0).astype(BF16)
        low = (row & 255).astype(F32)
        high = (row >> 8).astype(F32)
        parts = jnp.concatenate([mine * low, mine * high], axis=0).astype(BF16)
        want = want + dot(parts, slot, NT)
    want_ref[...] = (want[:16] + 256.0 * want[16:]).astype(I32)
    for fetch in fetches:
        fetch.wait()


def pick_body(want_ref, bricks_ref, out_ref):
    bricks = bricks_ref[...]
    rows = iota((CELLS, 128), 0)
    for r in range(4):
        index = jnp.sum(want_ref[pl.ds(4 * r, 4), :], axis=0, keepdims=True)
        chosen = jnp.where(rows == index, 1.0, 0.0).astype(BF16)
        out_ref[pl.ds(128 * r, 128), :] = dot(chosen, bricks, TN).astype(BF16)


def columns(j):
    return pl.ds(128 * j, 128)


def spread_sums(values):
    lane = iota((128, 128), 1)
    out = jnp.zeros((128, 128), F32)
    for n, value in enumerate(values):
        total = jnp.sum(jnp.sum(value, axis=0, keepdims=True), axis=1, keepdims=True)
        out = jnp.where(lane == n, total, out)
    return out


def gathered_sums(ref, count):
    sums = jnp.sum(ref[...], axis=0, keepdims=True)
    lane = iota((1, 128), 1)
    return [
        jnp.sum(jnp.where(lane == n, sums, 0.0), axis=1, keepdims=True) for n in range(count)
    ]


def plane_step(tap, lane):
    step_x = jnp.where(((tap & 1) == 1) & ((lane & 7) < 7), 1, 0)
    step_y = jnp.where(((tap & 2) == 2) & ((lane & 56) < 56), 8, 0)
    return lane + step_x + step_y


def shift_table(shape, target):
    return jnp.where(iota(shape, 0) == target, 1.0, 0.0).astype(BF16)


def level_table():
    at = iota((1, 384), 1)
    return shift_table((128, 384), plane_step((at >> 7) + 1, at & 127))


def rise_table(width):
    at = iota((1, 512), 1)
    lane = at & 127
    rise = jnp.where(lane < 64, 64, 64 if width == 256 else 0)
    return shift_table((width, 512), plane_step(at >> 7, lane) + rise)


def slope_table():
    at = iota((1, 256), 1)
    lane = at & 127
    along_x = at >= 128
    place = jnp.where(along_x, lane & 7, (lane >> 3) & 7)
    stride = jnp.where(along_x, 1, 8)
    front = lane + jnp.where(place < 7, stride, 0)
    back = lane - jnp.where(place > 0, stride, 0)
    row = iota((256, 256), 0) & 127
    return (jnp.where(row == front, 0.5, 0.0) - jnp.where(row == back, 0.5, 0.0)).astype(BF16)


def warp_body(
    pos_ref, recv_ref, level_ref, inner_ref, outer_ref, slope_ref, image_hbm, taps_hbm, valid_hbm,
    grad_ref, misfit_ref, sums_ref,
    planes_ref, split_ref, mask_ref, image_ref, taps_ref, valid_ref, sems,
):
    copies = []
    for r in range(4):
        at = pl.ds(128 * r, 128)
        copies.append(
            [
                pltpu.make_async_copy(taps_hbm.at[:, at], taps_ref.at[:, at], sems.at[0, r]),
                pltpu.make_async_copy(valid_hbm.at[at], valid_ref.at[at], sems.at[1, r]),
                pltpu.make_async_copy(image_hbm.at[at], image_ref.at[at], sems.at[2, r]),
            ]
        )
    for group in copies:
        for copy in group:
            copy.start()
    lane = iota((128, 128), 1).astype(F32)
    low = iota((ROWS, 128), 1) < 64
    table = slope_ref[...]

    def planes(r):
        at = pl.ds(128 * r, 128)
        pos = pos_ref[at, :]
        chosen = jnp.concatenate(
            [jnp.where(pos == lane + 128.0 * q, 1.0, 0.0).astype(BF16) for q in range(4)], axis=1
        )
        picked = dot(chosen, recv_ref[...], NN)
        planes_ref[0, at, :] = picked
        source = picked.astype(BF16)
        parts = [source[:, 128 * j : 128 * j + 128] for j in range(CHUNKS)]
        shifted = dot(jnp.concatenate(parts, axis=0), level_ref[...], NN)
        for j in range(CHUNKS):
            for tap in range(3):
                planes_ref[tap + 1, at, columns(j)] = shifted[
                    128 * j : 128 * (j + 1), 128 * tap : 128 * tap + 128
                ]
        pairs = jnp.concatenate([source[:, 128 * j : 128 * j + 256] for j in range(3)], axis=0)
        raised = dot(pairs, inner_ref[...], NN)
        for j in range(CHUNKS):
            found = dot(parts[3], outer_ref[...], NN) if j == 3 else raised[128 * j : 128 * (j + 1)]
            for tap in range(4):
                planes_ref[tap + 4, at, columns(j)] = found[:, 128 * tap : 128 * tap + 128]

    def block(at, squares, counted):
        warped = []
        for j in range(CHUNKS):
            terms = [
                taps_ref[tap, at, columns(j)].astype(F32) * planes_ref[tap, at, columns(j)]
                for tap in range(8)
            ]
            warped.append(
                ((terms[0] + terms[1]) + (terms[2] + terms[3]))
                + ((terms[4] + terms[5]) + (terms[6] + terms[7]))
            )
        swapped = [pltpu.roll(c, 64, 1) for c in warped]
        for j in range(CHUNKS):
            field = warped[j]
            mask = valid_ref[at, columns(j)].astype(F32)
            mask_ref[at, columns(j)] = mask
            front = jnp.where(low, swapped[j], swapped[j + 1] if j + 1 < CHUNKS else field)
            back = jnp.where(low, swapped[j - 1] if j else field, swapped[j])
            grad_ref[0, at, columns(j)] = (0.5 * mask) * (front - back)
            coarse = field.astype(BF16)
            split_ref[at, pl.ds(256 * j, 128)] = coarse
            split_ref[at, pl.ds(256 * j + 128, 128)] = (field - coarse.astype(F32)).astype(BF16)
            misfit = mask * (field - image_ref[at, columns(j)].astype(F32))
            misfit_ref[at, columns(j)] = misfit
            squares = squares + misfit * misfit
            counted = counted + mask
        return squares, counted

    def slopes(r):
        at = pl.ds(128 * r, 128)
        for j in range(CHUNKS):
            both = dot(split_ref[at, pl.ds(256 * j, 256)], table, NN)
            mask = mask_ref[at, columns(j)]
            grad_ref[1, at, columns(j)] = mask * both[:, :128]
            grad_ref[2, at, columns(j)] = mask * both[:, 128:]

    squares = counted = jnp.zeros((ROWS, 128), F32)
    for r in range(3):
        planes(r)
    for r in range(4):
        for copy in copies[r]:
            copy.wait()
        if r + 3 < 4:
            planes(r + 3)
        for i in range(128 // ROWS):
            squares, counted = block(pl.ds(128 * r + ROWS * i, ROWS), squares, counted)
        if r > 0:
            slopes(r - 1)
    slopes(3)
    sums_ref[...] = spread_sums([squares, counted])


def high_z(j, shape):
    vz = 2 * j + (iota(shape, 1) >> 6)
    return (vz.astype(F32) + 0.5) * 0.125


def plane_basis(corner, lane):
    vy = (((lane >> 3) & 7).astype(F32) + 0.5) * 0.125
    vx = ((lane & 7).astype(F32) + 0.5) * 0.125
    along_y = (corner & 2) == 2
    along_x = (corner & 1) == 1
    return jnp.where(along_y, vy, 1.0 - vy) * jnp.where(along_x, vx, 1.0 - vx)


def force_nodes(misfit_at, inverse, grad_ref, near_ref, mid_ref, far_ref, parts_ref):
    high = [high_z(j, (1, 128)) for j in range(CHUNKS)]

    def block(i, carry):
        at = pl.ds(pl.multiple_of(i * ROWS, ROWS), ROWS)
        pull = []
        for j in range(CHUNKS):
            misfit = misfit_at(at, j)
            pull.append(misfit / (1.0 + misfit * misfit * inverse))
        for k in range(3):
            force = [pull[j] * grad_ref[k, at, columns(j)] for j in range(CHUNKS)]
            total = (force[0] + force[1]) + (force[2] + force[3])
            upper = (force[0] * high[0] + force[1] * high[1]) + (
                force[2] * high[2] + force[3] * high[3]
            )
            for a, value in enumerate((total - upper, upper)):
                coarse = value.astype(BF16)
                parts_ref[2 * k + a, at, pl.ds(0, 128)] = coarse
                parts_ref[2 * k + a, at, pl.ds(128, 128)] = (value - coarse.astype(F32)).astype(BF16)
        return carry

    lax.fori_loop(0, BLOCKS, block, 0, unroll=4)
    corner = iota((16, 256), 0)
    basis = jnp.where(corner < 4, plane_basis(corner, iota((16, 256), 1)), 0.0).astype(BF16)
    first = iota((16, 128), 1) == 0
    nodes = {}
    for k in range(3):
        for a in range(2):
            parts = dot(basis, parts_ref[2 * k + a], NT)
            for r in range(4):
                own = parts[:, 128 * r : 128 * r + 128]
                moved = jnp.where(first, 0.0, pltpu.roll(own, 1, 1))
                for b in range(2):
                    value = own[2 * b : 2 * b + 1] + moved[2 * b + 1 : 2 * b + 2]
                    key = (r % 2 + b, (r // 2 + a) * 3 + k)
                    nodes[key] = nodes[key] + value if key in nodes else value
    upward = is_even("grp")
    for row in range(9):
        near, far = nodes[(0, row)], nodes[(2, row)]
        near_ref[pl.ds(row, 1), :] = jnp.where(upward, far, near)
        mid_ref[pl.ds(row, 1), :] = nodes[(1, row)]
        far_ref[pl.ds(row, 1), :] = jnp.where(upward, near, far)


def first_force_body(sums_ref, misfit_ref, grad_ref, near_ref, mid_ref, far_ref, parts_ref):
    square_sum, counted = gathered_sums(sums_ref, 2)
    inverse = 1.0 / (square_sum / counted + 1e-06)
    force_nodes(
        lambda at, j: misfit_ref[at, columns(j)],
        inverse,
        grad_ref,
        near_ref,
        mid_ref,
        far_ref,
        parts_ref,
    )


def second_spread(sums_ref, steps_ref):
    square_sum, counted = gathered_sums(sums_ref, 2)
    steep, curve, cross, moved_sum = gathered_sums(steps_ref, 4)
    step = steep / curve
    updated = jnp.maximum(square_sum + step * (2.0 * cross + step * moved_sum), 0.0)
    return step, 1.0 / (updated / counted + 1e-06)


def second_force_body(
    sums_ref, steps_ref, misfit_ref, change_ref, grad_ref, near_ref, mid_ref, far_ref, out_ref, parts_ref
):
    step, inverse = second_spread(sums_ref, steps_ref)

    def misfit_at(at, j):
        misfit = misfit_ref[at, columns(j)] + step * change_ref[at, columns(j)]
        out_ref[at, columns(j)] = misfit
        return misfit

    force_nodes(misfit_at, inverse, grad_ref, near_ref, mid_ref, far_ref, parts_ref)


def is_even(axis):
    return lax.axis_index(axis) % 2 == 0


def band_sums(pair_ref, mid_ref, cross_ref, from_pair_ref, from_cross_ref):
    band = lax.axis_index("grp")
    last = lax.axis_size("grp") - 1
    upward = is_even("grp")
    pair, cross = pair_ref[...], cross_ref[...]
    from_pair, from_cross = from_pair_ref[...], from_cross_ref[...]
    below = jnp.where(upward, from_cross, from_pair)
    above = jnp.where(upward, from_pair, from_cross)
    near = jnp.where(upward, cross, pair) + jnp.where(band > 0, below, 0.0)
    far = jnp.where(band < last, jnp.where(upward, pair, cross) + above, 0.0)
    return near, mid_ref[...], far


def edge_body(near_ref, mid_ref, far_ref, below_ref, above_ref, pair_ref, cross_ref):
    upward = is_even("slab")
    for y, part in enumerate(band_sums(near_ref, mid_ref, far_ref, below_ref, above_ref)):
        pair_ref[pl.ds(3 * y, 3), :] = jnp.where(upward, part[6:9], part[0:3])
        cross_ref[pl.ds(3 * y, 3), :] = jnp.where(upward, part[0:3], part[6:9])


def move_body(
    near_ref, mid_ref, far_ref, below_ref, above_ref, under_ref, over_ref,
    sums_ref, steps_ref, misfit_ref, grad_ref, change_ref, out_ref, dir_ref, fields_ref, second,
):
    slab = lax.axis_index("slab")
    last = lax.axis_size("slab") - 1
    bands = band_sums(near_ref, mid_ref, far_ref, below_ref, above_ref)
    upward = is_even("slab")
    steep = jnp.zeros((1, 128), F32)
    nodes = {}
    for y in range(3):
        from_pair, from_cross = under_ref[pl.ds(3 * y, 3), :], over_ref[pl.ds(3 * y, 3), :]
        under = jnp.where(slab > 0, jnp.where(upward, from_cross, from_pair), 0.0)
        over = jnp.where(upward, from_pair, from_cross)
        layers = (
            bands[y][0:3] + under,
            bands[y][3:6],
            jnp.where(slab < last, bands[y][6:9] + over, 0.0),
        )
        for z, layer in enumerate(layers):
            direction = -layer
            if z < 2 and y < 2:
                for k in range(3):
                    dir_ref[k, z, pl.ds(y, 1), :] = direction[k : k + 1]
                steep = steep + jnp.sum(direction * direction, axis=0, keepdims=True)
            nodes[(z, y)] = jnp.concatenate([direction[k : k + 1] for k in range(3)], axis=1)
    end = (iota((1, 384), 1) & 127) == 127
    shifted = {key: jnp.where(end, 0.0, pltpu.roll(value, 383, 1)) for key, value in nodes.items()}
    rank = iota((24, 256), 0)
    lane = iota((24, 256), 1)
    basis = jnp.where(((rank >> 2) & 1) == (lane >> 7), plane_basis(rank & 3, lane), 0.0).astype(BF16)
    for r in range(4):
        rows = []
        for corner in range(8):
            key = (r // 2 + corner // 4, r % 2 + corner // 2 % 2)
            rows.append(shifted[key] if corner % 2 else nodes[key])
        full = jnp.concatenate(rows, axis=0)
        coarse = full.astype(BF16).astype(F32)
        rest = full - coarse
        middle = rest.astype(BF16).astype(F32)
        split = jnp.concatenate([coarse, middle, rest - middle], axis=0)
        fields_ref[r] = dot(split.astype(BF16), basis, TN)
    if second:
        _, inverse = second_spread(sums_ref, steps_ref)
    else:
        square_sum, counted = gathered_sums(sums_ref, 2)
        inverse = 1.0 / (square_sum / counted + 1e-06)
    high = [high_z(j, (1, 128)) for j in range(CHUNKS)]

    def block(i, carry):
        curve, cross, moved_sum = carry
        at = pl.ds(pl.multiple_of(i * ROWS, ROWS), ROWS)
        r = i // (128 // ROWS)
        x = (i % (128 // ROWS)) * ROWS
        change = [None] * CHUNKS
        for k in range(3):
            cells = pl.ds(pl.multiple_of(128 * k + x, ROWS), ROWS)
            lower = fields_ref[r, cells, pl.ds(0, 128)]
            slope = fields_ref[r, cells, pl.ds(128, 128)] - lower
            for j in range(CHUNKS):
                term = grad_ref[k, at, columns(j)] * (lower + high[j] * slope)
                change[j] = term if k == 0 else change[j] + term
        for j in range(CHUNKS):
            misfit = misfit_ref[at, columns(j)]
            change_ref[at, columns(j)] = change[j]
            square = change[j] * change[j]
            curve = curve + square / (1.0 + misfit * misfit * inverse)
            if not second:
                cross = cross + misfit * change[j]
                moved_sum = moved_sum + square
        return curve, cross, moved_sum

    zero = jnp.zeros((ROWS, 128), F32)
    curve, cross, moved_sum = lax.fori_loop(0, BLOCKS, block, (zero, zero, zero), unroll=4)
    out_ref[...] = spread_sums([steep, curve] + ([] if second else [cross, moved_sum]))


def first_move_body(
    near_ref, mid_ref, far_ref, below_ref, above_ref, under_ref, over_ref,
    sums_ref, misfit_ref, grad_ref, change_ref, out_ref, dir_ref, fields_ref,
):
    move_body(
        near_ref, mid_ref, far_ref, below_ref, above_ref, under_ref, over_ref,
        sums_ref, None, misfit_ref, grad_ref, change_ref, out_ref, dir_ref, fields_ref, False,
    )


def second_move_body(
    near_ref, mid_ref, far_ref, below_ref, above_ref, under_ref, over_ref,
    sums_ref, steps_ref, misfit_ref, grad_ref, change_ref, out_ref, dir_ref, fields_ref,
):
    move_body(
        near_ref, mid_ref, far_ref, below_ref, above_ref, under_ref, over_ref,
        sums_ref, steps_ref, misfit_ref, grad_ref, change_ref, out_ref, dir_ref, fields_ref, True,
    )


def finish_body(
    first_ref, second_ref, dir0_ref, dir1_ref, misfit_ref, change_ref, coef_hbm, out_hbm,
    coef_ref, out_ref, sems,
):
    steep, curve = gathered_sums(first_ref, 2)
    step0 = steep / curve
    steep, curve = gathered_sums(second_ref, 2)
    step1 = steep / curve
    coef_ref[...] = step0.reshape(1, 1, 1, 1) * dir0_ref[...] + step1.reshape(1, 1, 1, 1) * dir1_ref[...]
    copies = [pltpu.make_async_copy(coef_ref, coef_hbm, sems.at[4])]
    copies[0].start()
    for r in range(4):
        at = pl.ds(128 * r, 128)
        out_ref[at, :] = misfit_ref[at, :] + step1 * change_ref[at, :]
        copies.append(pltpu.make_async_copy(out_ref.at[at], out_hbm.at[at], sems.at[r]))
        copies[-1].start()
    for copy in copies:
        copy.wait()


def swap(block, axis, offset):
    size = lax.axis_size(axis)
    route = []
    for i in range(offset, size + offset, 2):
        route += [(i % size, (i + 1) % size), ((i + 1) % size, i % size)]
    return lax.ppermute(block, axis, route)


def to_all(sums):
    return lax.all_to_all(sums, EVERY, 0, 0, tiled=True)


def halo(near, mid, far):
    below = swap(near, "grp", 0)
    above = swap(far, "grp", 1)
    pair, cross = call(edge_body, [((9, 128), F32)] * 2, (near, mid, far, below, above), "edges")
    under = swap(pair, "slab", 0)
    over = swap(cross, "slab", 1)
    return below, above, under, over


def shards(reference_bricks, deformed, tap_weights, valid_voxels, sources):
    big = ((CELLS, 512), F32)
    sums_shape = ((128, 128), F32)
    nodes_shape = [((9, 128), F32)] * 3
    dir_shape = ((3, 2, 2, 128), F32)
    grad_shape = ((3, CELLS, 512), F32)
    parts = [pltpu.VMEM((6, CELLS, 256), BF16)]
    fields = [pltpu.VMEM((4, 384, 256), F32)]
    taps = tap_weights.reshape(8, CELLS, 512)
    image = deformed.reshape(CELLS, 512)
    valid = valid_voxels.reshape(CELLS, 512)

    pos, want, bricks, level, inner, outer, slope = call(
        wanted_body,
        [
            ((CELLS, 128), F32),
            ((16, 128), I32),
            ((CELLS, 512), BF16),
            ((128, 384), BF16),
            ((256, 512), BF16),
            ((128, 512), BF16),
            ((256, 256), BF16),
        ],
        (sources, reference_bricks.reshape(CELLS, 512)),
        "wanted",
        [pltpu.VMEM((2, 2, 128), I32), pltpu.SemaphoreType.DMA((5,))],
        far=(0, 1),
    )
    asked = lax.all_to_all(want, "slab", 0, 0, tiled=True)
    (sent,) = call(pick_body, [((CELLS, 512), BF16)], (asked, bricks), "pick")
    recv = lax.all_to_all(sent, "slab", 0, 0, tiled=True)
    grads, misfit, sums = call(
        warp_body,
        [grad_shape, big, sums_shape],
        (pos, recv, level, inner, outer, slope, image, taps, valid),
        "warp",
        [
            pltpu.VMEM((8, CELLS, 512), F32),
            pltpu.VMEM((CELLS, 1024), BF16),
            pltpu.VMEM((CELLS, 512), F32),
            pltpu.VMEM((CELLS, 512), BF16),
            pltpu.VMEM((8, CELLS, 512), BF16),
            pltpu.VMEM((CELLS, 512), I32),
            pltpu.SemaphoreType.DMA((3, 4)),
        ],
        40,
        (6, 7, 8),
    )
    sums = to_all(sums)
    near, mid, far = call(first_force_body, nodes_shape, (sums, misfit, grads), "force_first", parts)
    below, above, under, over = halo(near, mid, far)
    change, steps, dir0 = call(
        first_move_body,
        [big, sums_shape, dir_shape],
        (near, mid, far, below, above, under, over, sums, misfit, grads),
        "move_first",
        fields,
    )
    first = to_all(steps)
    near, mid, far, misfit = call(
        second_force_body,
        nodes_shape + [big],
        (sums, first, misfit, change, grads),
        "force_second",
        parts,
    )
    below, above, under, over = halo(near, mid, far)
    change, steps, dir1 = call(
        second_move_body,
        [big, sums_shape, dir_shape],
        (near, mid, far, below, above, under, over, sums, first, misfit, grads),
        "move_second",
        fields,
    )
    second = to_all(steps)
    coefficients, residual = call(
        finish_body,
        [dir_shape, big],
        (first, second, dir0, dir1, misfit, change),
        "finish",
        [
            pltpu.VMEM((3, 2, 2, 128), F32),
            pltpu.VMEM((CELLS, 512), F32),
            pltpu.SemaphoreType.DMA((5,)),
        ],
        stored=True,
    )
    return (coefficients, residual.reshape(2, 2, 128, 512))


def solution(mesh):
    in_specs = (
        P("grp", "slab", None),
        P("slab", "grp", None, None),
        P(None, "slab", "grp", None, None),
        P("slab", "grp", None, None),
        P("slab", "grp", None),
    )
    out_specs = (P(None, "slab", "grp", None), P("slab", "grp", None, None))
    return jax.shard_map(shards, mesh=mesh, in_specs=in_specs, out_specs=out_specs, check_vma=False)
```

```python
import jax
import jax.numpy as jnp
from jax import lax
from jax.experimental import pallas as pl
from jax.experimental.pallas import tpu as pltpu
from jax.sharding import PartitionSpec as P

F32 = jnp.float32
BF16 = jnp.bfloat16
I32 = jnp.int32
EVERY = ("slab", "grp")
CELLS = 512
ROWS = 16
BLOCKS = CELLS // ROWS
CHUNKS = 4
NN = (((1,), (0,)), ((), ()))
NT = (((1,), (1,)), ((), ()))
TN = (((0,), (0,)), ((), ()))
VMEM = pl.BlockSpec(memory_space=pltpu.VMEM)
HBM = pl.BlockSpec(memory_space=pltpu.HBM)


def iota(shape, axis):
    return lax.broadcasted_iota(I32, shape, axis)


def dot(a, b, dims):
    return lax.dot_general(a, b, dims, preferred_element_type=F32)


def call(body, outs, ins, name, scratch=(), limit=16, far=(), stored=False):
    return pl.pallas_call(
        body,
        out_shape=[jax.ShapeDtypeStruct(s, d) for s, d in outs],
        in_specs=[HBM if n in far else VMEM for n in range(len(ins))],
        out_specs=[HBM if stored else VMEM] * len(outs),
        scratch_shapes=list(scratch),
        compiler_params=pltpu.CompilerParams(vmem_limit_bytes=limit << 20),
        name=name,
    )(*[pltpu.with_memory_space_constraint(x, pltpu.HBM) if n in far else x for n, x in enumerate(ins)])


def wanted_body(
    src_hbm, bricks_hbm, pos_ref, want_ref, bricks_ref, level_ref, inner_ref, outer_ref, slope_ref,
    src_ref, sems,
):
    first = pltpu.make_async_copy(src_hbm, src_ref, sems.at[0])
    fetches = []
    for r in range(4):
        at = pl.ds(128 * r, 128)
        fetches.append(pltpu.make_async_copy(bricks_hbm.at[at], bricks_ref.at[at], sems.at[r + 1]))
    first.start()
    for fetch in fetches:
        fetch.start()
    place = 32 * (lax.axis_index("slab") % 4)
    earlier = (iota((128, 128), 0) < iota((128, 128), 1)).astype(F32).astype(BF16)
    owners = iota((16, 128), 0)
    lanes = iota((128, 128), 0)
    before = jnp.zeros((16, 1), F32)
    want = jnp.zeros((32, 128), F32)
    level_ref[...] = level_table()
    inner_ref[...] = rise_table(256)
    outer_ref[...] = rise_table(128)
    slope_ref[...] = slope_table()
    first.wait()
    for r in range(4):
        src = src_ref[r // 2, pl.ds(r % 2, 1), :]
        owner = src >> 9
        row = src & 511
        mine = jnp.where(owners == owner, 1.0, 0.0)
        count = dot(mine.astype(BF16), earlier, NN) + before
        before = before + jnp.sum(mine, axis=1, keepdims=True)
        rank = jnp.sum(mine * count, axis=0, keepdims=True).astype(I32)
        pos = (owner * 32 + rank).astype(F32)
        pos_ref[pl.ds(128 * r, 128), :] = jnp.transpose(jnp.broadcast_to(pos, (128, 128)))
        slot = jnp.where(lanes == rank + place, 1.0, 0.0).astype(BF16)
        low = (row & 255).astype(F32)
        high = (row >> 8).astype(F32)
        parts = jnp.concatenate([mine * low, mine * high], axis=0).astype(BF16)
        want = want + dot(parts, slot, NT)
    want_ref[...] = (want[:16] + 256.0 * want[16:]).astype(I32)
    for fetch in fetches:
        fetch.wait()


def pick_body(want_ref, bricks_ref, out_ref):
    bricks = bricks_ref[...]
    rows = iota((CELLS, 128), 0)
    for r in range(4):
        index = jnp.sum(want_ref[pl.ds(4 * r, 4), :], axis=0, keepdims=True)
        chosen = jnp.where(rows == index, 1.0, 0.0).astype(BF16)
        out_ref[pl.ds(128 * r, 128), :] = dot(chosen, bricks, TN).astype(BF16)


def columns(j):
    return pl.ds(128 * j, 128)


def spread_sums(values):
    lane = iota((128, 128), 1)
    out = jnp.zeros((128, 128), F32)
    for n, value in enumerate(values):
        total = jnp.sum(jnp.sum(value, axis=0, keepdims=True), axis=1, keepdims=True)
        out = jnp.where(lane == n, total, out)
    return out


def gathered_sums(ref, count):
    sums = jnp.sum(ref[...], axis=0, keepdims=True)
    lane = iota((1, 128), 1)
    return [
        jnp.sum(jnp.where(lane == n, sums, 0.0), axis=1, keepdims=True) for n in range(count)
    ]


def plane_step(tap, lane):
    step_x = jnp.where(((tap & 1) == 1) & ((lane & 7) < 7), 1, 0)
    step_y = jnp.where(((tap & 2) == 2) & ((lane & 56) < 56), 8, 0)
    return lane + step_x + step_y


def shift_table(shape, target):
    return jnp.where(iota(shape, 0) == target, 1.0, 0.0).astype(BF16)


def level_table():
    at = iota((1, 384), 1)
    return shift_table((128, 384), plane_step((at >> 7) + 1, at & 127))


def rise_table(width):
    at = iota((1, 512), 1)
    lane = at & 127
    rise = jnp.where(lane < 64, 64, 64 if width == 256 else 0)
    return shift_table((width, 512), plane_step(at >> 7, lane) + rise)


def slope_table():
    at = iota((1, 256), 1)
    lane = at & 127
    along_x = at >= 128
    place = jnp.where(along_x, lane & 7, (lane >> 3) & 7)
    stride = jnp.where(along_x, 1, 8)
    front = lane + jnp.where(place < 7, stride, 0)
    back = lane - jnp.where(place > 0, stride, 0)
    row = iota((256, 256), 0) & 127
    return (jnp.where(row == front, 0.5, 0.0) - jnp.where(row == back, 0.5, 0.0)).astype(BF16)


def warp_body(
    pos_ref, recv_ref, level_ref, inner_ref, outer_ref, slope_ref, image_hbm, taps_hbm, valid_hbm,
    grad_ref, misfit_ref, sums_ref,
    planes_ref, split_ref, mask_ref, image_ref, taps_ref, valid_ref, sems,
):
    copies = []
    for r in range(4):
        at = pl.ds(128 * r, 128)
        copies.append(
            [
                pltpu.make_async_copy(taps_hbm.at[:, at], taps_ref.at[:, at], sems.at[0, r]),
                pltpu.make_async_copy(valid_hbm.at[at], valid_ref.at[at], sems.at[1, r]),
                pltpu.make_async_copy(image_hbm.at[at], image_ref.at[at], sems.at[2, r]),
            ]
        )
    for group in copies:
        for copy in group:
            copy.start()
    lane = iota((128, 128), 1).astype(F32)
    low = iota((ROWS, 128), 1) < 64
    table = slope_ref[...]

    def planes(r):
        at = pl.ds(128 * r, 128)
        pos = pos_ref[at, :]
        chosen = jnp.concatenate(
            [jnp.where(pos == lane + 128.0 * q, 1.0, 0.0).astype(BF16) for q in range(4)], axis=1
        )
        picked = dot(chosen, recv_ref[...], NN)
        planes_ref[0, at, :] = picked
        source = picked.astype(BF16)
        parts = [source[:, 128 * j : 128 * j + 128] for j in range(CHUNKS)]
        shifted = dot(jnp.concatenate(parts, axis=0), level_ref[...], NN)
        for j in range(CHUNKS):
            for tap in range(3):
                planes_ref[tap + 1, at, columns(j)] = shifted[
                    128 * j : 128 * (j + 1), 128 * tap : 128 * tap + 128
                ]
        pairs = jnp.concatenate([source[:, 128 * j : 128 * j + 256] for j in range(3)], axis=0)
        raised = dot(pairs, inner_ref[...], NN)
        for j in range(CHUNKS):
            found = dot(parts[3], outer_ref[...], NN) if j == 3 else raised[128 * j : 128 * (j + 1)]
            for tap in range(4):
                planes_ref[tap + 4, at, columns(j)] = found[:, 128 * tap : 128 * tap + 128]

    def block(at, squares, counted):
        warped = []
        for j in range(CHUNKS):
            terms = [
                taps_ref[tap, at, columns(j)].astype(F32) * planes_ref[tap, at, columns(j)]
                for tap in range(8)
            ]
            warped.append(
                ((terms[0] + terms[1]) + (terms[2] + terms[3]))
                + ((terms[4] + terms[5]) + (terms[6] + terms[7]))
            )
        swapped = [pltpu.roll(c, 64, 1) for c in warped]
        for j in range(CHUNKS):
            field = warped[j]
            mask = valid_ref[at, columns(j)].astype(F32)
            mask_ref[at, columns(j)] = mask
            front = jnp.where(low, swapped[j], swapped[j + 1] if j + 1 < CHUNKS else field)
            back = jnp.where(low, swapped[j - 1] if j else field, swapped[j])
            grad_ref[0, at, columns(j)] = (0.5 * mask) * (front - back)
            coarse = field.astype(BF16)
            split_ref[at, pl.ds(256 * j, 128)] = coarse
            split_ref[at, pl.ds(256 * j + 128, 128)] = (field - coarse.astype(F32)).astype(BF16)
            misfit = mask * (field - image_ref[at, columns(j)].astype(F32))
            misfit_ref[at, columns(j)] = misfit
            squares = squares + misfit * misfit
            counted = counted + mask
        return squares, counted

    def slopes(r):
        at = pl.ds(128 * r, 128)
        for j in range(CHUNKS):
            both = dot(split_ref[at, pl.ds(256 * j, 256)], table, NN)
            mask = mask_ref[at, columns(j)]
            grad_ref[1, at, columns(j)] = mask * both[:, :128]
            grad_ref[2, at, columns(j)] = mask * both[:, 128:]

    squares = counted = jnp.zeros((ROWS, 128), F32)
    for r in range(3):
        planes(r)
    for r in range(4):
        for copy in copies[r]:
            copy.wait()
        if r + 3 < 4:
            planes(r + 3)
        for i in range(128 // ROWS):
            squares, counted = block(pl.ds(128 * r + ROWS * i, ROWS), squares, counted)
        if r > 0:
            slopes(r - 1)
    slopes(3)
    sums_ref[...] = spread_sums([squares, counted])


def base_z(lane):
    return (((lane >> 6) & 1).astype(F32) + 0.5) * 0.125


def round_down(value):
    return value.astype(BF16).astype(F32)


def plane_basis(corner, lane):
    vy = (((lane >> 3) & 7).astype(F32) + 0.5) * 0.125
    vx = ((lane & 7).astype(F32) + 0.5) * 0.125
    along_y = (corner & 2) == 2
    along_x = (corner & 1) == 1
    return jnp.where(along_y, vy, 1.0 - vy) * jnp.where(along_x, vx, 1.0 - vx)


def force_nodes(misfit_at, inverse, grad_ref, near_ref, mid_ref, far_ref, parts_ref):
    def block(i, carry):
        at = pl.ds(pl.multiple_of(i * ROWS, ROWS), ROWS)
        pull = []
        for j in range(CHUNKS):
            misfit = misfit_at(at, j)
            pull.append(misfit / (1.0 + misfit * misfit * inverse))
        for k in range(3):
            force = [pull[j] * grad_ref[k, at, columns(j)] for j in range(CHUNKS)]
            outer = force[2] + force[3]
            total = (force[0] + force[1]) + outer
            rising = (force[1] + force[3]) + (outer + outer)
            for a, value in enumerate((total, rising)):
                coarse = value.astype(BF16)
                parts_ref[2 * k + a, at, pl.ds(0, 128)] = coarse
                parts_ref[2 * k + a, at, pl.ds(128, 128)] = (value - coarse.astype(F32)).astype(BF16)
        return carry

    lax.fori_loop(0, BLOCKS, block, 0, unroll=4)
    rank = iota((16, 256), 0)
    lane = iota((16, 256), 1)
    plane = plane_basis(rank & 3, lane)
    lifted = plane * base_z(lane)
    coarse = round_down(lifted)
    total_basis = jnp.where(
        rank < 4, plane, jnp.where(rank < 8, coarse, jnp.where(rank < 12, lifted - coarse, 0.0))
    ).astype(BF16)
    rising_basis = jnp.where(rank < 4, 0.25 * plane, 0.0).astype(BF16)
    first = iota((4, 128), 1) == 0
    nodes = {}
    for k in range(3):
        total = dot(total_basis, parts_ref[2 * k], NT)
        upper = total[4:8] + total[8:12] + dot(rising_basis, parts_ref[2 * k + 1], NT)[0:4]
        for a, parts in enumerate((total[0:4] - upper, upper)):
            for r in range(4):
                own = parts[:, 128 * r : 128 * r + 128]
                moved = jnp.where(first, 0.0, pltpu.roll(own, 1, 1))
                for b in range(2):
                    value = own[2 * b : 2 * b + 1] + moved[2 * b + 1 : 2 * b + 2]
                    key = (r % 2 + b, (r // 2 + a) * 3 + k)
                    nodes[key] = nodes[key] + value if key in nodes else value
    upward = is_even("grp")
    for row in range(9):
        near, far = nodes[(0, row)], nodes[(2, row)]
        near_ref[pl.ds(row, 1), :] = jnp.where(upward, far, near)
        mid_ref[pl.ds(row, 1), :] = nodes[(1, row)]
        far_ref[pl.ds(row, 1), :] = jnp.where(upward, near, far)


def first_force_body(sums_ref, misfit_ref, grad_ref, near_ref, mid_ref, far_ref, parts_ref):
    square_sum, counted = gathered_sums(sums_ref, 2)
    inverse = 1.0 / (square_sum / counted + 1e-06)
    force_nodes(
        lambda at, j: misfit_ref[at, columns(j)],
        inverse,
        grad_ref,
        near_ref,
        mid_ref,
        far_ref,
        parts_ref,
    )


def second_spread(sums_ref, steps_ref):
    square_sum, counted = gathered_sums(sums_ref, 2)
    steep, curve, cross, moved_sum = gathered_sums(steps_ref, 4)
    step = steep / curve
    updated = jnp.maximum(square_sum + step * (2.0 * cross + step * moved_sum), 0.0)
    return step, 1.0 / (updated / counted + 1e-06)


def second_force_body(
    sums_ref, steps_ref, misfit_ref, change_ref, grad_ref, near_ref, mid_ref, far_ref, out_ref, parts_ref
):
    step, inverse = second_spread(sums_ref, steps_ref)

    def misfit_at(at, j):
        misfit = misfit_ref[at, columns(j)] + step * change_ref[at, columns(j)]
        out_ref[at, columns(j)] = misfit
        return misfit

    force_nodes(misfit_at, inverse, grad_ref, near_ref, mid_ref, far_ref, parts_ref)


def is_even(axis):
    return lax.axis_index(axis) % 2 == 0


def band_sums(pair_ref, mid_ref, cross_ref, from_pair_ref, from_cross_ref):
    band = lax.axis_index("grp")
    last = lax.axis_size("grp") - 1
    upward = is_even("grp")
    pair, cross = pair_ref[...], cross_ref[...]
    from_pair, from_cross = from_pair_ref[...], from_cross_ref[...]
    below = jnp.where(upward, from_cross, from_pair)
    above = jnp.where(upward, from_pair, from_cross)
    near = jnp.where(upward, cross, pair) + jnp.where(band > 0, below, 0.0)
    far = jnp.where(band < last, jnp.where(upward, pair, cross) + above, 0.0)
    return near, mid_ref[...], far


def edge_body(near_ref, mid_ref, far_ref, below_ref, above_ref, pair_ref, cross_ref):
    upward = is_even("slab")
    for y, part in enumerate(band_sums(near_ref, mid_ref, far_ref, below_ref, above_ref)):
        pair_ref[pl.ds(3 * y, 3), :] = jnp.where(upward, part[6:9], part[0:3])
        cross_ref[pl.ds(3 * y, 3), :] = jnp.where(upward, part[0:3], part[6:9])


def move_body(
    near_ref, mid_ref, far_ref, below_ref, above_ref, under_ref, over_ref,
    sums_ref, steps_ref, misfit_ref, grad_ref, change_ref, out_ref, dir_ref, fields_ref, second,
):
    slab = lax.axis_index("slab")
    last = lax.axis_size("slab") - 1
    bands = band_sums(near_ref, mid_ref, far_ref, below_ref, above_ref)
    upward = is_even("slab")
    steep = jnp.zeros((1, 128), F32)
    nodes = {}
    for y in range(3):
        from_pair, from_cross = under_ref[pl.ds(3 * y, 3), :], over_ref[pl.ds(3 * y, 3), :]
        under = jnp.where(slab > 0, jnp.where(upward, from_cross, from_pair), 0.0)
        over = jnp.where(upward, from_pair, from_cross)
        layers = (
            bands[y][0:3] + under,
            bands[y][3:6],
            jnp.where(slab < last, bands[y][6:9] + over, 0.0),
        )
        for z, layer in enumerate(layers):
            direction = -layer
            if z < 2 and y < 2:
                for k in range(3):
                    dir_ref[k, z, pl.ds(y, 1), :] = direction[k : k + 1]
                steep = steep + jnp.sum(direction * direction, axis=0, keepdims=True)
            nodes[(z, y)] = jnp.concatenate([direction[k : k + 1] for k in range(3)], axis=1)
    end = (iota((1, 384), 1) & 127) == 127
    shifted = {key: jnp.where(end, 0.0, pltpu.roll(value, 383, 1)) for key, value in nodes.items()}
    rank = iota((48, 256), 0)
    lane = iota((48, 256), 1)
    upper = (rank & 4) == 4
    base = base_z(lane)
    weight = jnp.where(
        lane < 128, jnp.where(upper, base, 1.0 - base), jnp.where(upper, 0.25, -0.25)
    )
    exact = plane_basis(rank & 3, lane) * weight
    coarse = round_down(exact)
    basis = jnp.where(rank < 24, coarse, exact - coarse).astype(BF16)
    for r in range(4):
        rows = []
        for corner in range(8):
            key = (r // 2 + corner // 4, r % 2 + corner // 2 % 2)
            rows.append(shifted[key] if corner % 2 else nodes[key])
        full = jnp.concatenate(rows, axis=0)
        coarse = round_down(full)
        rest = full - coarse
        middle = round_down(rest)
        split = jnp.concatenate([coarse, middle, rest - middle] * 2, axis=0)
        fields_ref[r] = dot(split.astype(BF16), basis, TN)
    if second:
        _, inverse = second_spread(sums_ref, steps_ref)
    else:
        square_sum, counted = gathered_sums(sums_ref, 2)
        inverse = 1.0 / (square_sum / counted + 1e-06)

    def block(i, carry):
        curve, cross, moved_sum = carry
        at = pl.ds(pl.multiple_of(i * ROWS, ROWS), ROWS)
        r = i // (128 // ROWS)
        x = (i % (128 // ROWS)) * ROWS
        change = [None] * CHUNKS
        for k in range(3):
            cells = pl.ds(pl.multiple_of(128 * k + x, ROWS), ROWS)
            field = fields_ref[r, cells, pl.ds(0, 128)]
            rise = fields_ref[r, cells, pl.ds(128, 128)]
            for j in range(CHUNKS):
                if j:
                    field = field + rise
                term = grad_ref[k, at, columns(j)] * field
                change[j] = term if k == 0 else change[j] + term
        for j in range(CHUNKS):
            misfit = misfit_ref[at, columns(j)]
            change_ref[at, columns(j)] = change[j]
            square = change[j] * change[j]
            curve = curve + square / (1.0 + misfit * misfit * inverse)
            if not second:
                cross = cross + misfit * change[j]
                moved_sum = moved_sum + square
        return curve, cross, moved_sum

    zero = jnp.zeros((ROWS, 128), F32)
    curve, cross, moved_sum = lax.fori_loop(0, BLOCKS, block, (zero, zero, zero), unroll=4)
    out_ref[...] = spread_sums([steep, curve] + ([] if second else [cross, moved_sum]))


def first_move_body(
    near_ref, mid_ref, far_ref, below_ref, above_ref, under_ref, over_ref,
    sums_ref, misfit_ref, grad_ref, change_ref, out_ref, dir_ref, fields_ref,
):
    move_body(
        near_ref, mid_ref, far_ref, below_ref, above_ref, under_ref, over_ref,
        sums_ref, None, misfit_ref, grad_ref, change_ref, out_ref, dir_ref, fields_ref, False,
    )


def second_move_body(
    near_ref, mid_ref, far_ref, below_ref, above_ref, under_ref, over_ref,
    sums_ref, steps_ref, misfit_ref, grad_ref, change_ref, out_ref, dir_ref, fields_ref,
):
    move_body(
        near_ref, mid_ref, far_ref, below_ref, above_ref, under_ref, over_ref,
        sums_ref, steps_ref, misfit_ref, grad_ref, change_ref, out_ref, dir_ref, fields_ref, True,
    )


def finish_body(
    first_ref, second_ref, dir0_ref, dir1_ref, misfit_ref, change_ref, coef_hbm, out_hbm,
    coef_ref, out_ref, sems,
):
    steep, curve = gathered_sums(first_ref, 2)
    step0 = steep / curve
    steep, curve = gathered_sums(second_ref, 2)
    step1 = steep / curve
    coef_ref[...] = step0.reshape(1, 1, 1, 1) * dir0_ref[...] + step1.reshape(1, 1, 1, 1) * dir1_ref[...]
    copies = [pltpu.make_async_copy(coef_ref, coef_hbm, sems.at[4])]
    copies[0].start()
    for r in range(4):
        at = pl.ds(128 * r, 128)
        out_ref[at, :] = misfit_ref[at, :] + step1 * change_ref[at, :]
        copies.append(pltpu.make_async_copy(out_ref.at[at], out_hbm.at[at], sems.at[r]))
        copies[-1].start()
    for copy in copies:
        copy.wait()


def swap(block, axis, offset):
    size = lax.axis_size(axis)
    route = []
    for i in range(offset, size + offset, 2):
        route += [(i % size, (i + 1) % size), ((i + 1) % size, i % size)]
    return lax.ppermute(block, axis, route)


def to_all(sums):
    return lax.all_to_all(sums, EVERY, 0, 0, tiled=True)


def halo(near, mid, far):
    below = swap(near, "grp", 0)
    above = swap(far, "grp", 1)
    pair, cross = call(edge_body, [((9, 128), F32)] * 2, (near, mid, far, below, above), "edges")
    under = swap(pair, "slab", 0)
    over = swap(cross, "slab", 1)
    return below, above, under, over


def shards(reference_bricks, deformed, tap_weights, valid_voxels, sources):
    big = ((CELLS, 512), F32)
    sums_shape = ((128, 128), F32)
    nodes_shape = [((9, 128), F32)] * 3
    dir_shape = ((3, 2, 2, 128), F32)
    grad_shape = ((3, CELLS, 512), F32)
    parts = [pltpu.VMEM((6, CELLS, 256), BF16)]
    fields = [pltpu.VMEM((4, 384, 256), F32)]
    taps = tap_weights.reshape(8, CELLS, 512)
    image = deformed.reshape(CELLS, 512)
    valid = valid_voxels.reshape(CELLS, 512)

    pos, want, bricks, level, inner, outer, slope = call(
        wanted_body,
        [
            ((CELLS, 128), F32),
            ((16, 128), I32),
            ((CELLS, 512), BF16),
            ((128, 384), BF16),
            ((256, 512), BF16),
            ((128, 512), BF16),
            ((256, 256), BF16),
        ],
        (sources, reference_bricks.reshape(CELLS, 512)),
        "wanted",
        [pltpu.VMEM((2, 2, 128), I32), pltpu.SemaphoreType.DMA((5,))],
        far=(0, 1),
    )
    asked = lax.all_to_all(want, "slab", 0, 0, tiled=True)
    (sent,) = call(pick_body, [((CELLS, 512), BF16)], (asked, bricks), "pick")
    recv = lax.all_to_all(sent, "slab", 0, 0, tiled=True)
    grads, misfit, sums = call(
        warp_body,
        [grad_shape, big, sums_shape],
        (pos, recv, level, inner, outer, slope, image, taps, valid),
        "warp",
        [
            pltpu.VMEM((8, CELLS, 512), F32),
            pltpu.VMEM((CELLS, 1024), BF16),
            pltpu.VMEM((CELLS, 512), F32),
            pltpu.VMEM((CELLS, 512), BF16),
            pltpu.VMEM((8, CELLS, 512), BF16),
            pltpu.VMEM((CELLS, 512), I32),
            pltpu.SemaphoreType.DMA((3, 4)),
        ],
        40,
        (6, 7, 8),
    )
    sums = to_all(sums)
    near, mid, far = call(first_force_body, nodes_shape, (sums, misfit, grads), "force_first", parts)
    below, above, under, over = halo(near, mid, far)
    change, steps, dir0 = call(
        first_move_body,
        [big, sums_shape, dir_shape],
        (near, mid, far, below, above, under, over, sums, misfit, grads),
        "move_first",
        fields,
    )
    first = to_all(steps)
    near, mid, far, misfit = call(
        second_force_body,
        nodes_shape + [big],
        (sums, first, misfit, change, grads),
        "force_second",
        parts,
    )
    below, above, under, over = halo(near, mid, far)
    change, steps, dir1 = call(
        second_move_body,
        [big, sums_shape, dir_shape],
        (near, mid, far, below, above, under, over, sums, first, misfit, grads),
        "move_second",
        fields,
    )
    second = to_all(steps)
    coefficients, residual = call(
        finish_body,
        [dir_shape, big],
        (first, second, dir0, dir1, misfit, change),
        "finish",
        [
            pltpu.VMEM((3, 2, 2, 128), F32),
            pltpu.VMEM((CELLS, 512), F32),
            pltpu.SemaphoreType.DMA((5,)),
        ],
        stored=True,
    )
    return (coefficients, residual.reshape(2, 2, 128, 512))


def solution(mesh):
    in_specs = (
        P("grp", "slab", None),
        P("slab", "grp", None, None),
        P(None, "slab", "grp", None, None),
        P("slab", "grp", None, None),
        P("slab", "grp", None),
    )
    out_specs = (P(None, "slab", "grp", None), P("slab", "grp", None, None))
    return jax.shard_map(shards, mesh=mesh, in_specs=in_specs, out_specs=out_specs, check_vma=False)
```

```python
import jax
import jax.numpy as jnp
from jax import lax
from jax.experimental import pallas as pl
from jax.experimental.pallas import tpu as pltpu
from jax.sharding import PartitionSpec as P

F32 = jnp.float32
BF16 = jnp.bfloat16
I32 = jnp.int32
EVERY = ("slab", "grp")
CELLS = 512
ROWS = 16
BLOCKS = CELLS // ROWS
CHUNKS = 4
NN = (((1,), (0,)), ((), ()))
NT = (((1,), (1,)), ((), ()))
TN = (((0,), (0,)), ((), ()))
VMEM = pl.BlockSpec(memory_space=pltpu.VMEM)
HBM = pl.BlockSpec(memory_space=pltpu.HBM)


def iota(shape, axis):
    return lax.broadcasted_iota(I32, shape, axis)


def dot(a, b, dims):
    return lax.dot_general(a, b, dims, preferred_element_type=F32)


def call(body, outs, ins, name, scratch=(), limit=16, far=(), stored=False):
    return pl.pallas_call(
        body,
        out_shape=[jax.ShapeDtypeStruct(s, d) for s, d in outs],
        in_specs=[HBM if n in far else VMEM for n in range(len(ins))],
        out_specs=[HBM if stored else VMEM] * len(outs),
        scratch_shapes=list(scratch),
        compiler_params=pltpu.CompilerParams(vmem_limit_bytes=limit << 20),
        name=name,
    )(*[pltpu.with_memory_space_constraint(x, pltpu.HBM) if n in far else x for n, x in enumerate(ins)])


def wanted_body(
    src_hbm, bricks_hbm, pos_ref, want_ref, bricks_ref, level_ref, inner_ref, outer_ref, slope_ref,
    src_ref, sems,
):
    first = pltpu.make_async_copy(src_hbm, src_ref, sems.at[0])
    fetches = []
    for r in range(4):
        at = pl.ds(128 * r, 128)
        fetches.append(pltpu.make_async_copy(bricks_hbm.at[at], bricks_ref.at[at], sems.at[r + 1]))
    first.start()
    for fetch in fetches:
        fetch.start()
    place = 32 * (lax.axis_index("slab") % 4)
    earlier = (iota((128, 128), 0) < iota((128, 128), 1)).astype(F32).astype(BF16)
    owners = iota((16, 128), 0)
    lanes = iota((128, 128), 0)
    before = jnp.zeros((16, 1), F32)
    want = jnp.zeros((32, 128), F32)
    level_ref[...] = level_table()
    inner_ref[...] = rise_table(256)
    outer_ref[...] = rise_table(128)
    slope_ref[...] = slope_table()
    first.wait()
    for r in range(4):
        src = src_ref[r // 2, pl.ds(r % 2, 1), :]
        owner = src >> 9
        row = src & 511
        mine = jnp.where(owners == owner, 1.0, 0.0)
        count = dot(mine.astype(BF16), earlier, NN) + before
        before = before + jnp.sum(mine, axis=1, keepdims=True)
        rank = jnp.sum(mine * count, axis=0, keepdims=True).astype(I32)
        pos = (owner * 32 + rank).astype(F32)
        pos_ref[pl.ds(128 * r, 128), :] = jnp.transpose(jnp.broadcast_to(pos, (128, 128)))
        slot = jnp.where(lanes == rank + place, 1.0, 0.0).astype(BF16)
        low = (row & 255).astype(F32)
        high = (row >> 8).astype(F32)
        parts = jnp.concatenate([mine * low, mine * high], axis=0).astype(BF16)
        want = want + dot(parts, slot, NT)
    want_ref[...] = (want[:16] + 256.0 * want[16:]).astype(I32)
    for fetch in fetches:
        fetch.wait()


def pick_body(want_ref, bricks_ref, out_ref):
    bricks = bricks_ref[...]
    rows = iota((CELLS, 128), 0)
    for r in range(4):
        index = jnp.sum(want_ref[pl.ds(4 * r, 4), :], axis=0, keepdims=True)
        chosen = jnp.where(rows == index, 1.0, 0.0).astype(BF16)
        out_ref[pl.ds(128 * r, 128), :] = dot(chosen, bricks, TN).astype(BF16)


def columns(j):
    return pl.ds(128 * j, 128)


def spread_sums(values):
    lane = iota((128, 128), 1)
    out = jnp.zeros((128, 128), F32)
    for n, value in enumerate(values):
        total = jnp.sum(jnp.sum(value, axis=0, keepdims=True), axis=1, keepdims=True)
        out = jnp.where(lane == n, total, out)
    return out


def gathered_sums(ref, count):
    sums = jnp.sum(ref[...], axis=0, keepdims=True)
    lane = iota((1, 128), 1)
    return [
        jnp.sum(jnp.where(lane == n, sums, 0.0), axis=1, keepdims=True) for n in range(count)
    ]


def plane_step(tap, lane):
    step_x = jnp.where(((tap & 1) == 1) & ((lane & 7) < 7), 1, 0)
    step_y = jnp.where(((tap & 2) == 2) & ((lane & 56) < 56), 8, 0)
    return lane + step_x + step_y


def shift_table(shape, target):
    return jnp.where(iota(shape, 0) == target, 1.0, 0.0).astype(BF16)


def level_table():
    at = iota((1, 384), 1)
    return shift_table((128, 384), plane_step((at >> 7) + 1, at & 127))


def rise_table(width):
    at = iota((1, 512), 1)
    lane = at & 127
    rise = jnp.where(lane < 64, 64, 64 if width == 256 else 0)
    return shift_table((width, 512), plane_step(at >> 7, lane) + rise)


def slope_table():
    at = iota((1, 256), 1)
    lane = at & 127
    along_x = at >= 128
    place = jnp.where(along_x, lane & 7, (lane >> 3) & 7)
    stride = jnp.where(along_x, 1, 8)
    front = lane + jnp.where(place < 7, stride, 0)
    back = lane - jnp.where(place > 0, stride, 0)
    row = iota((256, 256), 0) & 127
    return (jnp.where(row == front, 0.5, 0.0) - jnp.where(row == back, 0.5, 0.0)).astype(BF16)


def warp_body(
    pos_ref, recv_ref, level_ref, inner_ref, outer_ref, slope_ref, image_hbm, taps_hbm, valid_hbm,
    grad_ref, misfit_ref, sums_ref,
    planes_ref, split_ref, mask_ref, image_ref, taps_ref, valid_ref, sems,
):
    copies = []
    for r in range(4):
        at = pl.ds(128 * r, 128)
        copies.append(
            [
                pltpu.make_async_copy(taps_hbm.at[:, at], taps_ref.at[:, at], sems.at[0, r]),
                pltpu.make_async_copy(valid_hbm.at[at], valid_ref.at[at], sems.at[1, r]),
                pltpu.make_async_copy(image_hbm.at[at], image_ref.at[at], sems.at[2, r]),
            ]
        )
    for group in copies:
        for copy in group:
            copy.start()
    lane = iota((128, 128), 1).astype(F32)
    low = iota((ROWS, 128), 1) < 64
    table = slope_ref[...]

    def planes(r):
        at = pl.ds(128 * r, 128)
        pos = pos_ref[at, :]
        chosen = jnp.concatenate(
            [jnp.where(pos == lane + 128.0 * q, 1.0, 0.0).astype(BF16) for q in range(4)], axis=1
        )
        picked = dot(chosen, recv_ref[...], NN)
        planes_ref[0, at, :] = picked
        source = picked.astype(BF16)
        parts = [source[:, 128 * j : 128 * j + 128] for j in range(CHUNKS)]
        shifted = dot(jnp.concatenate(parts, axis=0), level_ref[...], NN)
        for j in range(CHUNKS):
            for tap in range(3):
                planes_ref[tap + 1, at, columns(j)] = shifted[
                    128 * j : 128 * (j + 1), 128 * tap : 128 * tap + 128
                ]
        pairs = jnp.concatenate([source[:, 128 * j : 128 * j + 256] for j in range(3)], axis=0)
        raised = dot(pairs, inner_ref[...], NN)
        for j in range(CHUNKS):
            found = dot(parts[3], outer_ref[...], NN) if j == 3 else raised[128 * j : 128 * (j + 1)]
            for tap in range(4):
                planes_ref[tap + 4, at, columns(j)] = found[:, 128 * tap : 128 * tap + 128]

    def block(at, squares, counted):
        warped = []
        for j in range(CHUNKS):
            terms = [
                taps_ref[tap, at, columns(j)].astype(F32) * planes_ref[tap, at, columns(j)]
                for tap in range(8)
            ]
            warped.append(
                ((terms[0] + terms[1]) + (terms[2] + terms[3]))
                + ((terms[4] + terms[5]) + (terms[6] + terms[7]))
            )
        swapped = [pltpu.roll(c, 64, 1) for c in warped]
        for j in range(CHUNKS):
            field = warped[j]
            mask = valid_ref[at, columns(j)].astype(F32)
            mask_ref[at, columns(j)] = mask
            front = jnp.where(low, swapped[j], swapped[j + 1] if j + 1 < CHUNKS else field)
            back = jnp.where(low, swapped[j - 1] if j else field, swapped[j])
            grad_ref[0, at, columns(j)] = (0.5 * mask) * (front - back)
            coarse = field.astype(BF16)
            split_ref[at, pl.ds(256 * j, 128)] = coarse
            split_ref[at, pl.ds(256 * j + 128, 128)] = (field - coarse.astype(F32)).astype(BF16)
            misfit = mask * (field - image_ref[at, columns(j)].astype(F32))
            misfit_ref[at, columns(j)] = misfit
            squares = squares + misfit * misfit
            counted = counted + mask
        return squares, counted

    def slopes(r):
        at = pl.ds(128 * r, 128)
        for j in range(CHUNKS):
            both = dot(split_ref[at, pl.ds(256 * j, 256)], table, NN)
            mask = mask_ref[at, columns(j)]
            grad_ref[1, at, columns(j)] = mask * both[:, :128]
            grad_ref[2, at, columns(j)] = mask * both[:, 128:]

    squares = counted = jnp.zeros((ROWS, 128), F32)
    for r in range(3):
        planes(r)
    for r in range(4):
        for copy in copies[r]:
            copy.wait()
        if r + 3 < 4:
            planes(r + 3)
        for i in range(128 // ROWS):
            squares, counted = block(pl.ds(128 * r + ROWS * i, ROWS), squares, counted)
        if r > 0:
            slopes(r - 1)
    slopes(3)
    sums_ref[...] = spread_sums([squares, counted])


def base_z(lane):
    return (((lane >> 6) & 1).astype(F32) + 0.5) * 0.125


def round_down(value):
    return value.astype(BF16).astype(F32)


def plane_basis(corner, lane):
    vy = (((lane >> 3) & 7).astype(F32) + 0.5) * 0.125
    vx = ((lane & 7).astype(F32) + 0.5) * 0.125
    along_y = (corner & 2) == 2
    along_x = (corner & 1) == 1
    return jnp.where(along_y, vy, 1.0 - vy) * jnp.where(along_x, vx, 1.0 - vx)


def force_nodes(misfit_at, inverse, grad_ref, near_ref, mid_ref, far_ref, parts_ref):
    def block(i, carry):
        at = pl.ds(pl.multiple_of(i * ROWS, ROWS), ROWS)
        pull = []
        for j in range(CHUNKS):
            misfit = misfit_at(at, j)
            pull.append(misfit / (1.0 + misfit * misfit * inverse))
        for k in range(3):
            force = [pull[j] * grad_ref[k, at, columns(j)] for j in range(CHUNKS)]
            outer = force[2] + force[3]
            total = (force[0] + force[1]) + outer
            rising = (force[1] + force[3]) + (outer + outer)
            for a, value in enumerate((total, rising)):
                coarse = value.astype(BF16)
                parts_ref[2 * k + a, at, pl.ds(0, 128)] = coarse
                parts_ref[2 * k + a, at, pl.ds(128, 128)] = (value - coarse.astype(F32)).astype(BF16)
        return carry

    lax.fori_loop(0, BLOCKS, block, 0, unroll=4)
    rank = iota((16, 256), 0)
    lane = iota((16, 256), 1)
    plane = plane_basis(rank & 3, lane)
    lifted = plane * base_z(lane)
    coarse = round_down(lifted)
    total_basis = jnp.where(
        rank < 4, plane, jnp.where(rank < 8, coarse, jnp.where(rank < 12, lifted - coarse, 0.0))
    ).astype(BF16)
    rising_basis = jnp.where(rank < 4, 0.25 * plane, 0.0).astype(BF16)
    first = iota((4, 128), 1) == 0
    nodes = {}
    for k in range(3):
        total = dot(total_basis, parts_ref[2 * k], NT)
        upper = total[4:8] + total[8:12] + dot(rising_basis, parts_ref[2 * k + 1], NT)[0:4]
        for a, parts in enumerate((total[0:4] - upper, upper)):
            for r in range(4):
                own = parts[:, 128 * r : 128 * r + 128]
                moved = jnp.where(first, 0.0, pltpu.roll(own, 1, 1))
                for b in range(2):
                    value = own[2 * b : 2 * b + 1] + moved[2 * b + 1 : 2 * b + 2]
                    key = (r % 2 + b, (r // 2 + a) * 3 + k)
                    nodes[key] = nodes[key] + value if key in nodes else value
    upward = is_even("grp")
    for row in range(9):
        near, far = nodes[(0, row)], nodes[(2, row)]
        near_ref[pl.ds(row, 1), :] = jnp.where(upward, far, near)
        mid_ref[pl.ds(row, 1), :] = nodes[(1, row)]
        far_ref[pl.ds(row, 1), :] = jnp.where(upward, near, far)


def first_force_body(sums_ref, misfit_ref, grad_ref, near_ref, mid_ref, far_ref, parts_ref):
    square_sum, counted = gathered_sums(sums_ref, 2)
    inverse = 1.0 / (square_sum / counted + 1e-06)
    force_nodes(
        lambda at, j: misfit_ref[at, columns(j)],
        inverse,
        grad_ref,
        near_ref,
        mid_ref,
        far_ref,
        parts_ref,
    )


def second_spread(sums_ref, steps_ref):
    square_sum, counted = gathered_sums(sums_ref, 2)
    steep, curve, cross, moved_sum = gathered_sums(steps_ref, 4)
    step = steep / curve
    updated = jnp.maximum(square_sum + step * (2.0 * cross + step * moved_sum), 0.0)
    return step, 1.0 / (updated / counted + 1e-06)


def second_force_body(
    sums_ref, steps_ref, misfit_ref, change_ref, grad_ref, near_ref, mid_ref, far_ref, out_ref, parts_ref
):
    step, inverse = second_spread(sums_ref, steps_ref)

    def misfit_at(at, j):
        misfit = misfit_ref[at, columns(j)] + step * change_ref[at, columns(j)]
        out_ref[at, columns(j)] = misfit
        return misfit

    force_nodes(misfit_at, inverse, grad_ref, near_ref, mid_ref, far_ref, parts_ref)


def is_even(axis):
    return lax.axis_index(axis) % 2 == 0


def band_sums(pair_ref, mid_ref, cross_ref, from_pair_ref, from_cross_ref):
    band = lax.axis_index("grp")
    last = lax.axis_size("grp") - 1
    upward = is_even("grp")
    pair, cross = pair_ref[...], cross_ref[...]
    from_pair, from_cross = from_pair_ref[...], from_cross_ref[...]
    below = jnp.where(upward, from_cross, from_pair)
    above = jnp.where(upward, from_pair, from_cross)
    near = jnp.where(upward, cross, pair) + jnp.where(band > 0, below, 0.0)
    far = jnp.where(band < last, jnp.where(upward, pair, cross) + above, 0.0)
    return near, mid_ref[...], far


def edge_body(near_ref, mid_ref, far_ref, below_ref, above_ref, pair_ref, cross_ref):
    upward = is_even("slab")
    for y, part in enumerate(band_sums(near_ref, mid_ref, far_ref, below_ref, above_ref)):
        pair_ref[pl.ds(3 * y, 3), :] = jnp.where(upward, part[6:9], part[0:3])
        cross_ref[pl.ds(3 * y, 3), :] = jnp.where(upward, part[0:3], part[6:9])


def move_body(
    near_ref, mid_ref, far_ref, below_ref, above_ref, under_ref, over_ref,
    robust_ref, misfit_ref, grad_ref, change_ref, out_ref, dir_ref, fields_ref, second,
):
    slab = lax.axis_index("slab")
    last = lax.axis_size("slab") - 1
    bands = band_sums(near_ref, mid_ref, far_ref, below_ref, above_ref)
    upward = is_even("slab")
    steep = jnp.zeros((1, 128), F32)
    nodes = {}
    for y in range(3):
        from_pair, from_cross = under_ref[pl.ds(3 * y, 3), :], over_ref[pl.ds(3 * y, 3), :]
        under = jnp.where(slab > 0, jnp.where(upward, from_cross, from_pair), 0.0)
        over = jnp.where(upward, from_pair, from_cross)
        layers = (
            bands[y][0:3] + under,
            bands[y][3:6],
            jnp.where(slab < last, bands[y][6:9] + over, 0.0),
        )
        for z, layer in enumerate(layers):
            direction = -layer
            if z < 2 and y < 2:
                for k in range(3):
                    dir_ref[k, z, pl.ds(y, 1), :] = direction[k : k + 1]
                steep = steep + jnp.sum(direction * direction, axis=0, keepdims=True)
            nodes[(z, y)] = jnp.concatenate([direction[k : k + 1] for k in range(3)], axis=1)
    end = (iota((1, 384), 1) & 127) == 127
    shifted = {key: jnp.where(end, 0.0, pltpu.roll(value, 383, 1)) for key, value in nodes.items()}
    rank = iota((48, 256), 0)
    lane = iota((48, 256), 1)
    upper = (rank & 4) == 4
    base = base_z(lane)
    weight = jnp.where(
        lane < 128, jnp.where(upper, base, 1.0 - base), jnp.where(upper, 0.25, -0.25)
    )
    exact = plane_basis(rank & 3, lane) * weight
    coarse = round_down(exact)
    basis = jnp.where(rank < 24, coarse, exact - coarse).astype(BF16)
    for r in range(4):
        rows = []
        for corner in range(8):
            key = (r // 2 + corner // 4, r % 2 + corner // 2 % 2)
            rows.append(shifted[key] if corner % 2 else nodes[key])
        full = jnp.concatenate(rows, axis=0)
        coarse = round_down(full)
        rest = full - coarse
        middle = round_down(rest)
        split = jnp.concatenate([coarse, middle, rest - middle] * 2, axis=0)
        fields_ref[r] = dot(split.astype(BF16), basis, TN)
    def block(i, carry):
        curve, cross, moved_sum = carry
        at = pl.ds(pl.multiple_of(i * ROWS, ROWS), ROWS)
        r = i // (128 // ROWS)
        x = (i % (128 // ROWS)) * ROWS
        change = [None] * CHUNKS
        for k in range(3):
            cells = pl.ds(pl.multiple_of(128 * k + x, ROWS), ROWS)
            field = fields_ref[r, cells, pl.ds(0, 128)]
            rise = fields_ref[r, cells, pl.ds(128, 128)]
            for j in range(CHUNKS):
                if j:
                    field = field + rise
                term = grad_ref[k, at, columns(j)] * field
                change[j] = term if k == 0 else change[j] + term
        for j in range(CHUNKS):
            misfit = None if second else misfit_ref[at, columns(j)]
            change_ref[at, columns(j)] = change[j]
            square = change[j] * change[j]
            curve = curve + square * robust_ref[at, columns(j)]
            if not second:
                cross = cross + misfit * change[j]
                moved_sum = moved_sum + square
        return curve, cross, moved_sum

    zero = jnp.zeros((ROWS, 128), F32)
    curve, cross, moved_sum = lax.fori_loop(0, BLOCKS, block, (zero, zero, zero), unroll=4)
    out_ref[...] = spread_sums([steep, curve] + ([] if second else [cross, moved_sum]))


def first_move_body(
    near_ref, mid_ref, far_ref, below_ref, above_ref, under_ref, over_ref,
    robust_ref, misfit_ref, grad_ref, change_ref, out_ref, dir_ref, fields_ref,
):
    move_body(
        near_ref, mid_ref, far_ref, below_ref, above_ref, under_ref, over_ref,
        robust_ref, misfit_ref, grad_ref, change_ref, out_ref, dir_ref, fields_ref, False,
    )


def second_move_body(
    near_ref, mid_ref, far_ref, below_ref, above_ref, under_ref, over_ref,
    robust_ref, grad_ref, change_ref, out_ref, dir_ref, fields_ref,
):
    move_body(
        near_ref, mid_ref, far_ref, below_ref, above_ref, under_ref, over_ref,
        robust_ref, None, grad_ref, change_ref, out_ref, dir_ref, fields_ref, True,
    )


def weigh(misfit_ref, inverse, out_ref):
    def block(i, carry):
        at = pl.ds(pl.multiple_of(i * ROWS, ROWS), ROWS)
        misfit = misfit_ref[at, :]
        out_ref[at, :] = 1.0 / (1.0 + misfit * misfit * inverse)
        return carry

    lax.fori_loop(0, BLOCKS, block, 0, unroll=4)


def first_weigh_body(after_ref, sums_ref, misfit_ref, out_ref):
    square_sum, counted = gathered_sums(sums_ref, 2)
    weigh(misfit_ref, 1.0 / (square_sum / counted + 1e-06), out_ref)


def second_weigh_body(after_ref, sums_ref, steps_ref, misfit_ref, out_ref):
    _, inverse = second_spread(sums_ref, steps_ref)
    weigh(misfit_ref, inverse, out_ref)


def finish_body(
    first_ref, second_ref, dir0_ref, dir1_ref, misfit_ref, change_ref, coef_hbm, out_hbm,
    coef_ref, out_ref, sems,
):
    steep, curve = gathered_sums(first_ref, 2)
    step0 = steep / curve
    steep, curve = gathered_sums(second_ref, 2)
    step1 = steep / curve
    coef_ref[...] = step0.reshape(1, 1, 1, 1) * dir0_ref[...] + step1.reshape(1, 1, 1, 1) * dir1_ref[...]
    copies = [pltpu.make_async_copy(coef_ref, coef_hbm, sems.at[4])]
    copies[0].start()
    for r in range(4):
        at = pl.ds(128 * r, 128)
        out_ref[at, :] = misfit_ref[at, :] + step1 * change_ref[at, :]
        copies.append(pltpu.make_async_copy(out_ref.at[at], out_hbm.at[at], sems.at[r]))
        copies[-1].start()
    for copy in copies:
        copy.wait()


def swap(block, axis, offset):
    size = lax.axis_size(axis)
    route = []
    for i in range(offset, size + offset, 2):
        route += [(i % size, (i + 1) % size), ((i + 1) % size, i % size)]
    return lax.ppermute(block, axis, route)


def to_all(sums):
    return lax.all_to_all(sums, EVERY, 0, 0, tiled=True)


def halo(near, mid, far):
    below = swap(near, "grp", 0)
    above = swap(far, "grp", 1)
    pair, cross = call(edge_body, [((9, 128), F32)] * 2, (near, mid, far, below, above), "edges")
    under = swap(pair, "slab", 0)
    over = swap(cross, "slab", 1)
    return below, above, under, over, pair


def shards(reference_bricks, deformed, tap_weights, valid_voxels, sources):
    big = ((CELLS, 512), F32)
    sums_shape = ((128, 128), F32)
    nodes_shape = [((9, 128), F32)] * 3
    dir_shape = ((3, 2, 2, 128), F32)
    grad_shape = ((3, CELLS, 512), F32)
    parts = [pltpu.VMEM((6, CELLS, 256), BF16)]
    fields = [pltpu.VMEM((4, 384, 256), F32)]
    taps = tap_weights.reshape(8, CELLS, 512)
    image = deformed.reshape(CELLS, 512)
    valid = valid_voxels.reshape(CELLS, 512)

    pos, want, bricks, level, inner, outer, slope = call(
        wanted_body,
        [
            ((CELLS, 128), F32),
            ((16, 128), I32),
            ((CELLS, 512), BF16),
            ((128, 384), BF16),
            ((256, 512), BF16),
            ((128, 512), BF16),
            ((256, 256), BF16),
        ],
        (sources, reference_bricks.reshape(CELLS, 512)),
        "wanted",
        [pltpu.VMEM((2, 2, 128), I32), pltpu.SemaphoreType.DMA((5,))],
        far=(0, 1),
    )
    asked = lax.all_to_all(want, "slab", 0, 0, tiled=True)
    (sent,) = call(pick_body, [((CELLS, 512), BF16)], (asked, bricks), "pick")
    recv = lax.all_to_all(sent, "slab", 0, 0, tiled=True)
    grads, misfit, sums = call(
        warp_body,
        [grad_shape, big, sums_shape],
        (pos, recv, level, inner, outer, slope, image, taps, valid),
        "warp",
        [
            pltpu.VMEM((8, CELLS, 512), F32),
            pltpu.VMEM((CELLS, 1024), BF16),
            pltpu.VMEM((CELLS, 512), F32),
            pltpu.VMEM((CELLS, 512), BF16),
            pltpu.VMEM((8, CELLS, 512), BF16),
            pltpu.VMEM((CELLS, 512), I32),
            pltpu.SemaphoreType.DMA((3, 4)),
        ],
        40,
        (6, 7, 8),
    )
    sums = to_all(sums)
    near, mid, far = call(first_force_body, nodes_shape, (sums, misfit, grads), "force_first", parts)
    below, above, under, over, pair = halo(near, mid, far)
    (robust,) = call(first_weigh_body, [big], (pair, sums, misfit), "weigh_first")
    change, steps, dir0 = call(
        first_move_body,
        [big, sums_shape, dir_shape],
        (near, mid, far, below, above, under, over, robust, misfit, grads),
        "move_first",
        fields,
    )
    first = to_all(steps)
    near, mid, far, misfit = call(
        second_force_body,
        nodes_shape + [big],
        (sums, first, misfit, change, grads),
        "force_second",
        parts,
    )
    below, above, under, over, pair = halo(near, mid, far)
    (robust,) = call(second_weigh_body, [big], (pair, sums, first, misfit), "weigh_second")
    change, steps, dir1 = call(
        second_move_body,
        [big, sums_shape, dir_shape],
        (near, mid, far, below, above, under, over, robust, grads),
        "move_second",
        fields,
    )
    second = to_all(steps)
    coefficients, residual = call(
        finish_body,
        [dir_shape, big],
        (first, second, dir0, dir1, misfit, change),
        "finish",
        [
            pltpu.VMEM((3, 2, 2, 128), F32),
            pltpu.VMEM((CELLS, 512), F32),
            pltpu.SemaphoreType.DMA((5,)),
        ],
        stored=True,
    )
    return (coefficients, residual.reshape(2, 2, 128, 512))


def solution(mesh):
    in_specs = (
        P("grp", "slab", None),
        P("slab", "grp", None, None),
        P(None, "slab", "grp", None, None),
        P("slab", "grp", None, None),
        P("slab", "grp", None),
    )
    out_specs = (P(None, "slab", "grp", None), P("slab", "grp", None, None))
    return jax.shard_map(shards, mesh=mesh, in_specs=in_specs, out_specs=out_specs, check_vma=False)
```

```python
import jax
import jax.numpy as jnp
from jax import lax
from jax.experimental import pallas as pl
from jax.experimental.pallas import tpu as pltpu
from jax.sharding import PartitionSpec as P

F32 = jnp.float32
BF16 = jnp.bfloat16
I32 = jnp.int32
EVERY = ("slab", "grp")
CELLS = 512
ROWS = 16
BLOCKS = CELLS // ROWS
CHUNKS = 4
NN = (((1,), (0,)), ((), ()))
NT = (((1,), (1,)), ((), ()))
TN = (((0,), (0,)), ((), ()))
VMEM = pl.BlockSpec(memory_space=pltpu.VMEM)
HBM = pl.BlockSpec(memory_space=pltpu.HBM)


def iota(shape, axis):
    return lax.broadcasted_iota(I32, shape, axis)


def dot(a, b, dims):
    return lax.dot_general(a, b, dims, preferred_element_type=F32)


def call(body, outs, ins, name, scratch=(), limit=16, far=(), stored=False):
    return pl.pallas_call(
        body,
        out_shape=[jax.ShapeDtypeStruct(s, d) for s, d in outs],
        in_specs=[HBM if n in far else VMEM for n in range(len(ins))],
        out_specs=[HBM if stored else VMEM] * len(outs),
        scratch_shapes=list(scratch),
        compiler_params=pltpu.CompilerParams(vmem_limit_bytes=limit << 20),
        name=name,
    )(*[pltpu.with_memory_space_constraint(x, pltpu.HBM) if n in far else x for n, x in enumerate(ins)])


def wanted_body(
    src_hbm, bricks_hbm, pos_ref, want_ref, bricks_ref, level_ref, inner_ref, outer_ref, slope_ref,
    src_ref, sems,
):
    first = pltpu.make_async_copy(src_hbm, src_ref, sems.at[0])
    fetches = []
    for r in range(4):
        at = pl.ds(128 * r, 128)
        fetches.append(pltpu.make_async_copy(bricks_hbm.at[at], bricks_ref.at[at], sems.at[r + 1]))
    first.start()
    for fetch in fetches:
        fetch.start()
    place = 32 * (lax.axis_index("slab") % 4)
    earlier = (iota((128, 128), 0) < iota((128, 128), 1)).astype(F32).astype(BF16)
    owners = iota((16, 128), 0)
    lanes = iota((128, 128), 0)
    before = jnp.zeros((16, 1), F32)
    want = jnp.zeros((32, 128), F32)
    level_ref[...] = level_table()
    inner_ref[...] = rise_table(256)
    outer_ref[...] = rise_table(128)
    slope_ref[...] = slope_table()
    first.wait()
    for r in range(4):
        src = src_ref[r // 2, pl.ds(r % 2, 1), :]
        owner = src >> 9
        row = src & 511
        mine = jnp.where(owners == owner, 1.0, 0.0)
        count = dot(mine.astype(BF16), earlier, NN) + before
        before = before + jnp.sum(mine, axis=1, keepdims=True)
        rank = jnp.sum(mine * count, axis=0, keepdims=True).astype(I32)
        pos = (owner * 32 + rank).astype(F32)
        pos_ref[pl.ds(128 * r, 128), :] = jnp.transpose(jnp.broadcast_to(pos, (128, 128)))
        slot = jnp.where(lanes == rank + place, 1.0, 0.0).astype(BF16)
        low = (row & 255).astype(F32)
        high = (row >> 8).astype(F32)
        parts = jnp.concatenate([mine * low, mine * high], axis=0).astype(BF16)
        want = want + dot(parts, slot, NT)
    want_ref[...] = (want[:16] + 256.0 * want[16:]).astype(I32)
    for fetch in fetches:
        fetch.wait()


def pick_body(want_ref, bricks_ref, out_ref):
    bricks = bricks_ref[...]
    rows = iota((CELLS, 128), 0)
    for r in range(4):
        index = jnp.sum(want_ref[pl.ds(4 * r, 4), :], axis=0, keepdims=True)
        chosen = jnp.where(rows == index, 1.0, 0.0).astype(BF16)
        out_ref[pl.ds(128 * r, 128), :] = dot(chosen, bricks, TN).astype(BF16)


def columns(j):
    return pl.ds(128 * j, 128)


def spread_sums(values):
    lane = iota((128, 128), 1)
    out = jnp.zeros((128, 128), F32)
    for n, value in enumerate(values):
        total = jnp.sum(jnp.sum(value, axis=0, keepdims=True), axis=1, keepdims=True)
        out = jnp.where(lane == n, total, out)
    return out


def gathered_sums(ref, count):
    sums = jnp.sum(ref[...], axis=0, keepdims=True)
    lane = iota((1, 128), 1)
    return [
        jnp.sum(jnp.where(lane == n, sums, 0.0), axis=1, keepdims=True) for n in range(count)
    ]


def plane_step(tap, lane):
    step_x = jnp.where(((tap & 1) == 1) & ((lane & 7) < 7), 1, 0)
    step_y = jnp.where(((tap & 2) == 2) & ((lane & 56) < 56), 8, 0)
    return lane + step_x + step_y


def shift_table(shape, target):
    return jnp.where(iota(shape, 0) == target, 1.0, 0.0).astype(BF16)


def level_table():
    at = iota((1, 384), 1)
    return shift_table((128, 384), plane_step((at >> 7) + 1, at & 127))


def rise_table(width):
    at = iota((1, 512), 1)
    lane = at & 127
    rise = jnp.where(lane < 64, 64, 64 if width == 256 else 0)
    return shift_table((width, 512), plane_step(at >> 7, lane) + rise)


def slope_table():
    at = iota((1, 256), 1)
    lane = at & 127
    along_x = at >= 128
    place = jnp.where(along_x, lane & 7, (lane >> 3) & 7)
    stride = jnp.where(along_x, 1, 8)
    front = lane + jnp.where(place < 7, stride, 0)
    back = lane - jnp.where(place > 0, stride, 0)
    row = iota((256, 256), 0) & 127
    return (jnp.where(row == front, 0.5, 0.0) - jnp.where(row == back, 0.5, 0.0)).astype(BF16)


def warp_body(
    pos_ref, recv_ref, level_ref, inner_ref, outer_ref, slope_ref, image_hbm, taps_hbm, valid_hbm,
    grad_ref, misfit_ref, sums_ref,
    planes_ref, split_ref, mask_ref, image_ref, taps_ref, valid_ref, sems,
):
    copies = []
    for r in range(4):
        at = pl.ds(128 * r, 128)
        copies.append(
            [
                pltpu.make_async_copy(taps_hbm.at[:, at], taps_ref.at[:, at], sems.at[0, r]),
                pltpu.make_async_copy(valid_hbm.at[at], valid_ref.at[at], sems.at[1, r]),
                pltpu.make_async_copy(image_hbm.at[at], image_ref.at[at], sems.at[2, r]),
            ]
        )
    for group in copies:
        for copy in group:
            copy.start()
    lane = iota((128, 128), 1).astype(F32)
    low = iota((ROWS, 128), 1) < 64
    table = slope_ref[...]

    def planes(r):
        at = pl.ds(128 * r, 128)
        pos = pos_ref[at, :]
        chosen = jnp.concatenate(
            [jnp.where(pos == lane + 128.0 * q, 1.0, 0.0).astype(BF16) for q in range(4)], axis=1
        )
        picked = dot(chosen, recv_ref[...], NN)
        planes_ref[0, at, :] = picked
        source = picked.astype(BF16)
        parts = [source[:, 128 * j : 128 * j + 128] for j in range(CHUNKS)]
        shifted = dot(jnp.concatenate(parts, axis=0), level_ref[...], NN)
        for j in range(CHUNKS):
            for tap in range(3):
                planes_ref[tap + 1, at, columns(j)] = shifted[
                    128 * j : 128 * (j + 1), 128 * tap : 128 * tap + 128
                ]
        pairs = jnp.concatenate([source[:, 128 * j : 128 * j + 256] for j in range(3)], axis=0)
        raised = dot(pairs, inner_ref[...], NN)
        for j in range(CHUNKS):
            found = dot(parts[3], outer_ref[...], NN) if j == 3 else raised[128 * j : 128 * (j + 1)]
            for tap in range(4):
                planes_ref[tap + 4, at, columns(j)] = found[:, 128 * tap : 128 * tap + 128]

    def block(at, squares, counted):
        warped = []
        for j in range(CHUNKS):
            terms = [
                taps_ref[tap, at, columns(j)].astype(F32) * planes_ref[tap, at, columns(j)]
                for tap in range(8)
            ]
            warped.append(
                ((terms[0] + terms[1]) + (terms[2] + terms[3]))
                + ((terms[4] + terms[5]) + (terms[6] + terms[7]))
            )
        swapped = [pltpu.roll(c, 64, 1) for c in warped]
        for j in range(CHUNKS):
            field = warped[j]
            mask = valid_ref[at, columns(j)].astype(F32)
            mask_ref[at, columns(j)] = mask
            front = jnp.where(low, swapped[j], swapped[j + 1] if j + 1 < CHUNKS else field)
            back = jnp.where(low, swapped[j - 1] if j else field, swapped[j])
            grad_ref[0, at, columns(j)] = (0.5 * mask) * (front - back)
            coarse = field.astype(BF16)
            split_ref[at, pl.ds(256 * j, 128)] = coarse
            split_ref[at, pl.ds(256 * j + 128, 128)] = (field - coarse.astype(F32)).astype(BF16)
            misfit = mask * (field - image_ref[at, columns(j)].astype(F32))
            misfit_ref[at, columns(j)] = misfit
            squares = squares + misfit * misfit
            counted = counted + mask
        return squares, counted

    def slopes(r):
        at = pl.ds(128 * r, 128)
        for j in range(CHUNKS):
            both = dot(split_ref[at, pl.ds(256 * j, 256)], table, NN)
            mask = mask_ref[at, columns(j)]
            grad_ref[1, at, columns(j)] = mask * both[:, :128]
            grad_ref[2, at, columns(j)] = mask * both[:, 128:]

    squares = counted = jnp.zeros((ROWS, 128), F32)
    for r in range(3):
        planes(r)
    for r in range(4):
        for copy in copies[r]:
            copy.wait()
        if r + 3 < 4:
            planes(r + 3)
        for i in range(128 // ROWS):
            squares, counted = block(pl.ds(128 * r + ROWS * i, ROWS), squares, counted)
        if r > 0:
            slopes(r - 1)
    slopes(3)
    sums_ref[...] = spread_sums([squares, counted])


def base_z(lane):
    return (((lane >> 6) & 1).astype(F32) + 0.5) * 0.125


def round_down(value):
    return value.astype(BF16).astype(F32)


def plane_basis(corner, lane):
    vy = (((lane >> 3) & 7).astype(F32) + 0.5) * 0.125
    vx = ((lane & 7).astype(F32) + 0.5) * 0.125
    along_y = (corner & 2) == 2
    along_x = (corner & 1) == 1
    return jnp.where(along_y, vy, 1.0 - vy) * jnp.where(along_x, vx, 1.0 - vx)


def force_nodes(misfit_at, inverse, grad_ref, near_ref, mid_ref, far_ref, parts_ref):
    def block(i, carry):
        at = pl.ds(pl.multiple_of(i * ROWS, ROWS), ROWS)
        pull = []
        for j in range(CHUNKS):
            misfit = misfit_at(at, j)
            pull.append(misfit / (1.0 + misfit * misfit * inverse))
        for k in range(3):
            force = [pull[j] * grad_ref[k, at, columns(j)] for j in range(CHUNKS)]
            outer = force[2] + force[3]
            total = (force[0] + force[1]) + outer
            rising = (force[1] + force[3]) + (outer + outer)
            for a, value in enumerate((total, rising)):
                coarse = value.astype(BF16)
                parts_ref[2 * k + a, at, pl.ds(0, 128)] = coarse
                parts_ref[2 * k + a, at, pl.ds(128, 128)] = (value - coarse.astype(F32)).astype(BF16)
        return carry

    lax.fori_loop(0, BLOCKS, block, 0, unroll=4)
    rank = iota((16, 256), 0)
    lane = iota((16, 256), 1)
    plane = plane_basis(rank & 3, lane)
    lifted = plane * base_z(lane)
    coarse = round_down(lifted)
    total_basis = jnp.where(
        rank < 4, plane, jnp.where(rank < 8, coarse, jnp.where(rank < 12, lifted - coarse, 0.0))
    ).astype(BF16)
    rising_basis = jnp.where(rank < 4, 0.25 * plane, 0.0).astype(BF16)
    first = iota((4, 128), 1) == 0
    nodes = {}
    for k in range(3):
        total = dot(total_basis, parts_ref[2 * k], NT)
        upper = total[4:8] + total[8:12] + dot(rising_basis, parts_ref[2 * k + 1], NT)[0:4]
        for a, parts in enumerate((total[0:4] - upper, upper)):
            for r in range(4):
                own = parts[:, 128 * r : 128 * r + 128]
                moved = jnp.where(first, 0.0, pltpu.roll(own, 1, 1))
                for b in range(2):
                    value = own[2 * b : 2 * b + 1] + moved[2 * b + 1 : 2 * b + 2]
                    key = (r % 2 + b, (r // 2 + a) * 3 + k)
                    nodes[key] = nodes[key] + value if key in nodes else value
    upward = is_even("grp")
    for row in range(9):
        near, far = nodes[(0, row)], nodes[(2, row)]
        near_ref[pl.ds(row, 1), :] = jnp.where(upward, far, near)
        mid_ref[pl.ds(row, 1), :] = nodes[(1, row)]
        far_ref[pl.ds(row, 1), :] = jnp.where(upward, near, far)


def first_force_body(sums_ref, misfit_ref, grad_ref, near_ref, mid_ref, far_ref, parts_ref):
    square_sum, counted = gathered_sums(sums_ref, 2)
    inverse = 1.0 / (square_sum / counted + 1e-06)
    force_nodes(
        lambda at, j: misfit_ref[at, columns(j)],
        inverse,
        grad_ref,
        near_ref,
        mid_ref,
        far_ref,
        parts_ref,
    )


def second_spread(sums_ref, steps_ref):
    square_sum, counted = gathered_sums(sums_ref, 2)
    steep, curve, cross, moved_sum = gathered_sums(steps_ref, 4)
    step = steep / curve
    updated = jnp.maximum(square_sum + step * (2.0 * cross + step * moved_sum), 0.0)
    return step, 1.0 / (updated / counted + 1e-06)


def second_force_body(
    sums_ref, steps_ref, misfit_ref, change_ref, grad_ref, near_ref, mid_ref, far_ref, out_ref, parts_ref
):
    step, inverse = second_spread(sums_ref, steps_ref)

    def misfit_at(at, j):
        misfit = misfit_ref[at, columns(j)] + step * change_ref[at, columns(j)]
        out_ref[at, columns(j)] = misfit
        return misfit

    force_nodes(misfit_at, inverse, grad_ref, near_ref, mid_ref, far_ref, parts_ref)


def is_even(axis):
    return lax.axis_index(axis) % 2 == 0


def band_sums(pair_ref, mid_ref, cross_ref, from_pair_ref, from_cross_ref):
    band = lax.axis_index("grp")
    last = lax.axis_size("grp") - 1
    upward = is_even("grp")
    pair, cross = pair_ref[...], cross_ref[...]
    from_pair, from_cross = from_pair_ref[...], from_cross_ref[...]
    below = jnp.where(upward, from_cross, from_pair)
    above = jnp.where(upward, from_pair, from_cross)
    near = jnp.where(upward, cross, pair) + jnp.where(band > 0, below, 0.0)
    far = jnp.where(band < last, jnp.where(upward, pair, cross) + above, 0.0)
    return near, mid_ref[...], far


def edge_body(near_ref, mid_ref, far_ref, below_ref, above_ref, pair_ref, cross_ref):
    upward = is_even("slab")
    for y, part in enumerate(band_sums(near_ref, mid_ref, far_ref, below_ref, above_ref)):
        pair_ref[pl.ds(3 * y, 3), :] = jnp.where(upward, part[6:9], part[0:3])
        cross_ref[pl.ds(3 * y, 3), :] = jnp.where(upward, part[0:3], part[6:9])


def move_body(
    near_ref, mid_ref, far_ref, below_ref, above_ref, under_ref, over_ref,
    robust_ref, misfit_ref, grad_ref, change_ref, out_ref, dir_ref, fields_ref, second,
):
    slab = lax.axis_index("slab")
    last = lax.axis_size("slab") - 1
    bands = band_sums(near_ref, mid_ref, far_ref, below_ref, above_ref)
    upward = is_even("slab")
    steep = jnp.zeros((1, 128), F32)
    nodes = {}
    for y in range(3):
        from_pair, from_cross = under_ref[pl.ds(3 * y, 3), :], over_ref[pl.ds(3 * y, 3), :]
        under = jnp.where(slab > 0, jnp.where(upward, from_cross, from_pair), 0.0)
        over = jnp.where(upward, from_pair, from_cross)
        layers = (
            bands[y][0:3] + under,
            bands[y][3:6],
            jnp.where(slab < last, bands[y][6:9] + over, 0.0),
        )
        for z, layer in enumerate(layers):
            direction = -layer
            if z < 2 and y < 2:
                for k in range(3):
                    dir_ref[k, z, pl.ds(y, 1), :] = direction[k : k + 1]
                steep = steep + jnp.sum(direction * direction, axis=0, keepdims=True)
            nodes[(z, y)] = jnp.concatenate([direction[k : k + 1] for k in range(3)], axis=1)
    end = (iota((1, 384), 1) & 127) == 127
    shifted = {key: jnp.where(end, 0.0, pltpu.roll(value, 383, 1)) for key, value in nodes.items()}
    rank = iota((48, 256), 0)
    lane = iota((48, 256), 1)
    upper = (rank & 4) == 4
    base = base_z(lane)
    weight = jnp.where(
        lane < 128, jnp.where(upper, base, 1.0 - base), jnp.where(upper, 0.25, -0.25)
    )
    exact = plane_basis(rank & 3, lane) * weight
    coarse = round_down(exact)
    basis = jnp.where(rank < 24, coarse, exact - coarse).astype(BF16)
    for r in range(4):
        rows = []
        for corner in range(8):
            key = (r // 2 + corner // 4, r % 2 + corner // 2 % 2)
            rows.append(shifted[key] if corner % 2 else nodes[key])
        full = jnp.concatenate(rows, axis=0)
        coarse = round_down(full)
        rest = full - coarse
        middle = round_down(rest)
        split = jnp.concatenate([coarse, middle, rest - middle] * 2, axis=0)
        fields_ref[r] = dot(split.astype(BF16), basis, TN)
    def block(i, carry):
        curve, cross, moved_sum = carry
        at = pl.ds(pl.multiple_of(i * ROWS, ROWS), ROWS)
        r = i // (128 // ROWS)
        x = (i % (128 // ROWS)) * ROWS
        change = [None] * CHUNKS
        for k in range(3):
            cells = pl.ds(pl.multiple_of(128 * k + x, ROWS), ROWS)
            field = fields_ref[r, cells, pl.ds(0, 128)]
            rise = fields_ref[r, cells, pl.ds(128, 128)]
            for j in range(CHUNKS):
                if j:
                    field = field + rise
                term = grad_ref[k, at, columns(j)] * field
                change[j] = term if k == 0 else change[j] + term
        for j in range(CHUNKS):
            misfit = None if second else misfit_ref[at, columns(j)]
            change_ref[at, columns(j)] = change[j]
            square = change[j] * change[j]
            curve = curve + square * robust_ref[at, columns(j)]
            if not second:
                cross = cross + misfit * change[j]
                moved_sum = moved_sum + square
        return curve, cross, moved_sum

    zero = jnp.zeros((ROWS, 128), F32)
    curve, cross, moved_sum = lax.fori_loop(0, BLOCKS, block, (zero, zero, zero), unroll=4)
    out_ref[...] = spread_sums([steep, curve] + ([] if second else [cross, moved_sum]))


def first_move_body(
    near_ref, mid_ref, far_ref, below_ref, above_ref, under_ref, over_ref,
    robust_ref, misfit_ref, grad_ref, change_ref, out_ref, dir_ref, fields_ref,
):
    move_body(
        near_ref, mid_ref, far_ref, below_ref, above_ref, under_ref, over_ref,
        robust_ref, misfit_ref, grad_ref, change_ref, out_ref, dir_ref, fields_ref, False,
    )


def second_move_body(
    near_ref, mid_ref, far_ref, below_ref, above_ref, under_ref, over_ref,
    robust_ref, grad_ref, change_ref, out_ref, dir_ref, fields_ref,
):
    move_body(
        near_ref, mid_ref, far_ref, below_ref, above_ref, under_ref, over_ref,
        robust_ref, None, grad_ref, change_ref, out_ref, dir_ref, fields_ref, True,
    )


def weigh(misfit_ref, inverse, out_ref):
    def block(i, carry):
        at = pl.ds(pl.multiple_of(i * ROWS, ROWS), ROWS)
        misfit = misfit_ref[at, :]
        out_ref[at, :] = 1.0 / (1.0 + misfit * misfit * inverse)
        return carry

    lax.fori_loop(0, BLOCKS, block, 0, unroll=4)


def first_scale_body(after_ref, sums_ref, out_ref):
    square_sum, counted = gathered_sums(sums_ref, 2)
    out_ref[...] = jnp.broadcast_to(1.0 / (square_sum / counted + 1e-06), (1, 128))


def second_scale_body(after_ref, sums_ref, steps_ref, out_ref):
    out_ref[...] = jnp.broadcast_to(second_spread(sums_ref, steps_ref)[1], (1, 128))


def weigh_body(after_ref, inverse_ref, misfit_ref, out_ref):
    weigh(misfit_ref, inverse_ref[:, 0:1], out_ref)


def finish_body(
    first_ref, second_ref, dir0_ref, dir1_ref, misfit_ref, change_ref, coef_hbm, out_hbm,
    coef_ref, out_ref, sems,
):
    steep, curve = gathered_sums(first_ref, 2)
    step0 = steep / curve
    steep, curve = gathered_sums(second_ref, 2)
    step1 = steep / curve
    coef_ref[...] = step0.reshape(1, 1, 1, 1) * dir0_ref[...] + step1.reshape(1, 1, 1, 1) * dir1_ref[...]
    copies = [pltpu.make_async_copy(coef_ref, coef_hbm, sems.at[4])]
    copies[0].start()
    for r in range(4):
        at = pl.ds(128 * r, 128)
        out_ref[at, :] = misfit_ref[at, :] + step1 * change_ref[at, :]
        copies.append(pltpu.make_async_copy(out_ref.at[at], out_hbm.at[at], sems.at[r]))
        copies[-1].start()
    for copy in copies:
        copy.wait()


def swap(block, axis, offset):
    size = lax.axis_size(axis)
    route = []
    for i in range(offset, size + offset, 2):
        route += [(i % size, (i + 1) % size), ((i + 1) % size, i % size)]
    return lax.ppermute(block, axis, route)


def to_all(sums):
    return lax.all_to_all(sums, EVERY, 0, 0, tiled=True)


def halo(near, mid, far):
    below = swap(near, "grp", 0)
    above = swap(far, "grp", 1)
    pair, cross = call(edge_body, [((9, 128), F32)] * 2, (near, mid, far, below, above), "edges")
    under = swap(pair, "slab", 0)
    over = swap(cross, "slab", 1)
    return below, above, under, over, pair


def shards(reference_bricks, deformed, tap_weights, valid_voxels, sources):
    big = ((CELLS, 512), F32)
    sums_shape = ((128, 128), F32)
    nodes_shape = [((9, 128), F32)] * 3
    dir_shape = ((3, 2, 2, 128), F32)
    grad_shape = ((3, CELLS, 512), F32)
    parts = [pltpu.VMEM((6, CELLS, 256), BF16)]
    fields = [pltpu.VMEM((4, 384, 256), F32)]
    taps = tap_weights.reshape(8, CELLS, 512)
    image = deformed.reshape(CELLS, 512)
    valid = valid_voxels.reshape(CELLS, 512)

    pos, want, bricks, level, inner, outer, slope = call(
        wanted_body,
        [
            ((CELLS, 128), F32),
            ((16, 128), I32),
            ((CELLS, 512), BF16),
            ((128, 384), BF16),
            ((256, 512), BF16),
            ((128, 512), BF16),
            ((256, 256), BF16),
        ],
        (sources, reference_bricks.reshape(CELLS, 512)),
        "wanted",
        [pltpu.VMEM((2, 2, 128), I32), pltpu.SemaphoreType.DMA((5,))],
        far=(0, 1),
    )
    asked = lax.all_to_all(want, "slab", 0, 0, tiled=True)
    (sent,) = call(pick_body, [((CELLS, 512), BF16)], (asked, bricks), "pick")
    recv = lax.all_to_all(sent, "slab", 0, 0, tiled=True)
    grads, misfit, sums = call(
        warp_body,
        [grad_shape, big, sums_shape],
        (pos, recv, level, inner, outer, slope, image, taps, valid),
        "warp",
        [
            pltpu.VMEM((8, CELLS, 512), F32),
            pltpu.VMEM((CELLS, 1024), BF16),
            pltpu.VMEM((CELLS, 512), F32),
            pltpu.VMEM((CELLS, 512), BF16),
            pltpu.VMEM((8, CELLS, 512), BF16),
            pltpu.VMEM((CELLS, 512), I32),
            pltpu.SemaphoreType.DMA((3, 4)),
        ],
        40,
        (6, 7, 8),
    )
    sums = to_all(sums)
    near, mid, far = call(first_force_body, nodes_shape, (sums, misfit, grads), "force_first", parts)
    below, above, under, over, pair = halo(near, mid, far)
    (inverse,) = call(first_scale_body, [((1, 128), F32)], (near, sums), "scale_first")
    (robust,) = call(weigh_body, [big], (pair, inverse, misfit), "weigh_first")
    change, steps, dir0 = call(
        first_move_body,
        [big, sums_shape, dir_shape],
        (near, mid, far, below, above, under, over, robust, misfit, grads),
        "move_first",
        fields,
    )
    first = to_all(steps)
    near, mid, far, misfit = call(
        second_force_body,
        nodes_shape + [big],
        (sums, first, misfit, change, grads),
        "force_second",
        parts,
    )
    below, above, under, over, pair = halo(near, mid, far)
    (inverse,) = call(second_scale_body, [((1, 128), F32)], (near, sums, first), "scale_second")
    (robust,) = call(weigh_body, [big], (pair, inverse, misfit), "weigh_second")
    change, steps, dir1 = call(
        second_move_body,
        [big, sums_shape, dir_shape],
        (near, mid, far, below, above, under, over, robust, grads),
        "move_second",
        fields,
    )
    second = to_all(steps)
    coefficients, residual = call(
        finish_body,
        [dir_shape, big],
        (first, second, dir0, dir1, misfit, change),
        "finish",
        [
            pltpu.VMEM((3, 2, 2, 128), F32),
            pltpu.VMEM((CELLS, 512), F32),
            pltpu.SemaphoreType.DMA((5,)),
        ],
        stored=True,
    )
    return (coefficients, residual.reshape(2, 2, 128, 512))


def solution(mesh):
    in_specs = (
        P("grp", "slab", None),
        P("slab", "grp", None, None),
        P(None, "slab", "grp", None, None),
        P("slab", "grp", None, None),
        P("slab", "grp", None),
    )
    out_specs = (P(None, "slab", "grp", None), P("slab", "grp", None, None))
    return jax.shard_map(shards, mesh=mesh, in_specs=in_specs, out_specs=out_specs, check_vma=False)
```

```python
import jax
import jax.numpy as jnp
from jax import lax
from jax.experimental import pallas as pl
from jax.experimental.pallas import tpu as pltpu
from jax.sharding import PartitionSpec as P

F32 = jnp.float32
BF16 = jnp.bfloat16
I32 = jnp.int32
EVERY = ("slab", "grp")
CELLS = 512
ROWS = 16
BLOCKS = CELLS // ROWS
CHUNKS = 4
NN = (((1,), (0,)), ((), ()))
NT = (((1,), (1,)), ((), ()))
TN = (((0,), (0,)), ((), ()))
VMEM = pl.BlockSpec(memory_space=pltpu.VMEM)
HBM = pl.BlockSpec(memory_space=pltpu.HBM)


def iota(shape, axis):
    return lax.broadcasted_iota(I32, shape, axis)


def dot(a, b, dims):
    return lax.dot_general(a, b, dims, preferred_element_type=F32)


def call(body, outs, ins, name, scratch=(), limit=16, far=(), stored=False):
    return pl.pallas_call(
        body,
        out_shape=[jax.ShapeDtypeStruct(s, d) for s, d in outs],
        in_specs=[HBM if n in far else VMEM for n in range(len(ins))],
        out_specs=[HBM if stored else VMEM] * len(outs),
        scratch_shapes=list(scratch),
        compiler_params=pltpu.CompilerParams(vmem_limit_bytes=limit << 20),
        name=name,
    )(*[pltpu.with_memory_space_constraint(x, pltpu.HBM) if n in far else x for n, x in enumerate(ins)])


def wanted_body(
    src_hbm, bricks_hbm, pos_ref, want_ref, bricks_ref, level_ref, inner_ref, outer_ref, slope_ref,
    src_ref, sems,
):
    first = pltpu.make_async_copy(src_hbm, src_ref, sems.at[0])
    fetches = []
    for r in range(4):
        at = pl.ds(128 * r, 128)
        fetches.append(pltpu.make_async_copy(bricks_hbm.at[at], bricks_ref.at[at], sems.at[r + 1]))
    first.start()
    for fetch in fetches:
        fetch.start()
    place = 32 * (lax.axis_index("slab") % 4)
    earlier = (iota((128, 128), 0) < iota((128, 128), 1)).astype(F32).astype(BF16)
    owners = iota((16, 128), 0)
    lanes = iota((128, 128), 0)
    before = jnp.zeros((16, 1), F32)
    want = jnp.zeros((32, 128), F32)
    level_ref[...] = level_table()
    inner_ref[...] = rise_table(256)
    outer_ref[...] = rise_table(128)
    slope_ref[...] = slope_table()
    first.wait()
    for r in range(4):
        src = src_ref[r // 2, pl.ds(r % 2, 1), :]
        owner = src >> 9
        row = src & 511
        mine = jnp.where(owners == owner, 1.0, 0.0)
        count = dot(mine.astype(BF16), earlier, NN) + before
        before = before + jnp.sum(mine, axis=1, keepdims=True)
        rank = jnp.sum(mine * count, axis=0, keepdims=True).astype(I32)
        pos = (owner * 32 + rank).astype(F32)
        pos_ref[pl.ds(128 * r, 128), :] = jnp.transpose(jnp.broadcast_to(pos, (128, 128)))
        slot = jnp.where(lanes == rank + place, 1.0, 0.0).astype(BF16)
        low = (row & 255).astype(F32)
        high = (row >> 8).astype(F32)
        parts = jnp.concatenate([mine * low, mine * high], axis=0).astype(BF16)
        want = want + dot(parts, slot, NT)
    want_ref[...] = (want[:16] + 256.0 * want[16:]).astype(I32)
    for fetch in fetches:
        fetch.wait()


def pick_body(want_ref, bricks_ref, out_ref):
    bricks = bricks_ref[...]
    rows = iota((CELLS, 128), 0)
    picks = []
    for r in range(4):
        index = jnp.sum(want_ref[pl.ds(4 * r, 4), :], axis=0, keepdims=True)
        picks.append(jnp.where(rows == index, 1.0, 0.0).astype(BF16))
    out_ref[...] = dot(jnp.concatenate(picks, axis=1), bricks, TN).astype(BF16)


def columns(j):
    return pl.ds(128 * j, 128)


def spread_sums(values):
    lane = iota((128, 128), 1)
    out = jnp.zeros((128, 128), F32)
    for n, value in enumerate(values):
        total = jnp.sum(jnp.sum(value, axis=0, keepdims=True), axis=1, keepdims=True)
        out = jnp.where(lane == n, total, out)
    return out


def gathered_sums(ref, count):
    sums = jnp.sum(ref[...], axis=0, keepdims=True)
    lane = iota((1, 128), 1)
    return [
        jnp.sum(jnp.where(lane == n, sums, 0.0), axis=1, keepdims=True) for n in range(count)
    ]


def plane_step(tap, lane):
    step_x = jnp.where(((tap & 1) == 1) & ((lane & 7) < 7), 1, 0)
    step_y = jnp.where(((tap & 2) == 2) & ((lane & 56) < 56), 8, 0)
    return lane + step_x + step_y


def shift_table(shape, target):
    return jnp.where(iota(shape, 0) == target, 1.0, 0.0).astype(BF16)


def level_table():
    at = iota((1, 384), 1)
    return shift_table((128, 384), plane_step((at >> 7) + 1, at & 127))


def rise_table(width):
    at = iota((1, 512), 1)
    lane = at & 127
    rise = jnp.where(lane < 64, 64, 64 if width == 256 else 0)
    return shift_table((width, 512), plane_step(at >> 7, lane) + rise)


def slope_table():
    at = iota((1, 256), 1)
    lane = at & 127
    along_x = at >= 128
    place = jnp.where(along_x, lane & 7, (lane >> 3) & 7)
    stride = jnp.where(along_x, 1, 8)
    front = lane + jnp.where(place < 7, stride, 0)
    back = lane - jnp.where(place > 0, stride, 0)
    row = iota((256, 256), 0) & 127
    return (jnp.where(row == front, 0.5, 0.0) - jnp.where(row == back, 0.5, 0.0)).astype(BF16)


def warp_body(
    pos_ref, recv_ref, level_ref, inner_ref, outer_ref, slope_ref, image_hbm, taps_hbm, valid_hbm,
    grad_ref, misfit_ref, sums_ref,
    planes_ref, split_ref, mask_ref, image_ref, taps_ref, valid_ref, sems,
):
    copies = []
    for r in range(4):
        at = pl.ds(128 * r, 128)
        copies.append(
            [
                pltpu.make_async_copy(taps_hbm.at[:, at], taps_ref.at[:, at], sems.at[0, r]),
                pltpu.make_async_copy(valid_hbm.at[at], valid_ref.at[at], sems.at[1, r]),
                pltpu.make_async_copy(image_hbm.at[at], image_ref.at[at], sems.at[2, r]),
            ]
        )
    for group in copies:
        for copy in group:
            copy.start()
    lane = iota((128, 128), 1).astype(F32)
    low = iota((ROWS, 128), 1) < 64
    table = slope_ref[...]

    def planes(r):
        at = pl.ds(128 * r, 128)
        pos = pos_ref[at, :]
        chosen = jnp.concatenate(
            [jnp.where(pos == lane + 128.0 * q, 1.0, 0.0).astype(BF16) for q in range(4)], axis=1
        )
        picked = dot(chosen, recv_ref[...], NN)
        planes_ref[0, at, :] = picked
        source = picked.astype(BF16)
        parts = [source[:, 128 * j : 128 * j + 128] for j in range(CHUNKS)]
        shifted = dot(jnp.concatenate(parts, axis=0), level_ref[...], NN)
        for j in range(CHUNKS):
            for tap in range(3):
                planes_ref[tap + 1, at, columns(j)] = shifted[
                    128 * j : 128 * (j + 1), 128 * tap : 128 * tap + 128
                ]
        pairs = jnp.concatenate([source[:, 128 * j : 128 * j + 256] for j in range(3)], axis=0)
        raised = dot(pairs, inner_ref[...], NN)
        for j in range(CHUNKS):
            found = dot(parts[3], outer_ref[...], NN) if j == 3 else raised[128 * j : 128 * (j + 1)]
            for tap in range(4):
                planes_ref[tap + 4, at, columns(j)] = found[:, 128 * tap : 128 * tap + 128]

    def block(at, squares, counted):
        warped = []
        for j in range(CHUNKS):
            terms = [
                taps_ref[tap, at, columns(j)].astype(F32) * planes_ref[tap, at, columns(j)]
                for tap in range(8)
            ]
            warped.append(
                ((terms[0] + terms[1]) + (terms[2] + terms[3]))
                + ((terms[4] + terms[5]) + (terms[6] + terms[7]))
            )
        swapped = [pltpu.roll(c, 64, 1) for c in warped]
        for j in range(CHUNKS):
            field = warped[j]
            mask = valid_ref[at, columns(j)].astype(F32)
            mask_ref[at, columns(j)] = mask
            front = jnp.where(low, swapped[j], swapped[j + 1] if j + 1 < CHUNKS else field)
            back = jnp.where(low, swapped[j - 1] if j else field, swapped[j])
            grad_ref[0, at, columns(j)] = (0.5 * mask) * (front - back)
            coarse = field.astype(BF16)
            split_ref[at, pl.ds(256 * j, 128)] = coarse
            split_ref[at, pl.ds(256 * j + 128, 128)] = (field - coarse.astype(F32)).astype(BF16)
            misfit = mask * (field - image_ref[at, columns(j)].astype(F32))
            misfit_ref[at, columns(j)] = misfit
            squares = squares + misfit * misfit
            counted = counted + mask
        return squares, counted

    def slopes(r):
        at = pl.ds(128 * r, 128)
        for j in range(CHUNKS):
            both = dot(split_ref[at, pl.ds(256 * j, 256)], table, NN)
            mask = mask_ref[at, columns(j)]
            grad_ref[1, at, columns(j)] = mask * both[:, :128]
            grad_ref[2, at, columns(j)] = mask * both[:, 128:]

    squares = counted = jnp.zeros((ROWS, 128), F32)
    for r in range(3):
        planes(r)
    for r in range(4):
        for copy in copies[r]:
            copy.wait()
        if r + 3 < 4:
            planes(r + 3)
        for i in range(128 // ROWS):
            squares, counted = block(pl.ds(128 * r + ROWS * i, ROWS), squares, counted)
        if r > 0:
            slopes(r - 1)
    slopes(3)
    sums_ref[...] = spread_sums([squares, counted])


def base_z(lane):
    return (((lane >> 6) & 1).astype(F32) + 0.5) * 0.125


def round_down(value):
    return value.astype(BF16).astype(F32)


def plane_basis(corner, lane):
    vy = (((lane >> 3) & 7).astype(F32) + 0.5) * 0.125
    vx = ((lane & 7).astype(F32) + 0.5) * 0.125
    along_y = (corner & 2) == 2
    along_x = (corner & 1) == 1
    return jnp.where(along_y, vy, 1.0 - vy) * jnp.where(along_x, vx, 1.0 - vx)


def force_nodes(misfit_at, inverse, grad_ref, near_ref, mid_ref, far_ref, parts_ref):
    def block(i, carry):
        at = pl.ds(pl.multiple_of(i * ROWS, ROWS), ROWS)
        pull = []
        for j in range(CHUNKS):
            misfit = misfit_at(at, j)
            pull.append(misfit / (1.0 + misfit * misfit * inverse))
        for k in range(3):
            force = [pull[j] * grad_ref[k, at, columns(j)] for j in range(CHUNKS)]
            outer = force[2] + force[3]
            total = (force[0] + force[1]) + outer
            rising = (force[1] + force[3]) + (outer + outer)
            for a, value in enumerate((total, rising)):
                coarse = value.astype(BF16)
                parts_ref[2 * k + a, at, pl.ds(0, 128)] = coarse
                parts_ref[2 * k + a, at, pl.ds(128, 128)] = (value - coarse.astype(F32)).astype(BF16)
        return carry

    lax.fori_loop(0, BLOCKS, block, 0, unroll=4)
    rank = iota((16, 256), 0)
    lane = iota((16, 256), 1)
    plane = plane_basis(rank & 3, lane)
    lifted = plane * base_z(lane)
    coarse = round_down(lifted)
    total_basis = jnp.where(
        rank < 4, plane, jnp.where(rank < 8, coarse, jnp.where(rank < 12, lifted - coarse, 0.0))
    ).astype(BF16)
    rising_basis = jnp.where(rank < 4, 0.25 * plane, 0.0).astype(BF16)
    first = iota((4, 128), 1) == 0
    nodes = {}
    for k in range(3):
        total = dot(total_basis, parts_ref[2 * k], NT)
        upper = total[4:8] + total[8:12] + dot(rising_basis, parts_ref[2 * k + 1], NT)[0:4]
        for a, parts in enumerate((total[0:4] - upper, upper)):
            for r in range(4):
                own = parts[:, 128 * r : 128 * r + 128]
                moved = jnp.where(first, 0.0, pltpu.roll(own, 1, 1))
                for b in range(2):
                    value = own[2 * b : 2 * b + 1] + moved[2 * b + 1 : 2 * b + 2]
                    key = (r % 2 + b, (r // 2 + a) * 3 + k)
                    nodes[key] = nodes[key] + value if key in nodes else value
    upward = is_even("grp")
    for row in range(9):
        near, far = nodes[(0, row)], nodes[(2, row)]
        near_ref[pl.ds(row, 1), :] = jnp.where(upward, far, near)
        mid_ref[pl.ds(row, 1), :] = nodes[(1, row)]
        far_ref[pl.ds(row, 1), :] = jnp.where(upward, near, far)


def first_force_body(sums_ref, misfit_ref, grad_ref, near_ref, mid_ref, far_ref, parts_ref):
    square_sum, counted = gathered_sums(sums_ref, 2)
    inverse = 1.0 / (square_sum / counted + 1e-06)
    force_nodes(
        lambda at, j: misfit_ref[at, columns(j)],
        inverse,
        grad_ref,
        near_ref,
        mid_ref,
        far_ref,
        parts_ref,
    )


def second_spread(sums_ref, steps_ref):
    square_sum, counted = gathered_sums(sums_ref, 2)
    steep, curve, cross, moved_sum = gathered_sums(steps_ref, 4)
    step = steep / curve
    updated = jnp.maximum(square_sum + step * (2.0 * cross + step * moved_sum), 0.0)
    return step, 1.0 / (updated / counted + 1e-06)


def second_force_body(
    sums_ref, steps_ref, misfit_ref, change_ref, grad_ref, near_ref, mid_ref, far_ref, out_ref, parts_ref
):
    step, inverse = second_spread(sums_ref, steps_ref)

    def misfit_at(at, j):
        misfit = misfit_ref[at, columns(j)] + step * change_ref[at, columns(j)]
        out_ref[at, columns(j)] = misfit
        return misfit

    force_nodes(misfit_at, inverse, grad_ref, near_ref, mid_ref, far_ref, parts_ref)


def is_even(axis):
    return lax.axis_index(axis) % 2 == 0


def band_sums(pair_ref, mid_ref, cross_ref, from_pair_ref, from_cross_ref):
    band = lax.axis_index("grp")
    last = lax.axis_size("grp") - 1
    upward = is_even("grp")
    pair, cross = pair_ref[...], cross_ref[...]
    from_pair, from_cross = from_pair_ref[...], from_cross_ref[...]
    below = jnp.where(upward, from_cross, from_pair)
    above = jnp.where(upward, from_pair, from_cross)
    near = jnp.where(upward, cross, pair) + jnp.where(band > 0, below, 0.0)
    far = jnp.where(band < last, jnp.where(upward, pair, cross) + above, 0.0)
    return near, mid_ref[...], far


def edge_body(near_ref, mid_ref, far_ref, below_ref, above_ref, pair_ref, cross_ref):
    upward = is_even("slab")
    for y, part in enumerate(band_sums(near_ref, mid_ref, far_ref, below_ref, above_ref)):
        pair_ref[pl.ds(3 * y, 3), :] = jnp.where(upward, part[6:9], part[0:3])
        cross_ref[pl.ds(3 * y, 3), :] = jnp.where(upward, part[0:3], part[6:9])


def move_body(
    near_ref, mid_ref, far_ref, below_ref, above_ref, under_ref, over_ref,
    robust_ref, misfit_ref, grad_ref, change_ref, out_ref, dir_ref, fields_ref, second,
):
    slab = lax.axis_index("slab")
    last = lax.axis_size("slab") - 1
    bands = band_sums(near_ref, mid_ref, far_ref, below_ref, above_ref)
    upward = is_even("slab")
    steep = jnp.zeros((1, 128), F32)
    nodes = {}
    for y in range(3):
        from_pair, from_cross = under_ref[pl.ds(3 * y, 3), :], over_ref[pl.ds(3 * y, 3), :]
        under = jnp.where(slab > 0, jnp.where(upward, from_cross, from_pair), 0.0)
        over = jnp.where(upward, from_pair, from_cross)
        layers = (
            bands[y][0:3] + under,
            bands[y][3:6],
            jnp.where(slab < last, bands[y][6:9] + over, 0.0),
        )
        for z, layer in enumerate(layers):
            direction = -layer
            if z < 2 and y < 2:
                for k in range(3):
                    dir_ref[k, z, pl.ds(y, 1), :] = direction[k : k + 1]
                steep = steep + jnp.sum(direction * direction, axis=0, keepdims=True)
            nodes[(z, y)] = jnp.concatenate([direction[k : k + 1] for k in range(3)], axis=1)
    end = (iota((1, 384), 1) & 127) == 127
    shifted = {key: jnp.where(end, 0.0, pltpu.roll(value, 383, 1)) for key, value in nodes.items()}
    rank = iota((48, 256), 0)
    lane = iota((48, 256), 1)
    upper = (rank & 4) == 4
    base = base_z(lane)
    weight = jnp.where(
        lane < 128, jnp.where(upper, base, 1.0 - base), jnp.where(upper, 0.25, -0.25)
    )
    exact = plane_basis(rank & 3, lane) * weight
    coarse = round_down(exact)
    basis = jnp.where(rank < 24, coarse, exact - coarse).astype(BF16)
    for r in range(4):
        rows = []
        for corner in range(8):
            key = (r // 2 + corner // 4, r % 2 + corner // 2 % 2)
            rows.append(shifted[key] if corner % 2 else nodes[key])
        full = jnp.concatenate(rows, axis=0)
        coarse = round_down(full)
        rest = full - coarse
        middle = round_down(rest)
        split = jnp.concatenate([coarse, middle, rest - middle] * 2, axis=0)
        fields_ref[r] = dot(split.astype(BF16), basis, TN)
    def block(i, carry):
        curve, cross, moved_sum = carry
        at = pl.ds(pl.multiple_of(i * ROWS, ROWS), ROWS)
        r = i // (128 // ROWS)
        x = (i % (128 // ROWS)) * ROWS
        change = [None] * CHUNKS
        for k in range(3):
            cells = pl.ds(pl.multiple_of(128 * k + x, ROWS), ROWS)
            field = fields_ref[r, cells, pl.ds(0, 128)]
            rise = fields_ref[r, cells, pl.ds(128, 128)]
            for j in range(CHUNKS):
                if j:
                    field = field + rise
                term = grad_ref[k, at, columns(j)] * field
                change[j] = term if k == 0 else change[j] + term
        for j in range(CHUNKS):
            misfit = None if second else misfit_ref[at, columns(j)]
            change_ref[at, columns(j)] = change[j]
            square = change[j] * change[j]
            curve = curve + square * robust_ref[at, columns(j)]
            if not second:
                cross = cross + misfit * change[j]
                moved_sum = moved_sum + square
        return curve, cross, moved_sum

    zero = jnp.zeros((ROWS, 128), F32)
    curve, cross, moved_sum = lax.fori_loop(0, BLOCKS, block, (zero, zero, zero), unroll=4)
    out_ref[...] = spread_sums([steep, curve] + ([] if second else [cross, moved_sum]))


def first_move_body(
    near_ref, mid_ref, far_ref, below_ref, above_ref, under_ref, over_ref,
    robust_ref, misfit_ref, grad_ref, change_ref, out_ref, dir_ref, fields_ref,
):
    move_body(
        near_ref, mid_ref, far_ref, below_ref, above_ref, under_ref, over_ref,
        robust_ref, misfit_ref, grad_ref, change_ref, out_ref, dir_ref, fields_ref, False,
    )


def second_move_body(
    near_ref, mid_ref, far_ref, below_ref, above_ref, under_ref, over_ref,
    robust_ref, grad_ref, change_ref, out_ref, dir_ref, fields_ref,
):
    move_body(
        near_ref, mid_ref, far_ref, below_ref, above_ref, under_ref, over_ref,
        robust_ref, None, grad_ref, change_ref, out_ref, dir_ref, fields_ref, True,
    )


def weigh(misfit_ref, inverse, out_ref):
    def block(i, carry):
        at = pl.ds(pl.multiple_of(i * ROWS, ROWS), ROWS)
        misfit = misfit_ref[at, :]
        out_ref[at, :] = 1.0 / (1.0 + misfit * misfit * inverse)
        return carry

    lax.fori_loop(0, BLOCKS, block, 0, unroll=4)


def first_weigh_body(after_ref, sums_ref, misfit_ref, out_ref):
    square_sum, counted = gathered_sums(sums_ref, 2)
    weigh(misfit_ref, 1.0 / (square_sum / counted + 1e-06), out_ref)


def second_weigh_body(after_ref, sums_ref, steps_ref, misfit_ref, out_ref):
    _, inverse = second_spread(sums_ref, steps_ref)
    weigh(misfit_ref, inverse, out_ref)


def finish_body(
    first_ref, second_ref, dir0_ref, dir1_ref, misfit_ref, change_ref, coef_hbm, out_hbm,
    coef_ref, out_ref, sems,
):
    steep, curve = gathered_sums(first_ref, 2)
    step0 = steep / curve
    steep, curve = gathered_sums(second_ref, 2)
    step1 = steep / curve
    coef_ref[...] = step0.reshape(1, 1, 1, 1) * dir0_ref[...] + step1.reshape(1, 1, 1, 1) * dir1_ref[...]
    copies = [pltpu.make_async_copy(coef_ref, coef_hbm, sems.at[4])]
    copies[0].start()
    for r in range(4):
        at = pl.ds(128 * r, 128)
        out_ref[at, :] = misfit_ref[at, :] + step1 * change_ref[at, :]
        copies.append(pltpu.make_async_copy(out_ref.at[at], out_hbm.at[at], sems.at[r]))
        copies[-1].start()
    for copy in copies:
        copy.wait()


def swap(block, axis, offset):
    size = lax.axis_size(axis)
    route = []
    for i in range(offset, size + offset, 2):
        route += [(i % size, (i + 1) % size), ((i + 1) % size, i % size)]
    return lax.ppermute(block, axis, route)


def to_all(sums):
    return lax.all_to_all(sums, EVERY, 0, 0, tiled=True)


def halo(near, mid, far):
    below = swap(near, "grp", 0)
    above = swap(far, "grp", 1)
    pair, cross = call(edge_body, [((9, 128), F32)] * 2, (near, mid, far, below, above), "edges")
    under = swap(pair, "slab", 0)
    over = swap(cross, "slab", 1)
    return below, above, under, over, pair


def shards(reference_bricks, deformed, tap_weights, valid_voxels, sources):
    big = ((CELLS, 512), F32)
    sums_shape = ((128, 128), F32)
    nodes_shape = [((9, 128), F32)] * 3
    dir_shape = ((3, 2, 2, 128), F32)
    grad_shape = ((3, CELLS, 512), F32)
    parts = [pltpu.VMEM((6, CELLS, 256), BF16)]
    fields = [pltpu.VMEM((4, 384, 256), F32)]
    taps = tap_weights.reshape(8, CELLS, 512)
    image = deformed.reshape(CELLS, 512)
    valid = valid_voxels.reshape(CELLS, 512)

    pos, want, bricks, level, inner, outer, slope = call(
        wanted_body,
        [
            ((CELLS, 128), F32),
            ((16, 128), I32),
            ((CELLS, 512), BF16),
            ((128, 384), BF16),
            ((256, 512), BF16),
            ((128, 512), BF16),
            ((256, 256), BF16),
        ],
        (sources, reference_bricks.reshape(CELLS, 512)),
        "wanted",
        [pltpu.VMEM((2, 2, 128), I32), pltpu.SemaphoreType.DMA((5,))],
        far=(0, 1),
    )
    asked = lax.all_to_all(want, "slab", 0, 0, tiled=True)
    (sent,) = call(pick_body, [((CELLS, 512), BF16)], (asked, bricks), "pick")
    recv = lax.all_to_all(sent, "slab", 0, 0, tiled=True)
    grads, misfit, sums = call(
        warp_body,
        [grad_shape, big, sums_shape],
        (pos, recv, level, inner, outer, slope, image, taps, valid),
        "warp",
        [
            pltpu.VMEM((8, CELLS, 512), F32),
            pltpu.VMEM((CELLS, 1024), BF16),
            pltpu.VMEM((CELLS, 512), F32),
            pltpu.VMEM((CELLS, 512), BF16),
            pltpu.VMEM((8, CELLS, 512), BF16),
            pltpu.VMEM((CELLS, 512), I32),
            pltpu.SemaphoreType.DMA((3, 4)),
        ],
        40,
        (6, 7, 8),
    )
    sums = to_all(sums)
    near, mid, far = call(first_force_body, nodes_shape, (sums, misfit, grads), "force_first", parts)
    below, above, under, over, pair = halo(near, mid, far)
    (robust,) = call(first_weigh_body, [big], (pair, sums, misfit), "weigh_first")
    change, steps, dir0 = call(
        first_move_body,
        [big, sums_shape, dir_shape],
        (near, mid, far, below, above, under, over, robust, misfit, grads),
        "move_first",
        fields,
    )
    first = to_all(steps)
    near, mid, far, misfit = call(
        second_force_body,
        nodes_shape + [big],
        (sums, first, misfit, change, grads),
        "force_second",
        parts,
    )
    below, above, under, over, pair = halo(near, mid, far)
    (robust,) = call(second_weigh_body, [big], (pair, sums, first, misfit), "weigh_second")
    change, steps, dir1 = call(
        second_move_body,
        [big, sums_shape, dir_shape],
        (near, mid, far, below, above, under, over, robust, grads),
        "move_second",
        fields,
    )
    second = to_all(steps)
    coefficients, residual = call(
        finish_body,
        [dir_shape, big],
        (first, second, dir0, dir1, misfit, change),
        "finish",
        [
            pltpu.VMEM((3, 2, 2, 128), F32),
            pltpu.VMEM((CELLS, 512), F32),
            pltpu.SemaphoreType.DMA((5,)),
        ],
        stored=True,
    )
    return (coefficients, residual.reshape(2, 2, 128, 512))


def solution(mesh):
    in_specs = (
        P("grp", "slab", None),
        P("slab", "grp", None, None),
        P(None, "slab", "grp", None, None),
        P("slab", "grp", None, None),
        P("slab", "grp", None),
    )
    out_specs = (P(None, "slab", "grp", None), P("slab", "grp", None, None))
    return jax.shard_map(shards, mesh=mesh, in_specs=in_specs, out_specs=out_specs, check_vma=False)
```
